32 devices in a mesh: fsdp: 4 (over y, x), ctx: 8 (over z, core).
Axes of the slice: x: 2, y: 2, z: 4, core: 2. Of those that a mesh axis runs over, the one named last changes fastest.
Arguments:
- block_input: bfloat16 [8, 1024, 768], P('fsdp', 'ctx'), may hold values from -6 to 6
- attn_gain: bfloat16 [768], P('fsdp'), may hold values from 0.5 to 1.5
- w_qkv: bfloat16 [768, 2304], P('fsdp'), may hold values from -0.21875 to 0.21875
- w_out: bfloat16 [768, 768], P('fsdp'), may hold values from -0.875 to 0.875
- ffn_gain: bfloat16 [768], P('fsdp'), may hold values from 0.5 to 1.5
- w_router: bfloat16 [768, 8], P('fsdp'), may hold values from -0.21875 to 0.21875
- w_gate: bfloat16 [768, 4, 2048], P('fsdp'), may hold values from -0.21875 to 0.21875
- w_up: bfloat16 [768, 4, 2048], P('fsdp'), may hold values from -0.21875 to 0.21875
- w_down: bfloat16 [768, 4, 2048], P('fsdp'), may hold values from -0.5 to 0.5
- const_mix: bfloat16 [768, 4], P('fsdp'), may hold values from -0.21875 to 0.21875
- const_vec: bfloat16 [768, 2], P('fsdp'), may hold values from -8 to 8
- prev_logits: float32 [8, 1024, 8], P('fsdp', 'ctx'), may hold values from -8 to 8
- routes: int32 [8, 1024, 2], P('fsdp', 'ctx'), may hold values from 0 to 7, all different within a row; in each aligned block of 128 rows (0 to 127, 128 to 255, ..., all dimensions but the last counted through in order) at most 48 rows name the same one
- doc_ids: int32 [8, 1024], P('fsdp'), may hold values from 0 to 3, never falling along the last dimension, each value on 1 to 512 neighbouring positions
- d_out: bfloat16 [8, 1024, 768], P('fsdp', 'ctx'), may hold values from -6 to 6
Outputs:
- out_block: bfloat16 [8, 1024, 768], P('fsdp', 'ctx')
- grad_x: float32 [8, 1024, 768], P('fsdp', 'ctx')
- grad_prev_logits: float32 [8, 1024, 8], P('fsdp', 'ctx')
- grad_attn_gain: float32 [768], P('fsdp')
- grad_w_qkv: float32 [768, 2304], P('fsdp')
- grad_w_out: float32 [768, 768], P('fsdp')
- grad_ffn_gain: float32 [768], P('fsdp')
- grad_w_router: float32 [768, 8], P('fsdp')
- grad_w_gate: float32 [768, 4, 2048], P('fsdp')
- grad_w_up: float32 [768, 4, 2048], P('fsdp')
- grad_w_down: float32 [768, 4, 2048], P('fsdp')
- grad_const_mix: float32 [768, 4], P('fsdp')
- grad_const_vec: float32 [768, 2], P('fsdp')
The draws below stay inside these ranges and needn't reach their ends.
Inputs may be any that keep to these rules, and one draw needn't show every extreme that they name: `routes`: each token names two different experts. Within each aligned block of 128 positions of a sequence, no expert is named by more than 48 of the block's pairs, a bound that some block reaches. `doc_ids`: along each sequence the document number never falls, all 4 documents occur, and each spans at most 512 positions.
All inputs are finite; a program needn't handle non-finite values.
Results may differ from the reference program's by a relative error of at most 0.022.
Values may be sent and summed in bfloat16 or wider, within the bound.
No kernel may reach another device: no remote copies, remote signals or barrier semaphores. Data moves between devices by JAX's collectives and lax.ppermute only.
A program may use at most 384 MiB of HBM per device.

```python
import math
import jax
import jax.numpy as jnp
import numpy as np
from jax import lax

D = 768
H = 12
HD = 64
FF = 2048
NF = 4
NC = 2
NE = 8
TOP = 2
T_BLK = 128
MOST = 48
DOCS = 4
SEQS = 8
SEQ_LEN = 1024


def shard_levels(rng, dims, pieces, smallest, high):
    level = 1.0
    for axis_at, blocks in pieces:
        steps = jax.random.uniform(jax.random.fold_in(jax.random.fold_in(rng, 6), axis_at), (blocks,), jnp.float32, smallest / len(pieces), high / len(pieces))
        level = level * jnp.repeat(jnp.exp(steps), dims[axis_at] // blocks).reshape((-1,) + (1,) * (len(dims) - 1 - axis_at))
    return level


def length_profile(count, total, limit, lean):
    portions = [(1 << 20) // math.isqrt(standing ** lean) + 1 for standing in range(2, count + 1)]
    spare, given = total - limit - (count - 1), [1] * (count - 1)
    while spare > 0:
        candidates = [i for i in range(count - 1) if given[i] < limit]
        whole, remaining = sum([portions[i] for i in candidates]), spare
        for i in candidates:
            addition = min(limit - given[i], max(1, remaining * portions[i] // whole), spare)
            given[i] = given[i] + addition
            spare = spare - addition
    return np.array([limit] + given)


def ragged(key, count, total, limit, slope):
    if count == 2:
        one = jax.random.randint(key, (), max(1, total - limit), min(limit, total - 1) + 1)
        return jnp.stack([one, total - one])
    lengths = jnp.asarray(length_profile(count, total, limit, slope), jnp.int32)
    pairs = (count - 1) // 2
    donor, taker = lengths[1:1 + 2 * pairs:2], lengths[2:2 + 2 * pairs:2]
    margin = jnp.minimum(donor - 1, limit - taker)
    passed = jax.random.randint(jax.random.fold_in(key, 1), (pairs,), 0, 1 << 20) % (margin + 1)
    lengths = lengths.at[1:1 + 2 * pairs:2].set(donor - passed).at[2:2 + 2 * pairs:2].set(taker + passed)
    return lengths[jax.random.permutation(jax.random.fold_in(key, 2), count)]


def deal_out(key, own, number, rows, amount, top, most, slope):
    sequence = jax.random.permutation(key, amount)
    heavy_load, usual = load_shares(amount, rows * top, most, slope, True), load_shares(amount, rows * top, most, slope, False)
    places = jnp.arange(amount)

    def named(tallies, rotation):
        used = int((tallies > 0).sum())
        fixed = max(1, used // 4)
        moved = fixed + (places - fixed + rotation * (used - fixed)) % max(1, amount - fixed)
        return jnp.zeros((amount,), jnp.int32).at[sequence[jnp.where(places < fixed, places, moved)]].set(jnp.asarray(tallies, jnp.int32))

    tallies = jnp.where(number % 4 == 0, named(heavy_load, number // 4), named(usual, number - number // 4 - 1))
    mixed = jax.random.permutation(jax.random.fold_in(own, 3), amount)
    source_of, taker = mixed[0:amount // 2 * 2:2], mixed[1:amount // 2 * 2:2]
    slack = jnp.minimum(tallies[source_of] - 1, most - tallies[taker]) // 2
    slack = jnp.where((source_of == sequence[0]) | (taker == sequence[0]) | (tallies[taker] == 0), 0, jnp.maximum(slack, 0))
    moved = jax.random.randint(jax.random.fold_in(own, 4), (amount // 2,), 0, 1 << 20) % (slack + 1)
    tallies = tallies.at[source_of].add(-moved).at[taker].add(moved)
    items = jnp.searchsorted(jnp.cumsum(tallies), jnp.arange(rows * top), side="right").astype(jnp.int32)
    listing = items.reshape(top, rows).T
    listing = listing[jax.random.permutation(jax.random.fold_in(own, 1), rows)]
    rotation = jax.random.randint(jax.random.fold_in(own, 2), (rows, 1), 0, top)
    return jnp.take_along_axis(listing, (jnp.arange(top)[None, :] + rotation) % top, axis=1)


def load_shares(count, total, most, lean, full):
    weights = [(1 << 20) // math.isqrt(grade ** lean) + 1 for grade in range(1, count + 1)]
    largest = most if full else min(most, max(-(-total // count), total * weights[0] // sum(weights)))
    least = 1 if total - largest >= count - 1 else 0
    given, rest = [largest] + [least] * (count - 1), total - largest - least * (count - 1)
    while rest > 0:
        movable = [i for i in range(1, count) if given[i] < largest] or [i for i in range(1, count) if given[i] < most]
        mass, budget = sum([weights[i] for i in movable]), rest
        for i in movable:
            more = min(most - given[i], max(1, budget * weights[i] // mass), rest)
            given[i] = given[i] + more
            rest = rest - more
    return np.array(given)


def normal_values(stream_key, extent, spread, limit, cuts=(), held_as=jnp.bfloat16):
    values = jax.random.normal(stream_key, extent, jnp.float32) * spread
    if len(cuts) > 0:
        values = shard_levels(stream_key, extent, cuts, -0.22, 0.18) * values
    return jnp.clip(values, min=-limit, max=limit).astype(held_as)


def setup_inputs(seed: int = 0) -> dict:
    seeds = jax.random.split(jax.random.key(seed), 16)
    block_input = normal_values(seeds[0], (SEQS, SEQ_LEN, D), 1.0, 6.0, ((0, 4), (1, 8)))
    attn_gain = jnp.clip(1.0 + 0.1 * jax.random.normal(seeds[1], (D,), jnp.float32), 0.5, 1.5).astype(jnp.bfloat16)
    w_qkv = normal_values(seeds[2], (D, 3 * D), D ** -0.5, 0.21875, ((0, 4),))
    w_out = normal_values(seeds[3], (D, D), (D // 16) ** -0.5, 0.875, ((0, 4),))
    ffn_gain = jnp.clip(1.0 + 0.1 * jax.random.normal(seeds[4], (D,), jnp.float32), 0.5, 1.5).astype(jnp.bfloat16)
    w_router = normal_values(seeds[5], (D, NE), D ** -0.5, 0.21875, ((0, 4),))
    w_gate = normal_values(seeds[6], (D, NF, FF), D ** -0.5, 0.21875, ((0, 4),))
    w_up = normal_values(seeds[7], (D, NF, FF), D ** -0.5, 0.21875, ((0, 4),))
    w_down = normal_values(seeds[8], (D, NF, FF), (FF // 16) ** -0.5, 0.5, ((0, 4),))
    const_mix = normal_values(seeds[9], (D, 2 * NC), D ** -0.5, 0.21875, ((0, 4),))
    const_vec = normal_values(seeds[10], (D, NC), 2.0, 8.0, ((0, 4),))
    prev_logits = normal_values(seeds[11], (SEQS, SEQ_LEN, NE), 1.5, 8.0, ((0, 4), (1, 8)), jnp.float32)
    routes_keys = jax.random.split(jax.random.fold_in(seeds[12], 1), SEQS * SEQ_LEN // T_BLK)
    routes_turns = jax.random.permutation(jax.random.fold_in(seeds[12], 3), SEQS * SEQ_LEN // T_BLK)
    routes = jax.vmap(lambda own, number: deal_out(jax.random.fold_in(seeds[12], 2), own, number, T_BLK, NE, TOP, MOST, 1))(routes_keys, routes_turns).reshape((SEQS, SEQ_LEN, TOP))
    doc_ids = jax.vmap(lambda own: jnp.searchsorted(jnp.cumsum(ragged(own, DOCS, SEQ_LEN, SEQ_LEN // 2, 0)), jnp.arange(SEQ_LEN), side="right"))(jax.random.split(seeds[13], SEQS)).reshape((SEQS, SEQ_LEN)).astype(jnp.int32)
    d_out = normal_values(seeds[14], (SEQS, SEQ_LEN, D), 1.0, 6.0, ((0, 4), (1, 8)))
    return dict(block_input=block_input, attn_gain=attn_gain, w_qkv=w_qkv, w_out=w_out, ffn_gain=ffn_gain, w_router=w_router, w_gate=w_gate, w_up=w_up, w_down=w_down, const_mix=const_mix, const_vec=const_vec, prev_logits=prev_logits, routes=routes, doc_ids=doc_ids, d_out=d_out)


@jax.custom_vjp
def low(v):
    return lax.optimization_barrier(v.astype(jnp.bfloat16)).astype(jnp.float32)

@jax.custom_vjp
def low_back(v):
    return v

def low_keep(v):
    return (low(v), None)

def low_pass(kept, grad):
    return (grad,)

def back_keep(v):
    return (v, None)

def back_low(kept, grad):
    return (low(grad),)
low.defvjp(low_keep, low_pass)
low_back.defvjp(back_keep, back_low)

def norm_scale(tensor, gain_vec):
    return tensor * lax.rsqrt(lax.optimization_barrier(jnp.mean(tensor * tensor, axis=-1, keepdims=True)) + 1e-05) * gain_vec

def rotary_tables(positions):
    half_dim = HD // 2
    frequency = jnp.exp(jnp.arange(half_dim, dtype=jnp.float32) * (-2.0 * math.log(10000.0) / HD))
    angles = positions.astype(jnp.float32)[:, None] * frequency[None, :]
    return (jnp.cos(angles)[:, None, :], jnp.sin(angles)[:, None, :])

def rotate(tensor, cosine_table, sine_table):
    half_dim = tensor.shape[-1] // 2
    front_half = tensor[..., :half_dim]
    back_half = tensor[..., half_dim:]
    return jnp.concatenate([front_half * cosine_table - back_half * sine_table, back_half * cosine_table + front_half * sine_table], axis=-1)

def attend(queries, key_heads, values, documents):
    length = queries.shape[0]
    scores = low_back(jnp.einsum('qhd,khd->hqk', queries, key_heads, precision=lax.Precision.HIGHEST) * HD ** (-0.5))
    places = jnp.arange(length)
    allowed = (places[:, None] >= places[None, :]) & (documents[:, None] == documents[None, :])
    scores = jnp.where(allowed[None], scores, -1e+30)
    weights = low(jax.nn.softmax(scores, axis=-1))
    return jnp.einsum('hqk,khd->qhd', weights, values, precision=lax.Precision.HIGHEST)

def block_layer(weight_set, token_rows, prev_rows, route_rows, doc_rows):
    attn_gain, w_qkv, w_out, ffn_gain, w_router, w_gate, w_up, w_down, const_mix, const_vec = weight_set
    highest = lax.Precision.HIGHEST
    length = token_rows.shape[0]
    normed = low(norm_scale(token_rows, attn_gain))
    qkv_mixed = low_back(jnp.dot(normed, w_qkv, precision=highest)).reshape(length, 3, H, HD)
    cosine_table, sine_table = rotary_tables(jnp.arange(length))
    queries = low(rotate(qkv_mixed[:, 0], cosine_table, sine_table))
    key_heads = low(rotate(qkv_mixed[:, 1], cosine_table, sine_table))
    values = low(qkv_mixed[:, 2])
    attended = low(low_back(attend(queries, key_heads, values, doc_rows).reshape(length, D)))
    hidden = token_rows + low_back(jnp.dot(attended, w_out, precision=highest))
    unit_norm = norm_scale(hidden, ffn_gain)
    unit_low = low(unit_norm)
    router = jax.nn.softmax(jnp.dot(unit_low, w_router, precision=highest) + prev_rows, axis=-1)
    groups = length // T_BLK
    pair_experts = route_rows.reshape(groups, T_BLK * TOP)
    route_hot = (pair_experts[:, :, None] == jnp.arange(NE)[None, None, :]).astype(jnp.int32)
    pair_ranks = lax.optimization_barrier(jnp.sum((jnp.cumsum(route_hot, axis=1) - route_hot) * route_hot, axis=2))
    stride = NF * MOST + 1
    local_slot = jnp.where(pair_experts < NF, pair_experts * MOST + pair_ranks, NF * MOST)
    slot_index = (local_slot + jnp.arange(groups)[:, None] * stride).reshape(-1).astype(jnp.int32)
    packed = jnp.zeros((groups * stride, D), unit_low.dtype).at[slot_index].add(jnp.repeat(unit_low, TOP, axis=0))
    packed = packed.reshape(groups, stride, D)[:, :NF * MOST].reshape(groups, NF, MOST, D)
    gate_act = low_back(jnp.einsum('gemd,def->gemf', packed, w_gate, precision=highest))
    up_act = low_back(jnp.einsum('gemd,def->gemf', packed, w_up, precision=highest))
    inner_act = low(jax.nn.silu(gate_act) * up_act)
    result = low(low_back(jnp.einsum('gemf,def->gemd', inner_act, w_down, precision=highest)))
    result = jnp.concatenate([result.reshape(groups, NF * MOST, D), jnp.zeros((groups, 1, D), result.dtype)], axis=1)
    routed = result.reshape(groups * stride, D)[slot_index].reshape(length, TOP, D)
    mix_share = jax.nn.softmax(jnp.dot(unit_low, const_mix, precision=highest).reshape(length, NC, 2), axis=-1)
    constant = mix_share[:, :, 0:1] * unit_norm[:, None, :] + mix_share[:, :, 1:2] * const_vec.T[None]
    chosen = route_rows[:, :, None]
    route_value = jnp.where(chosen < NF, routed, 0.0) + (chosen == NF + 1) * unit_norm[:, None, :]
    for const_index in range(NC):
        route_value = route_value + (chosen == NF + 2 + const_index) * constant[:, None, const_index, :]
    gate_probs = jnp.take_along_axis(router, route_rows, axis=1)
    return hidden + lax.optimization_barrier(jnp.sum(gate_probs[:, :, None] * route_value, axis=1))

def reference(block_input, attn_gain, w_qkv, w_out, ffn_gain, w_router, w_gate, w_up, w_down, const_mix, const_vec, prev_logits, routes, doc_ids, d_out):
    weight_set = (attn_gain.astype(jnp.float32), w_qkv.astype(jnp.float32), w_out.astype(jnp.float32), ffn_gain.astype(jnp.float32), w_router.astype(jnp.float32), w_gate.astype(jnp.float32), w_up.astype(jnp.float32), w_down.astype(jnp.float32), const_mix.astype(jnp.float32), const_vec.astype(jnp.float32))

    def forward(inputs, prev_all, weights_now):

        def one_sequence(seq_item):
            token_rows, prev_rows, route_rows, doc_rows = seq_item
            return block_layer(weights_now, token_rows, prev_rows, route_rows, doc_rows)
        return lax.map(jax.checkpoint(one_sequence), (inputs, prev_all, routes, doc_ids))
    output, pullback = jax.vjp(forward, block_input.astype(jnp.float32), prev_logits, weight_set)
    grad_x, grad_prev, grads = pullback(d_out.astype(jnp.float32))
    return (output.astype(jnp.bfloat16), grad_x, grad_prev, grads[0], grads[1], grads[2], grads[3], grads[4], grads[5], grads[6], grads[7], grads[8], grads[9])
```

```python
import functools
import math

import jax
import jax.numpy as jnp
from jax import lax
from jax.experimental import pallas as pl
from jax.experimental.pallas import tpu as pltpu
from jax.sharding import PartitionSpec as P

H = 12
HD = 64
NF = 4
NC = 2
NE = 8
TOP = 2
MOST = 48
BF = jnp.bfloat16
F32 = jnp.float32


def dot(a, b, dims):
    return lax.dot_general(a, b, (dims, ((), ())), preferred_element_type=F32)


def mm(a, b):
    return dot(a, b, ((1,), (0,)))


def mm_nt(a, b):
    return dot(a, b, ((1,), (1,)))


def mm_tn(a, b):
    return dot(a, b, ((0,), (0,)))


def halves_swapped(t):
    half = t.shape[-1] // 2
    return jnp.concatenate([t[:, half:], t[:, :half]], axis=-1)


VMEM = pl.BlockSpec(memory_space=pltpu.VMEM)
SMEM = pl.BlockSpec(memory_space=pltpu.SMEM)


def attend_kernel(dims, meta, start, cos, sin, gain, *refs):
    Z, F, R, D, L, hpd, block = dims
    hw = hpd * HD
    xs, refs = refs[: 2 * Z], refs[2 * Z :]
    ws, refs = refs[:F], refs[F:]
    normed, weight, q_out, k_out, v_out, o_out, lse_out, mine_out, theirs_out = refs
    z, core, f = meta[0], meta[1], meta[2]
    d_local = D // F
    for k in range(F):
        row = pl.multiple_of(lax.rem(f - k + F, F) * d_local, d_local)
        weight[pl.ds(row, d_local), :] = ws[k][...]
    gain_row = gain[...].astype(F32)
    for k in range(Z):
        for side in range(2):
            at = lax.rem(z - k + Z, Z) * 2 + (core if side == 0 else 1 - core)
            tile = xs[side * Z + k][...].astype(F32)
            factor = lax.rsqrt(jnp.mean(tile * tile, axis=-1, keepdims=True) + 1e-05)
            row = pl.multiple_of(at * R, R)
            normed[pl.ds(row, R), :] = (tile * factor * gain_row).astype(BF)

    def project(step, carry):
        rows = pl.ds(pl.multiple_of(step * block, block), block)
        mixed = mm(normed[rows, :], weight[...])
        cosine, sine = cos[rows, :], sin[rows, :]
        for h in range(hpd):
            q = mixed[:, h * HD : (h + 1) * HD]
            k = mixed[:, hw + h * HD : hw + (h + 1) * HD]
            v = mixed[:, 2 * hw + h * HD : 2 * hw + (h + 1) * HD]
            q = (q * cosine + halves_swapped(q) * sine).astype(BF)
            q_out[h, rows, :] = (q.astype(F32) * HD ** (-0.5)).astype(BF)
            k_out[h, rows, :] = (k * cosine + halves_swapped(k) * sine).astype(BF)
            v_out[h, rows, :] = v.astype(BF)
        return carry

    lax.fori_loop(0, L // block, project, 0)

    def query_step(qb, carry):
        rows = pl.ds(pl.multiple_of(qb * block, block), block)
        first = start[rows, :]
        q_pos = qb * block + lax.broadcasted_iota(jnp.int32, (block, block), 0)
        column = lax.broadcasted_iota(jnp.int32, (block, block), 1)
        queries = [q_out[h, rows, :] for h in range(hpd)]

        def key_step(kb, state):
            keys = pl.ds(pl.multiple_of(kb * block, block), block)
            k_pos = kb * block + column
            allowed = (k_pos <= q_pos) & (k_pos >= first)
            new = []
            for h in range(hpd):
                high, total, acc = state[h]
                scores = mm_nt(queries[h], k_out[h, keys, :])
                scores = jnp.where(allowed, scores, -1e30)
                top = jnp.maximum(high, jnp.max(scores, axis=-1, keepdims=True))
                scale = jnp.exp(high - top)
                weights = jnp.where(allowed, jnp.exp(scores - top), 0.0)
                total = total * scale + jnp.sum(weights, axis=-1, keepdims=True)
                acc = acc * scale + mm(weights.astype(BF), v_out[h, keys, :])
                new.append((top, total, acc))
            return tuple(new)

        begin = tuple(
            (
                jnp.full((block, 1), -1e30, F32),
                jnp.zeros((block, 1), F32),
                jnp.zeros((block, HD), F32),
            )
            for _ in range(hpd)
        )
        state = lax.fori_loop(meta[4 + qb], qb + 1, key_step, begin)
        outs = []
        for h in range(hpd):
            high, total, acc = state[h]
            out = acc / total
            o_out[h, rows, :] = out
            lse_out[h, rows, :] = high + jnp.log(total)
            outs.append(out.astype(BF))
        whole = jnp.concatenate(outs, axis=-1)
        for part in range(block // R):
            index = qb * (block // R) + part
            piece = whole[part * R : (part + 1) * R, :]
            chip, parity = lax.div(index, 2), lax.rem(index, 2)

            @pl.when(parity == core)
            def _():
                mine_out[chip] = piece

            @pl.when(parity != core)
            def _():
                theirs_out[chip] = piece

        return carry

    lax.fori_loop(0, L // block, query_step, 0)


def back_kernel(dims, meta, start, cos, sin, gain, *refs):
    Z, F, R, D, L, hpd, block = dims
    hw = hpd * HD
    xs, refs = refs[: 2 * Z], refs[2 * Z :]
    dos, refs = refs[: 2 * Z], refs[2 * Z :]
    (normed, weight, q_in, k_in, v_in, o_in, lse_in), refs = refs[:7], refs[7:]
    (gw_out, gain_out, mine_out, theirs_out), refs = refs[:4], refs[4:]
    do_s, dq_s, dk_s, dv_s, mixed_s = refs
    z, core, f = meta[0], meta[1], meta[2]
    for k in range(Z):
        for side in range(2):
            at = lax.rem(z + k, Z) * 2 + (core if side == 0 else 1 - core)
            row = pl.multiple_of(at * R, R)
            tile = dos[side * Z + k][...]
            for h in range(hpd):
                do_s[h, pl.ds(row, R), :] = tile[:, h * HD : (h + 1) * HD]
    dk_s[...] = jnp.zeros_like(dk_s)
    dv_s[...] = jnp.zeros_like(dv_s)

    def query_step(qb, carry):
        rows = pl.ds(pl.multiple_of(qb * block, block), block)
        first = start[rows, :]
        q_pos = qb * block + lax.broadcasted_iota(jnp.int32, (block, block), 0)
        column = lax.broadcasted_iota(jnp.int32, (block, block), 1)
        queries = [q_in[h, rows, :] for h in range(hpd)]
        upstream = [do_s[h, rows, :] for h in range(hpd)]
        lses = [lse_in[h, rows, :] for h in range(hpd)]
        deltas = [
            jnp.sum(upstream[h].astype(F32) * o_in[h, rows, :], axis=-1, keepdims=True)
            for h in range(hpd)
        ]

        def key_step(kb, state):
            keys = pl.ds(pl.multiple_of(kb * block, block), block)
            k_pos = kb * block + column
            allowed = (k_pos <= q_pos) & (k_pos >= first)
            new = []
            for h in range(hpd):
                key, value = k_in[h, keys, :], v_in[h, keys, :]
                scores = mm_nt(queries[h], key)
                weights = jnp.where(allowed, jnp.exp(scores - lses[h]), 0.0)
                dp = mm_nt(upstream[h], value)
                ds = (weights * (dp - deltas[h])).astype(BF)
                dv_s[h, keys, :] += mm_tn(weights.astype(BF), upstream[h])
                dk_s[h, keys, :] += mm_tn(ds, queries[h])
                new.append(state[h] + mm(ds, key))
            return tuple(new)

        begin = tuple(jnp.zeros((block, HD), F32) for _ in range(hpd))
        state = lax.fori_loop(meta[4 + qb], qb + 1, key_step, begin)
        for h in range(hpd):
            dq_s[h, rows, :] = state[h]
        return carry

    lax.fori_loop(0, L // block, query_step, 0)

    def unrotate(step, carry):
        rows = pl.ds(pl.multiple_of(step * block, block), block)
        cosine, sine = cos[rows, :], sin[rows, :]
        parts = [[], [], []]
        for h in range(hpd):
            dq = dq_s[h, rows, :] * HD ** (-0.5)
            dk = dk_s[h, rows, :]
            parts[0].append((dq * cosine - halves_swapped(dq) * sine).astype(BF))
            parts[1].append((dk * cosine - halves_swapped(dk) * sine).astype(BF))
            parts[2].append(dv_s[h, rows, :].astype(BF))
        mixed_s[rows, :] = jnp.concatenate(parts[0] + parts[1] + parts[2], axis=-1)
        return carry

    lax.fori_loop(0, L // block, unrotate, 0)
    gw_out[...] = mm_tn(normed[...], mixed_s[...]).astype(BF)
    total = jnp.zeros((1, D), F32)
    for k in range(Z):
        for side in range(2):
            chip = lax.rem(z - k + Z, Z)
            at = chip * 2 + (core if side == 0 else 1 - core)
            tile = xs[side * Z + k][...].astype(F32)
            factor = lax.rsqrt(jnp.mean(tile * tile, axis=-1, keepdims=True) + 1e-05)
            row = pl.multiple_of(at * R, R)
            dn = mm_nt(mixed_s[pl.ds(row, R), :], weight[...])
            total = total + jnp.sum(dn * (tile * factor), axis=0, keepdims=True)
            if side == 0:
                mine_out[chip] = dn.astype(BF)
            else:
                theirs_out[chip] = dn.astype(BF)
    gain_out[...] = total


def body(
    block_input,
    attn_gain,
    w_qkv,
    w_out,
    ffn_gain,
    w_router,
    w_gate,
    w_up,
    w_down,
    const_mix,
    const_vec,
    prev_logits,
    routes,
    doc_ids,
    d_out,
    *,
    F,
    C,
):
    S, R, D = block_input.shape
    L = doc_ids.shape[1]
    Z = C // 2
    G = C // S
    hpd = -(-H // G)
    hw = hpd * HD
    FF = w_gate.shape[2]
    per = F // NF
    CW = FF // (2 * per)
    d_local = D // F
    T = S * R
    block = min(256, L)
    highest = lax.Precision.HIGHEST
    f = lax.axis_index("fsdp")
    c = lax.axis_index("ctx")
    core = c % 2
    z = c // 2

    def fs(t, k):
        return lax.ppermute(t, "fsdp", [(i, (i + k) % F) for i in range(F)])

    def zs(t, k):
        return lax.ppermute(
            t, "ctx", [(2 * i + j, 2 * ((i + k) % Z) + j) for i in range(Z) for j in range(2)]
        )

    def cx(t):
        return lax.ppermute(t, "ctx", [(i, i ^ 1) for i in range(C)])

    def pick(t, index, axis=0):
        return lax.dynamic_index_in_dim(t, index, axis, keepdims=False)

    def natural(pieces, at):
        out = jnp.zeros((len(pieces),) + pieces[0].shape, pieces[0].dtype)
        for piece, index in zip(pieces, at):
            out = lax.dynamic_update_index_in_dim(out, piece, index, 0)
        return out

    def gathered(t):
        return natural([t] + [fs(t, k) for k in range(1, F)], [(f - k) % F for k in range(F)])

    def seq_of(chip):
        return chip // (Z // S)

    x_mine = [pick(block_input, seq_of(z))] + [
        zs(pick(block_input, seq_of((z + k) % Z)), k) for k in range(1, Z)
    ]
    x_theirs = [cx(t) for t in x_mine]
    small = jnp.concatenate(
        [attn_gain[None], ffn_gain[None], w_router.T, const_mix.T, const_vec.T], axis=0
    )
    small = gathered(small).transpose(1, 0, 2).reshape(-1, D)
    hg = c % G
    heads = w_qkv.reshape(d_local, 3, H, HD)
    heads = jnp.pad(heads, ((0, 0), (0, 0), (0, G * hpd - H), (0, 0)))
    mine_w = lax.dynamic_slice_in_dim(heads, hg * hpd, hpd, 2).reshape(d_local, 3 * hw)
    w_pieces = [mine_w] + [fs(mine_w, k) for k in range(1, F)]
    half = lax.dynamic_slice_in_dim(w_out, core * (D // 2), D // 2, 1)
    half = gathered(half).reshape(D, D // 2)
    other = cx(half)
    out_weight = jnp.where(
        core == 0,
        jnp.concatenate([half, other], axis=1),
        jnp.concatenate([other, half], axis=1),
    )
    out_weight = jnp.pad(out_weight, ((0, G * hw - D), (0, 0)))

    def expert_of(dev):
        return dev // per

    def chunk_of(dev, side):
        return (dev % per) * 2 + side

    trio = jnp.stack([w_gate, w_up, w_down])

    def expert_slice(dev):
        part = lax.dynamic_slice_in_dim(trio, chunk_of(dev, core) * CW, CW, 3)
        return pick(part, expert_of(dev), 2)

    e_pieces = [expert_slice(f)] + [fs(expert_slice((f + k) % F), k) for k in range(1, F)]
    experts = natural(e_pieces, [(f - k) % F for k in range(F)])
    experts = experts.transpose(1, 0, 2, 3).reshape(3, D, CW)
    gate_w, up_w, down_w = experts[0], experts[1], experts[2]

    my_docs = pick(doc_ids, c // G)
    start = jnp.sum((my_docs[None, :] < my_docs[:, None]).astype(jnp.int32), axis=1)
    first_block = start.reshape(L // block, block)[:, 0] // block
    meta = jnp.concatenate([jnp.stack([z, core, f, c]).astype(jnp.int32), first_block])
    frequency = jnp.exp(jnp.arange(HD // 2, dtype=F32) * (-2.0 * math.log(10000.0) / HD))
    angles = jnp.arange(L).astype(F32)[:, None] * frequency[None, :]
    cosine, sine = jnp.cos(angles), jnp.sin(angles)
    cosine = jnp.concatenate([cosine, cosine], axis=1)
    sine = jnp.concatenate([-sine, sine], axis=1)
    dims = (Z, F, R, D, L, hpd, block)
    shaped = jax.ShapeDtypeStruct
    normed, qkv_w, q, k, v, o, lse, att_mine, att_theirs = pl.pallas_call(
        functools.partial(attend_kernel, dims),
        out_shape=(
            shaped((L, D), BF),
            shaped((D, 3 * hw), BF),
            shaped((hpd, L, HD), BF),
            shaped((hpd, L, HD), BF),
            shaped((hpd, L, HD), BF),
            shaped((hpd, L, HD), F32),
            shaped((hpd, L, 1), F32),
            shaped((Z, R, hw), BF),
            shaped((Z, R, hw), BF),
        ),
        in_specs=[SMEM] + [VMEM] * (4 + 2 * Z + F),
        out_specs=tuple([VMEM] * 9),
        name="attend",
    )(meta, start[:, None], cosine, sine, small[0:1], *x_mine, *x_theirs, *w_pieces)

    both = jnp.stack([att_mine, cx(att_theirs)], axis=1)
    pieces = [pick(both, z)] + [zs(pick(both, (z + k) % Z), k) for k in range(1, Z)]
    attended = jnp.zeros((S * G, R, hw), BF)
    for k_at, piece in enumerate(pieces):
        chip = (z - k_at) % Z
        attended = lax.dynamic_update_index_in_dim(attended, piece[0], chip * 2 + core, 0)
        attended = lax.dynamic_update_index_in_dim(attended, piece[1], chip * 2 + 1 - core, 0)
    attended = attended.reshape(S, G, R, hw).transpose(0, 2, 1, 3).reshape(T, G * hw)
    source = block_input.astype(F32)
    hidden = source + mm(attended, out_weight).reshape(S, R, D)
    factor_two = lax.rsqrt(jnp.mean(hidden * hidden, axis=-1, keepdims=True) + 1e-05)
    gain_two = small[1].astype(F32)
    unit_norm = hidden * factor_two * gain_two
    unit_low = unit_norm.astype(BF)
    unit_flat = unit_low.reshape(T, D)
    router_t, mix_t, vec_t = small[2:10], small[10:14], small[14:16]
    logits = mm_nt(unit_flat, router_t).reshape(S, R, NE) + prev_logits
    router = jax.nn.softmax(logits, axis=-1)
    route_hot = (routes[..., None] == jnp.arange(NE)).astype(jnp.int32)
    flat_hot = route_hot.reshape(S, R * TOP, NE)
    pair_ranks = jnp.sum((jnp.cumsum(flat_hot, axis=1) - flat_hot) * flat_hot, axis=2).reshape(
        S, R, TOP
    )
    slot_ids = jnp.where(routes < NF, routes * MOST + pair_ranks, -1)
    slot_range = jnp.arange(NF * MOST)
    picks = [
        (slot_ids[:, None, :, w] == slot_range[None, :, None]).astype(BF) for w in range(TOP)
    ]
    route_float = route_hot.astype(F32)
    gate_probs = jnp.sum(router[:, :, None, :] * route_float, axis=-1)
    upstream = d_out.astype(F32)
    value_grads = [gate_probs[..., w, None] * upstream for w in range(TOP)]
    packed = jnp.einsum(
        "sct,std->scd", picks[0] + picks[1], unit_low, preferred_element_type=F32
    ).astype(BF)
    result_grad = sum(
        jnp.einsum(
            "sct,std->scd", picks[w], value_grads[w].astype(BF), preferred_element_type=F32
        )
        for w in range(TOP)
    ).astype(BF)
    tok = jnp.stack([packed, result_grad]).reshape(2, S, NF, MOST, D).transpose(2, 0, 1, 3, 4)
    own = [pick(tok, expert_of(f))] + [
        fs(pick(tok, expert_of((f + k) % F)), k) for k in range(1, F)
    ]
    own = jnp.stack(own, axis=1).reshape(2, F * S * MOST, D)
    pair = jnp.concatenate([own, cx(own)], axis=1)

    def activations(rows):
        gate_act, up_act = mm(rows[0], gate_w), mm(rows[0], up_w)
        inner_grad = mm(rows[1], down_w)
        sig = jax.nn.sigmoid(gate_act)
        act = gate_act * sig
        inner = (act * up_act).astype(BF)
        gate_grad = (inner_grad * up_act * sig * (1.0 + gate_act * (1.0 - sig))).astype(BF)
        up_grad = (inner_grad * act).astype(BF)
        return inner, gate_grad, up_grad

    def weight_grads(rows, acts):
        inner, gate_grad, up_grad = acts
        return mm_tn(rows[0], gate_grad), mm_tn(rows[0], up_grad), mm_tn(rows[1], inner)

    acts = activations(pair)
    inner, gate_grad, up_grad = acts
    back = jnp.stack(
        [mm_nt(inner, down_w), mm_nt(gate_grad, gate_w) + mm_nt(up_grad, up_w)]
    )
    half_rows = F * S * MOST
    back = back[:, :half_rows] + cx(back[:, half_rows:].astype(BF)).astype(F32)
    back = back.astype(BF).reshape(2, F, S, MOST, D)
    ret = [back[:, 0]] + [fs(back[:, k], -k) for k in range(1, F)]
    ret = natural(ret, [(f + k) % F for k in range(F)])
    if per > 1:
        ret = jnp.sum(ret.reshape(NF, per, 2, S, MOST, D).astype(F32), axis=1).astype(BF)
    ret = ret.transpose(1, 2, 0, 3, 4).reshape(2, S, NF * MOST, D)
    result, packed_grad = ret[0], ret[1]

    grads = weight_grads(pair, acts)
    travelling = own
    for _ in range(1, Z):
        travelling = zs(travelling, 1)
        rows = jnp.concatenate([travelling, cx(travelling)], axis=1)
        more = weight_grads(rows, activations(rows))
        grads = tuple(a + b for a, b in zip(grads, more))

    mix_share = jax.nn.softmax(mm_nt(unit_flat, mix_t).reshape(S, R, NC, 2), axis=-1)
    vectors = vec_t.astype(F32)
    constant = (
        mix_share[..., 0:1] * unit_norm[:, :, None, :] + mix_share[..., 1:2] * vectors[None, None]
    )
    values = []
    for w in range(TOP):
        expert_now = routes[:, :, w][..., None]
        current = jnp.einsum("sct,scd->std", picks[w], result, preferred_element_type=F32)
        current = current + (expert_now == NF + 1) * unit_norm
        for i in range(NC):
            current = current + (expert_now == NF + 2 + i) * constant[:, :, i]
        values.append(current)
    mixture = gate_probs[..., 0, None] * values[0] + gate_probs[..., 1, None] * values[1]
    out_block = (hidden + mixture).astype(BF)
    gate_grads = [jnp.sum(upstream * values[w], axis=-1) for w in range(TOP)]
    unit_grad = jnp.einsum(
        "sct,scd->std", picks[0] + picks[1], packed_grad, preferred_element_type=F32
    )
    prob_grad = sum(route_float[:, :, w] * gate_grads[w][..., None] for w in range(TOP))
    grad_prev = router * (prob_grad - jnp.sum(router * prob_grad, axis=-1, keepdims=True))
    unit_wide = unit_flat.astype(F32)
    grad_router = jnp.dot(grad_prev.reshape(-1, NE).T, unit_wide, precision=highest)
    unit_grad = unit_grad + jnp.dot(grad_prev, router_t.astype(F32), precision=highest)
    const_grad = jnp.stack(
        [
            sum(
                (routes[:, :, w] == NF + 2 + i)[..., None] * value_grads[w] for w in range(TOP)
            )
            for i in range(NC)
        ],
        axis=2,
    )
    grad_vec = jnp.sum(mix_share[..., 1:2] * const_grad, axis=(0, 1))
    share_grad = jnp.stack(
        [
            jnp.sum(const_grad * unit_norm[:, :, None, :], axis=-1),
            jnp.sum(const_grad * vectors[None, None], axis=-1),
        ],
        axis=-1,
    )
    mix_grad = (
        mix_share * (share_grad - jnp.sum(mix_share * share_grad, axis=-1, keepdims=True))
    ).reshape(-1, 2 * NC)
    grad_mix = jnp.dot(mix_grad.T, unit_wide, precision=highest)
    unit_grad = unit_grad + jnp.dot(mix_grad, mix_t.astype(F32), precision=highest).reshape(S, R, D)
    unit_grad = unit_grad + jnp.sum(mix_share[..., 0:1] * const_grad, axis=2)
    for w in range(TOP):
        unit_grad = unit_grad + (routes[:, :, w] == NF + 1)[..., None] * value_grads[w]
    normal = hidden * factor_two
    scaled = unit_grad * gain_two
    grad_gain_two = jnp.sum(unit_grad * normal, axis=(0, 1))
    hidden_grad = upstream + factor_two * (
        scaled - normal * jnp.mean(scaled * normal, axis=-1, keepdims=True)
    )
    proj_grad = hidden_grad.astype(BF).reshape(T, D)
    grad_out = mm_tn(attended, proj_grad)[:D]
    att_grad = mm_nt(proj_grad, out_weight).astype(BF)
    att_grad = att_grad.reshape(S, R, G, hw).transpose(0, 2, 1, 3).reshape(S * G, R, hw)

    def for_chip(chip):
        return jnp.stack([pick(att_grad, chip * 2 + core), pick(att_grad, chip * 2 + 1 - core)])

    do_pieces = [for_chip(z)] + [zs(for_chip((z - k) % Z), -k) for k in range(1, Z)]
    do_mine = [t[0] for t in do_pieces]
    do_theirs = [cx(t[1]) for t in do_pieces]
    gw, gain_part, dn_mine, dn_theirs = pl.pallas_call(
        functools.partial(back_kernel, dims),
        out_shape=(
            shaped((D, 3 * hw), BF),
            shaped((1, D), F32),
            shaped((Z, R, D), BF),
            shaped((Z, R, D), BF),
        ),
        in_specs=[SMEM] + [VMEM] * (4 + 4 * Z + 7),
        out_specs=tuple([VMEM] * 4),
        scratch_shapes=[
            pltpu.VMEM((hpd, L, HD), BF),
            pltpu.VMEM((hpd, L, HD), F32),
            pltpu.VMEM((hpd, L, HD), F32),
            pltpu.VMEM((hpd, L, HD), F32),
            pltpu.VMEM((L, 3 * hw), BF),
        ],
        name="attend_back",
    )(
        meta,
        start[:, None],
        cosine,
        sine,
        small[0:1],
        *x_mine,
        *x_theirs,
        *do_mine,
        *do_theirs,
        normed,
        qkv_w,
        q,
        k,
        v,
        o,
        lse,
    )
    dn = dn_mine.astype(F32) + cx(dn_theirs).astype(F32)
    dn = dn.astype(BF)
    dn_pieces = [pick(dn, z)] + [zs(pick(dn, (z + k) % Z), k) for k in range(1, Z)]
    dn_all = natural(dn_pieces, [(z - k) % Z for k in range(Z)])
    normed_grad = jnp.sum(dn_all.reshape(S, Z // S, R, D).astype(F32), axis=1)
    gain_one = small[0].astype(F32)
    factor_one = lax.rsqrt(jnp.mean(source * source, axis=-1, keepdims=True) + 1e-05)
    normal_one = source * factor_one
    scaled_one = normed_grad * gain_one
    grad_x = hidden_grad + factor_one * (
        scaled_one - normal_one * jnp.mean(scaled_one * normal_one, axis=-1, keepdims=True)
    )

    def rows_summed(t):
        parts = [pick(t, f)] + [fs(pick(t, (f + k) % F), k) for k in range(1, F)]
        return sum(p.astype(F32) for p in parts).astype(BF)

    def over_ctx(t):
        step = 1
        while step < C:
            moved = lax.ppermute(t, "ctx", [(i, i ^ step) for i in range(C)])
            t = (t.astype(F32) + moved.astype(F32)).astype(BF)
            step *= 2
        return t

    gain_rows = gain_part.reshape(F, 1, d_local)
    gain_rows = jnp.pad(gain_rows, ((0, 0), (0, 15), (0, 3 * hw - d_local)))
    payload = jnp.concatenate([gw.reshape(F, d_local, 3 * hw), gain_rows.astype(BF)], axis=1)
    payload = rows_summed(payload)
    summed = payload.astype(F32)
    for j in range(1, S):
        moved = lax.ppermute(payload, "ctx", [(i, (i + j * G) % C) for i in range(C)])
        summed = summed + moved.astype(F32)
    payload = summed.astype(BF)[None]
    step = 1
    while step < G:
        moved = lax.ppermute(payload, "ctx", [(i, i ^ step) for i in range(C)])
        payload = jnp.concatenate([payload, moved], axis=0)
        step *= 2
    qkv_all = jnp.stack([pick(payload, hg ^ i) for i in range(G)])
    grad_gain_one = jnp.sum(qkv_all[:, d_local, :d_local].astype(F32), axis=0)
    grad_qkv = qkv_all[:, :d_local].reshape(G, d_local, 3, hw).transpose(1, 2, 0, 3)
    grad_qkv = grad_qkv.reshape(d_local, 3, G * hw)[:, :, :D].reshape(d_local, 3 * D).astype(F32)

    smalls = jnp.concatenate([grad_gain_two[None], grad_router, grad_mix, grad_vec], axis=0)
    smalls = jnp.pad(smalls, ((0, 1), (0, 0))).reshape(16, F, d_local).transpose(1, 0, 2)
    smalls = jnp.pad(smalls, ((0, 0), (0, 0), (0, D - d_local)))
    payload = jnp.concatenate([grad_out.reshape(F, d_local, D), smalls], axis=1).astype(BF)
    payload = over_ctx(rows_summed(payload)).astype(F32)
    grad_w_out = payload[:d_local]
    smalls = payload[d_local:, :d_local]

    blocks = jnp.stack(grads).astype(BF).reshape(3, F, d_local, CW)
    parts = [pick(blocks, f, 1)] + [fs(pick(blocks, (f + k) % F, 1), k) for k in range(1, F)]
    ours = natural(parts, [(f - k) % F for k in range(F)])
    theirs = cx(ours)
    ordered = jnp.where(
        core == 0, jnp.stack([ours, theirs], axis=1), jnp.stack([theirs, ours], axis=1)
    )
    ordered = ordered.reshape(NF, per, 2, 3, d_local, CW).transpose(3, 4, 0, 1, 2, 5)
    ordered = ordered.reshape(3, d_local, NF, FF).astype(F32)
    return (
        out_block,
        grad_x,
        grad_prev,
        grad_gain_one,
        grad_qkv,
        grad_w_out,
        smalls[0],
        smalls[1:9].T,
        ordered[0],
        ordered[1],
        ordered[2],
        smalls[9:13].T,
        smalls[13:15].T,
    )


def solution(mesh):
    return jax.shard_map(
        functools.partial(body, F=mesh.shape["fsdp"], C=mesh.shape["ctx"]),
        mesh=mesh,
        in_specs=(
            P("fsdp", "ctx", None),
            P("fsdp"),
            P("fsdp", None),
            P("fsdp", None),
            P("fsdp"),
            P("fsdp", None),
            P("fsdp", None, None),
            P("fsdp", None, None),
            P("fsdp", None, None),
            P("fsdp", None),
            P("fsdp", None),
            P("fsdp", "ctx", None),
            P("fsdp", "ctx", None),
            P("fsdp", None),
            P("fsdp", "ctx", None),
        ),
        out_specs=(
            P("fsdp", "ctx", None),
            P("fsdp", "ctx", None),
            P("fsdp", "ctx", None),
            P("fsdp"),
            P("fsdp", None),
            P("fsdp", None),
            P("fsdp"),
            P("fsdp", None),
            P("fsdp", None, None),
            P("fsdp", None, None),
            P("fsdp", None, None),
            P("fsdp", None),
            P("fsdp", None),
        ),
        check_vma=False,
    )
```

```python
import functools
import math

import jax
import jax.numpy as jnp
from jax import lax
from jax.experimental import pallas as pl
from jax.experimental.pallas import tpu as pltpu
from jax.sharding import PartitionSpec as P


H = 12
HD = 64
NF = 4
NC = 2
NE = 8
TOP = 2
MOST = 48
BF = jnp.bfloat16
F32 = jnp.float32


def dot(a, b, dims):
    return lax.dot_general(a, b, (dims, ((), ())), preferred_element_type=F32)


def mm(a, b):
    return dot(a, b, ((1,), (0,)))


def mm_nt(a, b):
    return dot(a, b, ((1,), (1,)))


def mm_tn(a, b):
    return dot(a, b, ((0,), (0,)))


def halves_swapped(t):
    half = t.shape[-1] // 2
    return jnp.concatenate([t[:, half:], t[:, :half]], axis=-1)


VMEM = pl.BlockSpec(memory_space=pltpu.VMEM)
SMEM = pl.BlockSpec(memory_space=pltpu.SMEM)


GRANTS = {
    "pack": 3,
    "grad_rows": 3,
    "order": 8,
    "attend": 14,
    "dispatch": 6,
    "experts0": 24,
    "experts": 14,
    "combine": 16,
    "expert_grads": 18,
    "attend_back": 20,
    "pair": 3,
    "input_grad": 6,
    "place": 13,
    "qkv_grad": 5,
}


def params(name, long=False):
    return pltpu.CompilerParams(vmem_limit_bytes=(56 if long else GRANTS[name]) << 20)


def norm_of(tile):
    return lax.rsqrt(jnp.mean(tile * tile, axis=-1, keepdims=True) + 1e-05)


def split(t):
    high = t.astype(BF)
    return high, (t - high.astype(F32)).astype(BF)


def pack_kernel(dims, meta, w_qkv, gain_a, gain_f, router, mix, vec, first):
    F, D, G, hpd = dims
    hw = hpd * HD
    d_local = D // F
    group = lax.rem(meta[3], G)
    for g in range(G):
        width = max(0, min(hw, H * HD - g * hw))

        @pl.when(group == g)
        def _():
            for part in range(3):
                if width:
                    first[:d_local, part * hw : part * hw + width] = w_qkv[
                        :, part * H * HD + g * hw : part * H * HD + g * hw + width
                    ]
                if width < hw:
                    first[:d_local, part * hw + width : (part + 1) * hw] = jnp.zeros(
                        (d_local, hw - width), BF
                    )

    rows = [t[...].astype(F32) for t in (gain_a, gain_f, router, mix, vec)]
    first[d_local:, :d_local] = jnp.concatenate(rows, axis=0).astype(BF)
    if d_local < 3 * hw:
        first[d_local:, d_local:] = jnp.zeros((16, 3 * hw - d_local), BF)


def grad_rows_kernel(dims, meta, grad, routes, slots, *outs):
    F, S, R, _, expert_of = dims
    table = outs[-1]
    below = lax.broadcasted_iota(jnp.int32, (R, R), 0)
    earlier = (below < lax.broadcasted_iota(jnp.int32, (R, R), 1)).astype(F32).astype(BF)
    expert = lax.broadcasted_iota(jnp.int32, (8, R), 0)
    for s in range(S):
        named = [routes[2 * s + w : 2 * s + w + 1, :] for w in range(TOP)]
        hots = [(expert == t).astype(F32) for t in named]
        counts = mm((hots[0] + hots[1]).astype(BF), earlier)
        lines = []
        for w in range(TOP):
            rank = jnp.sum(hots[w] * counts, axis=0, keepdims=True).astype(jnp.int32)
            line = jnp.where(named[w] < NF, named[w] * MOST + rank, -1)
            slots[2 * s + w : 2 * s + w + 1, :] = line
            lines.append(line)
        slot = lax.broadcasted_iota(jnp.int32, (NF * MOST, R), 0)
        picks = (slot == lines[0]) | (slot == lines[1])
        moved = mm(picks.astype(F32).astype(BF), grad[s]).astype(BF)
        for e in range(NF):
            table[e, s * MOST : (s + 1) * MOST, :] = moved[e * MOST : (e + 1) * MOST, :]
    for k in range(F):
        outs[k][...] = table[expert_of(lax.rem(meta[2] + k, F))]


def order_kernel(dims, meta, *refs):
    F = dims
    for k in range(F):
        e = lax.rem(meta[2] + k, F)
        for i in range(3):
            refs[3 + k][i] = refs[i][e]


def attend_kernel(dims, meta, start, cos, sin, *refs):
    Z, F, R, D, L, hpd, block = dims
    hw = hpd * HD
    xs, refs = refs[: 2 * Z], refs[2 * Z :]
    ws, refs = refs[:F], refs[F:]
    normed, weight, small_out, q_out, k_out, v_out, o_out, lse_out = refs[:8]
    pieces, small_s, att_s = refs[8 : 8 + Z], refs[8 + Z], refs[9 + Z]
    z, core, f = meta[0], meta[1], meta[2]
    d_local = D // F
    for k in range(F):
        row = pl.multiple_of(lax.rem(f - k + F, F) * d_local, d_local)
        weight[pl.ds(row, d_local), :] = ws[k][:d_local, :]
        small_s[k] = ws[k][d_local:, :d_local].astype(F32)
    small = jnp.concatenate([small_s[lax.rem(f - i + F, F)] for i in range(F)], axis=1)
    small_out[...] = small
    gain_row = small[0:1, :]
    for k in range(Z):
        for side in range(2):
            at = lax.rem(z - k + Z, Z) * 2 + (core if side == 0 else 1 - core)
            tile = xs[side * Z + k][...].astype(F32)
            row = pl.multiple_of(at * R, R)
            normed[pl.ds(row, R), :] = (tile * norm_of(tile) * gain_row).astype(BF)

    def project(step, carry):
        rows = pl.ds(pl.multiple_of(step * block, block), block)
        mixed = mm(normed[rows, :], weight[...])
        cosine, sine = cos[rows, :], sin[rows, :]
        for h in range(hpd):
            q = mixed[:, h * HD : (h + 1) * HD]
            k = mixed[:, hw + h * HD : hw + (h + 1) * HD]
            v = mixed[:, 2 * hw + h * HD : 2 * hw + (h + 1) * HD]
            q = (q * cosine + halves_swapped(q) * sine).astype(BF)
            q_out[h, rows, :] = (q.astype(F32) * HD ** (-0.5)).astype(BF)
            k_out[h, rows, :] = (k * cosine + halves_swapped(k) * sine).astype(BF)
            v_out[h, rows, :] = v.astype(BF)
        return carry

    lax.fori_loop(0, L // block, project, 0)

    def query_step(qb, carry):
        rows = pl.ds(pl.multiple_of(qb * block, block), block)
        first = start[rows, :]
        q_pos = qb * block + lax.broadcasted_iota(jnp.int32, (block, block), 0)
        column = lax.broadcasted_iota(jnp.int32, (block, block), 1)
        queries = [q_out[h, rows, :] for h in range(hpd)]

        def key_step(kb, state):
            keys = pl.ds(pl.multiple_of(kb * block, block), block)
            k_pos = kb * block + column
            allowed = (k_pos <= q_pos) & (k_pos >= first)
            new = []
            for h in range(hpd):
                high, total, acc = state[h]
                scores = mm_nt(queries[h], k_out[h, keys, :])
                scores = jnp.where(allowed, scores, -1e30)
                top = jnp.maximum(high, jnp.max(scores, axis=-1, keepdims=True))
                scale = jnp.exp(high - top)
                weights = jnp.where(allowed, jnp.exp(scores - top), 0.0)
                total = total * scale + jnp.sum(weights, axis=-1, keepdims=True)
                acc = acc * scale + mm(weights.astype(BF), v_out[h, keys, :])
                new.append((top, total, acc))
            return tuple(new)

        begin = tuple(
            (
                jnp.full((block, 1), -1e30, F32),
                jnp.zeros((block, 1), F32),
                jnp.zeros((block, HD), F32),
            )
            for _ in range(hpd)
        )
        state = lax.fori_loop(meta[4 + qb], qb + 1, key_step, begin)
        outs = []
        for h in range(hpd):
            high, total, acc = state[h]
            out = acc / total
            o_out[h, rows, :] = out
            lse_out[h, rows, :] = high + jnp.log(total)
            outs.append(out.astype(BF))
        whole = jnp.concatenate(outs, axis=-1)
        for part in range(block // R):
            att_s[qb * (block // R) + part] = whole[part * R : (part + 1) * R, :]
        return carry

    lax.fori_loop(0, L // block, query_step, 0)
    for k in range(Z):
        chip = lax.rem(z + k, Z) * 2
        pieces[k][0] = att_s[chip + core]
        pieces[k][1] = att_s[chip + 1 - core]


def piece_at(dims, meta, k, side):
    Z, G = dims
    chip = lax.rem(meta[0] - k + Z, Z)
    group = lax.rem(2 * chip + (meta[1] if side == 0 else 1 - meta[1]), G)
    return lax.div(2 * chip, G), group


def columns_of(prev, routes, s):
    width = prev.shape[2]
    gap = jnp.zeros((2, width), F32)
    tall = jnp.concatenate([gap, prev[s], jnp.zeros((6, width), F32)], axis=0)
    named = routes[2 * s : 2 * s + 2, :].astype(F32)
    named = jnp.concatenate([named, jnp.zeros((6, width), F32)], axis=0)
    return tall.T, named.T.astype(jnp.int32)


def router_parts(logits, prev, routes):
    lane = lax.broadcasted_iota(jnp.int32, logits.shape, 1)
    inside = (lane >= 2) & (lane < 2 + NE)
    shown = jnp.where(inside, logits + prev, -1e30)
    weights = jnp.exp(shown - jnp.max(shown, axis=-1, keepdims=True))
    weights = jnp.where(inside, weights, 0.0)
    router = weights / jnp.sum(weights, axis=-1, keepdims=True)
    hots = [lane == routes[:, w : w + 1] + 2 for w in range(TOP)]
    gates = [jnp.sum(jnp.where(hot, router, 0.0), axis=-1, keepdims=True) for hot in hots]
    return lane, router, hots, gates


def dispatch_kernel(dims, meta, x, small, prev, routes, slots, *refs):
    Z, F, S, R, D, G, hw, expert_of = dims
    atts, refs = refs[: 2 * Z], refs[2 * Z :]
    ws, refs = refs[:F], refs[F:]
    hidden, w_full, toks, table = refs[0], refs[1], refs[2:-1], refs[-1]

    def att(k, side):
        return atts[k][0] if side == 0 else atts[Z + k][...]

    f = meta[2]
    d_local = D // F
    if G * hw > D:
        w_full[D:, :] = jnp.zeros((G * hw - D, D), BF)
    for k in range(F):
        row = pl.multiple_of(lax.rem(f - k + F, F) * d_local, d_local)
        w_full[pl.ds(row, d_local), :] = ws[k][...]
    for s in range(S):
        hidden[s * R : (s + 1) * R, :] = x[s].astype(F32)
    for k in range(Z):
        for side in range(2):
            seq, group = piece_at((Z, G), meta, k, side)
            rows = pl.ds(pl.multiple_of(seq * R, R), R)
            heads = pl.ds(pl.multiple_of(group * hw, hw), hw)
            hidden[rows, :] += mm(att(k, side), w_full[heads, :])
    gain = small[1:2, :]
    small_low = small[...].astype(BF)
    for s in range(S):
        at = slice(s * R, (s + 1) * R)
        tile = hidden[at, :]
        unit_low = (tile * norm_of(tile) * gain).astype(BF)
        logits = mm_nt(unit_low, small_low)
        _, _, _, gates = router_parts(logits, *columns_of(prev, routes, s))
        slot = lax.broadcasted_iota(jnp.int32, (NF * MOST, R), 0)
        picks = [
            (slot == slots[2 * s + w : 2 * s + w + 1, :]).astype(F32).astype(BF)
            for w in range(TOP)
        ]
        packed = mm(picks[0] + picks[1], unit_low).astype(BF)
        wide = lax.broadcasted_iota(jnp.int32, (R, 128), 1)
        columns = jnp.zeros((NF * MOST, 128), F32)
        for w in range(TOP):
            high, low = split(gates[w])
            both = jnp.where(
                wide == 0, high.astype(F32), jnp.where(wide == 1, low.astype(F32), 0.0)
            )
            columns = columns + mm(picks[w], both.astype(BF))
        for e in range(NF):
            to = slice(s * MOST, (s + 1) * MOST)
            table[e, to, :D] = packed[e * MOST : (e + 1) * MOST, :]
            table[e, to, D:] = columns[e * MOST : (e + 1) * MOST, :].astype(BF)
    for k in range(F):
        toks[k][...] = table[expert_of(lax.rem(f + k, F))]


def ffn_kernel(dims, own, meta, rows_a, rows_b, g_a, g_b, *refs):
    F, D = dims
    n = rows_a.shape[0]
    ws, refs = refs[:F], refs[F:]
    (inner_out, gate_out, up_out, xt_out, drt_out), refs = refs[:5], refs[5:]
    if own:
        mine_out, theirs_out, x_s, dr_s, w_s, acc = refs
    else:
        x_s, dr_s, w_s = refs
    step = pl.program_id(0)
    d_local = D // F

    @pl.when(step == 0)
    def _():
        for i, (rows, g) in enumerate(((rows_a, g_a), (rows_b, g_b))):
            at = slice(i * n, (i + 1) * n)
            x_s[at, :] = rows[:, :D]
            xt_out[:, at] = rows[:, :D].T
            gate = rows[:, D : D + 1].astype(F32) + rows[:, D + 1 : D + 2].astype(F32)
            dr = (gate * g[...].astype(F32)).astype(BF)
            dr_s[at, :] = dr
            drt_out[:, at] = dr.T

    for k in range(F):
        at = pl.ds(pl.multiple_of(lax.rem(meta[2] - k + F, F) * d_local, d_local), d_local)
        for i in range(3):
            w_s[i, at, :] = ws[k][i]
    piece = n // 2
    for r in range(4):
        rows = slice(r * piece, (r + 1) * piece)
        gate_act = mm(x_s[rows, :], w_s[0])
        up_act = mm(x_s[rows, :], w_s[1])
        inner_grad = mm(dr_s[rows, :], w_s[2])
        sig = 0.5 * jnp.tanh(0.5 * gate_act) + 0.5
        act = gate_act * sig
        inner_out[rows, :] = (act * up_act).astype(BF)
        gate_out[rows, :] = (inner_grad * up_act * (sig + act * (1.0 - sig))).astype(BF)
        up_out[rows, :] = (inner_grad * act).astype(BF)
    if own:
        result = mm_nt(inner_out[...], w_s[2])
        packed = mm_nt(gate_out[...], w_s[0]) + mm_nt(up_out[...], w_s[1])

        @pl.when(step == 0)
        def _():
            acc[0] = result
            acc[1] = packed

        @pl.when(step > 0)
        def _():
            acc[0] += result
            acc[1] += packed

        @pl.when(step == pl.num_programs(0) - 1)
        def _():
            mine_out[...] = acc[:, :n, :]
            theirs_out[...] = acc[:, n:, :].astype(BF)


def weight_kernel(dims, meta, *refs):
    F, D, Z = dims
    planes, refs = [refs[5 * p : 5 * p + 5] for p in range(Z)], refs[5 * Z :]
    outs, (acc,) = refs[:F], refs[F:]
    d_local = D // F
    for i, (left, right) in enumerate(((3, 1), (3, 2), (4, 0))):
        total = mm(planes[0][left][...], planes[0][right][...])
        for p in range(1, Z):
            total = total + mm(planes[p][left][...], planes[p][right][...])
        acc[i] = total.astype(BF)
    for k in range(F):
        at = pl.ds(pl.multiple_of(lax.rem(meta[2] + k, F) * d_local, d_local), d_local)
        for i in range(3):
            outs[k][i] = acc[i, at, :]


def combine_kernel(dims, meta, hidden, grad, small, prev, routes, slots, *refs):
    Z, F, S, R, D, G, hw, per, _ = dims
    rets, refs = refs[:F], refs[F:]
    atts, refs = refs[: 2 * Z], refs[2 * Z :]
    w_full, refs = refs[0], refs[1:]
    out_block, dh_out, prev_out, refs = refs[0], refs[1], refs[2], refs[3:]
    das, refs = refs[:Z], refs[Z:]
    payloads, refs = refs[:F], refs[F:]
    back_s, gw_s, dproj_s, rows_s = refs

    def att(k, side):
        return atts[k][0] if side == 0 else atts[Z + k][...]

    f = meta[2]
    d_local = D // F
    for k in range(F):
        back_s[lax.rem(f + k, F)] = rets[k][...]
    gain = small[1:2, :]
    small_all = small[...]
    small_low = small_all.astype(BF)
    small_grads = jnp.zeros((16, D), F32)
    gain_grad = jnp.zeros((1, D), F32)
    for s in range(S):
        at = slice(s * R, (s + 1) * R)
        tile = hidden[at, :]
        factor = norm_of(tile)
        normal = tile * factor
        unit = normal * gain
        unit_low = unit.astype(BF)
        logits = mm_nt(unit_low, small_low)
        before, route = columns_of(prev, routes, s)
        lane, router, hots, gates = router_parts(logits, before, route)
        g_low = grad[s]
        g = g_low.astype(F32)

        def column(t, index):
            return jnp.sum(jnp.where(lane == index, t, 0.0), axis=-1, keepdims=True)

        shares = []
        for i in range(NC):
            a, b = column(logits, 10 + 2 * i), column(logits, 11 + 2 * i)
            top = jnp.maximum(a, b)
            ea, eb = jnp.exp(a - top), jnp.exp(b - top)
            shares.append((ea / (ea + eb), eb / (ea + eb)))
        back = []
        for part in range(2):
            experts = []
            for e in range(NF):
                to = slice(s * MOST, (s + 1) * MOST)
                total = back_s[e * per, part, to, :]
                for j in range(1, per):
                    total = total.astype(F32) + back_s[e * per + j, part, to, :].astype(F32)
                experts.append(total.astype(BF))
            back.append(jnp.concatenate(experts, axis=0))
        slot = lax.broadcasted_iota(jnp.int32, (NF * MOST, R), 0)
        picks = [
            (slot == slots[2 * s + w : 2 * s + w + 1, :]).astype(F32).astype(BF)
            for w in range(TOP)
        ]
        values = [mm_tn(picks[w], back[0]) for w in range(TOP)]
        unit_grad = mm_tn(picks[0] + picks[1], back[1])
        ug = jnp.sum(unit * g, axis=-1, keepdims=True)
        vg_all = mm_nt(g_low, small_low)
        vg = [column(vg_all, 14 + i) for i in range(NC)]

        def named(w, e):
            return (route[:, w : w + 1] == e).astype(F32)

        gate_grads = []
        coef_unit = jnp.zeros((R, 1), F32)
        for w in range(TOP):
            total = jnp.sum(g * values[w], axis=-1, keepdims=True) + named(w, NF + 1) * ug
            coef_unit = coef_unit + gates[w] * named(w, NF + 1)
            for i in range(NC):
                here = named(w, NF + 2 + i)
                total = total + here * (shares[i][0] * ug + shares[i][1] * vg[i])
                coef_unit = coef_unit + gates[w] * here * shares[i][0]
            gate_grads.append(total)
        mixture = gates[0] * values[0] + gates[1] * values[1] + coef_unit * unit
        prob_grad = sum(jnp.where(hots[w], gate_grads[w], 0.0) for w in range(TOP))
        prev_grad = router * (prob_grad - jnp.sum(router * prob_grad, axis=-1, keepdims=True))
        prev_out[s] = prev_grad.T[2 : 2 + NE, :]
        left = prev_grad
        right = jnp.zeros_like(prev_grad)
        for i in range(NC):
            amount = sum(gates[w] * named(w, NF + 2 + i) for w in range(TOP))
            s0, s1 = shares[i]
            mixture = mixture + amount * s1 * small_all[14 + i : 15 + i, :]
            d0, d1 = amount * ug, amount * vg[i]
            inner = s0 * d0 + s1 * d1
            left = left + jnp.where(lane == 10 + 2 * i, s0 * (d0 - inner), 0.0)
            left = left + jnp.where(lane == 11 + 2 * i, s1 * (d1 - inner), 0.0)
            right = right + jnp.where(lane == 14 + i, amount * s1, 0.0)
        out_block[s] = (tile + mixture).astype(BF)
        left_high, left_low = split(left)
        right_high, right_low = split(right)
        unit_grad = unit_grad + mm(left_high, small_low) + mm(left_low, small_low)
        unit_grad = unit_grad + coef_unit * g
        small_grads = small_grads + mm_tn(left_high, unit_low) + mm_tn(left_low, unit_low)
        small_grads = small_grads + mm_tn(right_high, g_low) + mm_tn(right_low, g_low)
        gain_grad = gain_grad + jnp.sum(unit_grad * normal, axis=0, keepdims=True)
        scaled = unit_grad * gain
        dh = g + factor * (scaled - normal * jnp.mean(scaled * normal, axis=-1, keepdims=True))
        dh_out[at, :] = dh
        dproj_s[at, :] = dh.astype(BF)
    row = lax.broadcasted_iota(jnp.int32, (16, D), 0)
    small_grads = jnp.where(row == 1, gain_grad, small_grads).astype(BF)
    for i in range(F):
        rows_s[i] = small_grads[:, i * d_local : (i + 1) * d_local]
    gw_s[...] = jnp.zeros_like(gw_s)
    for k in range(Z):
        for side in range(2):
            seq, group = piece_at((Z, G), meta, k, side)
            dproj = dproj_s[pl.ds(pl.multiple_of(seq * R, R), R), :]
            heads = pl.ds(pl.multiple_of(group * hw, hw), hw)
            das[k][side] = mm_nt(dproj, w_full[heads, :]).astype(BF)
            gw_s[heads, :] += mm_tn(att(k, side), dproj)
    for k in range(F):
        ff = lax.rem(f + k, F)
        at = pl.ds(pl.multiple_of(ff * d_local, d_local), d_local)
        payloads[k][:d_local, :] = gw_s[at, :].astype(BF)
        payloads[k][d_local:, :d_local] = rows_s[ff]
        payloads[k][d_local:, d_local:] = jnp.zeros((16, D - d_local), BF)


def back_kernel(dims, meta, start, cos, sin, small, *refs):
    Z, F, R, D, L, hpd, block = dims
    hw = hpd * HD
    xs, refs = refs[: 2 * Z], refs[2 * Z :]
    dos, refs = refs[: 2 * Z], refs[2 * Z :]
    (normed, weight, q_in, k_in, v_in, o_in, lse_in), refs = refs[:7], refs[7:]
    payloads, refs = refs[:F], refs[F:]
    (mine_out, theirs_out), refs = refs[:2], refs[2:]
    do_s, dq_s, dk_s, dv_s, mixed_s, gw_s, rows_s = refs
    z, core, f = meta[0], meta[1], meta[2]
    d_local = D // F
    for k in range(Z):
        for side in range(2):
            at = lax.rem(z + k, Z) * 2 + (core if side == 0 else 1 - core)
            row = pl.multiple_of(at * R, R)
            tile = dos[k][0] if side == 0 else dos[Z + k][...]
            for h in range(hpd):
                do_s[h, pl.ds(row, R), :] = tile[:, h * HD : (h + 1) * HD]
    dk_s[...] = jnp.zeros_like(dk_s)
    dv_s[...] = jnp.zeros_like(dv_s)

    def query_step(qb, carry):
        rows = pl.ds(pl.multiple_of(qb * block, block), block)
        first = start[rows, :]
        q_pos = qb * block + lax.broadcasted_iota(jnp.int32, (block, block), 0)
        column = lax.broadcasted_iota(jnp.int32, (block, block), 1)
        queries = [q_in[h, rows, :] for h in range(hpd)]
        upstream = [do_s[h, rows, :] for h in range(hpd)]
        lses = [lse_in[h, rows, :] for h in range(hpd)]
        deltas = [
            jnp.sum(upstream[h].astype(F32) * o_in[h, rows, :], axis=-1, keepdims=True)
            for h in range(hpd)
        ]

        def key_step(kb, state):
            keys = pl.ds(pl.multiple_of(kb * block, block), block)
            k_pos = kb * block + column
            allowed = (k_pos <= q_pos) & (k_pos >= first)
            new = []
            for h in range(hpd):
                key, value = k_in[h, keys, :], v_in[h, keys, :]
                scores = mm_nt(queries[h], key)
                weights = jnp.where(allowed, jnp.exp(scores - lses[h]), 0.0)
                dp = mm_nt(upstream[h], value)
                ds = (weights * (dp - deltas[h])).astype(BF)
                dv_s[h, keys, :] += mm_tn(weights.astype(BF), upstream[h])
                dk_s[h, keys, :] += mm_tn(ds, queries[h])
                new.append(state[h] + mm(ds, key))
            return tuple(new)

        begin = tuple(jnp.zeros((block, HD), F32) for _ in range(hpd))
        state = lax.fori_loop(meta[4 + qb], qb + 1, key_step, begin)
        for h in range(hpd):
            dq_s[h, rows, :] = state[h]
        return carry

    lax.fori_loop(0, L // block, query_step, 0)

    def unrotate(step, carry):
        rows = pl.ds(pl.multiple_of(step * block, block), block)
        cosine, sine = cos[rows, :], sin[rows, :]
        parts = [[], [], []]
        for h in range(hpd):
            dq = dq_s[h, rows, :] * HD ** (-0.5)
            dk = dk_s[h, rows, :]
            parts[0].append((dq * cosine - halves_swapped(dq) * sine).astype(BF))
            parts[1].append((dk * cosine - halves_swapped(dk) * sine).astype(BF))
            parts[2].append(dv_s[h, rows, :].astype(BF))
        mixed_s[rows, :] = jnp.concatenate(parts[0] + parts[1] + parts[2], axis=-1)
        return carry

    lax.fori_loop(0, L // block, unrotate, 0)
    gw_s[...] = mm_tn(normed[...], mixed_s[...]).astype(BF)
    total = jnp.zeros((1, D), F32)
    for k in range(Z):
        for side in range(2):
            chip = lax.rem(z - k + Z, Z)
            at = chip * 2 + (core if side == 0 else 1 - core)
            tile = xs[side * Z + k][...].astype(F32)
            row = pl.multiple_of(at * R, R)
            dn = mm_nt(mixed_s[pl.ds(row, R), :], weight[...])
            total = total + jnp.sum(dn * (tile * norm_of(tile)), axis=0, keepdims=True)
            if side == 0:
                mine_out[chip] = dn.astype(BF)
            else:
                theirs_out[chip] = dn.astype(BF)
    total = jnp.broadcast_to(total, (16, D)).astype(BF)
    for i in range(F):
        rows_s[i] = total[:, i * d_local : (i + 1) * d_local]
    for k in range(F):
        ff = lax.rem(f + k, F)
        at = pl.ds(pl.multiple_of(ff * d_local, d_local), d_local)
        payloads[k][:d_local, :] = gw_s[at, :]
        payloads[k][d_local:, :d_local] = rows_s[ff]
        if d_local < 3 * hw:
            payloads[k][d_local:, d_local:] = jnp.zeros((16, 3 * hw - d_local), BF)


def pair_kernel(Z, meta, mine, theirs, *outs):
    for k in range(Z):
        chip = lax.rem(meta[0] + k, Z)
        outs[k][...] = (mine[chip].astype(F32) + theirs[chip].astype(F32)).astype(BF)


def last_kernel(dims, meta, x, dh, small, *refs):
    Z, S, R, _, G = dims
    dns, out, acc = refs[:Z], refs[Z], refs[Z + 1]
    acc[...] = jnp.zeros_like(acc)
    for k in range(Z):
        seq, _ = piece_at((Z, G), meta, k, 0)
        acc[seq] += dns[k][...].astype(F32)
    gain = small[0:1, :]
    for s in range(S):
        tile = x[s].astype(F32)
        factor = norm_of(tile)
        normal = tile * factor
        scaled = acc[s] * gain
        out[s] = dh[s * R : (s + 1) * R, :] + factor * (
            scaled - normal * jnp.mean(scaled * normal, axis=-1, keepdims=True)
        )


def place_kernel(dims, ks, part, meta, *refs):
    F, per, CW, width = dims
    n = len(ks)
    ours, theirs, refs = refs[:n], refs[n : 2 * n], refs[2 * n :]
    outs, (buf, sems) = refs[-5:-2], refs[-2:]
    copies = []
    for side in range(2):
        for j, k in enumerate(ks):
            dev = lax.rem(meta[2] - k + F, F)
            core = meta[1] if side == 0 else 1 - meta[1]
            e = lax.div(dev, per)
            lane = (lax.rem(dev, per) * 2 + core) * CW + part * width
            lanes = pl.ds(pl.multiple_of(lane, 128), width)
            for i in range(3):
                at = (side * n + j) * 3 + i
                buf[at] = (ours if side == 0 else theirs)[j][i].astype(F32)
                copy = pltpu.make_async_copy(buf.at[at], outs[i].at[:, e, lanes], sems.at[at])
                copy.start()
                copies.append(copy)
    for copy in copies:
        copy.wait()


def qkv_grad_kernel(dims, meta, *refs):
    G, D, d_local, hw = dims
    pieces, (out, gain_out, table) = refs[:-3], refs[-3:]
    group = lax.rem(meta[3], G)
    at = 0
    for piece in pieces:
        for j in range(piece.shape[0]):
            table[at] = piece[j]
            at += 1
    gain = jnp.zeros((1, d_local), F32)
    for i in range(G):
        tile = table[jnp.bitwise_xor(group, i)].astype(F32)
        gain = gain + tile[d_local : d_local + 1, :d_local]
        width = max(0, min(hw, D - i * hw))
        if width:
            for part in range(3):
                out[:, part * D + i * hw : part * D + i * hw + width] = tile[
                    :d_local, part * hw : part * hw + width
                ]
    gain_out[...] = gain


def body(
    block_input,
    attn_gain,
    w_qkv,
    w_out,
    ffn_gain,
    w_router,
    w_gate,
    w_up,
    w_down,
    const_mix,
    const_vec,
    prev_logits,
    routes,
    doc_ids,
    d_out,
    *,
    F,
    C,
):
    S, R, D = block_input.shape
    L = doc_ids.shape[1]
    Z = C // 2
    G = C // S
    hpd = -(-H // G)
    hw = hpd * HD
    FF = w_gate.shape[2]
    per = F // NF
    CW = FF // (2 * per)
    d_local = D // F
    T = S * R
    block = min(256, L)
    shaped = jax.ShapeDtypeStruct
    f = lax.axis_index("fsdp")
    c = lax.axis_index("ctx")
    core = c % 2
    z = c // 2

    def fs(t, k):
        return lax.ppermute(t, "fsdp", [(i, (i + k) % F) for i in range(F)])

    def zs(t, k):
        return lax.ppermute(
            t, "ctx", [(2 * i + j, 2 * ((i + k) % Z) + j) for i in range(Z) for j in range(2)]
        )

    def cx(t):
        return lax.ppermute(t, "ctx", [(i, i ^ 1) for i in range(C)])

    def pick(t, index, axis=0):
        return lax.dynamic_index_in_dim(t, index, axis, keepdims=False)

    def seq_of(chip):
        return chip // (Z // S)

    def expert_of(dev):
        return lax.div(dev, per)

    def chunk_of(dev):
        return (dev % per) * 2 + core

    def call(kernel, name, out_shape, args, scratch=(), smem=1, **kw):
        return pl.pallas_call(
            kernel,
            out_shape=out_shape,
            in_specs=[SMEM] * smem + [VMEM] * (len(args) - smem),
            out_specs=tuple([VMEM] * len(out_shape)),
            scratch_shapes=list(scratch),
            compiler_params=params(name, L > 2048),
            **kw,
        )(*args)

    x_mine = [pick(block_input, seq_of(z))] + [
        zs(pick(block_input, seq_of((z + k) % Z)), k) for k in range(1, Z)
    ]
    x_theirs = [cx(t) for t in x_mine]

    my_docs = pick(doc_ids, c // G)
    start = jnp.sum((my_docs[None, :] < my_docs[:, None]).astype(jnp.int32), axis=1)
    first_block = start.reshape(L // block, block)[:, 0] // block
    meta = jnp.concatenate([jnp.stack([z, core, f, c]).astype(jnp.int32), first_block])
    route_rows = routes.transpose(0, 2, 1).reshape(S * TOP, R)
    prev = prev_logits.transpose(0, 2, 1)

    (first,) = call(
        functools.partial(pack_kernel, (F, D, G, hpd)),
        "pack",
        (shaped((d_local + 16, 3 * hw), BF),),
        (
            meta,
            w_qkv,
            attn_gain[None],
            ffn_gain[None],
            w_router.T,
            const_mix.T,
            const_vec.T,
        ),
    )
    w_pieces = [first] + [fs(first, k) for k in range(1, F)]
    slot_rows, *g_outs = call(
        functools.partial(grad_rows_kernel, (F, S, R, D, expert_of)),
        "grad_rows",
        (shaped((S * TOP, R), jnp.int32),) + (shaped((S * MOST, D), BF),) * F,
        (meta, d_out, route_rows),
        [pltpu.VMEM((NF, S * MOST, D), BF)],
    )
    g_mine = jnp.concatenate([g_outs[0]] + [fs(g_outs[k], k) for k in range(1, F)], axis=0)
    o_pieces = [w_out] + [fs(w_out, k) for k in range(1, F)]

    def expert_slices():
        if per == 1:
            cut = [
                lax.dynamic_slice_in_dim(w, core * CW, CW, 2).transpose(1, 0, 2)
                for w in (w_gate, w_up, w_down)
            ]
            cut = lax.optimization_barrier(cut)
            return call(
                functools.partial(order_kernel, F),
                "order",
                (shaped((3, d_local, CW), BF),) * F,
                (meta, *cut),
            )
        out = []
        for k in range(F):
            dev = (f + k) % F
            out.append(
                jnp.stack(
                    [
                        pick(
                            lax.dynamic_slice_in_dim(w, chunk_of(dev) * CW, CW, 2),
                            expert_of(dev),
                            1,
                        )
                        for w in (w_gate, w_up, w_down)
                    ]
                )
            )
        return out

    slices = expert_slices()
    e_pieces = [slices[0]] + [fs(slices[k], k) for k in range(1, F)]

    frequency = jnp.exp(jnp.arange(HD // 2, dtype=F32) * (-2.0 * math.log(10000.0) / HD))
    angles = jnp.arange(L).astype(F32)[:, None] * frequency[None, :]
    cosine, sine = jnp.cos(angles), jnp.sin(angles)
    cosine = jnp.concatenate([cosine, cosine], axis=1)
    sine = jnp.concatenate([-sine, sine], axis=1)
    dims = (Z, F, R, D, L, hpd, block)
    normed, qkv_w, small, q, k_, v, o, lse, *att_pieces = call(
        functools.partial(attend_kernel, dims),
        "attend",
        (
            shaped((L, D), BF),
            shaped((D, 3 * hw), BF),
            shaped((16, D), F32),
            shaped((hpd, L, HD), BF),
            shaped((hpd, L, HD), BF),
            shaped((hpd, L, HD), BF),
            shaped((hpd, L, HD), F32),
            shaped((hpd, L, 1), F32),
        )
        + (shaped((2, R, hw), BF),) * Z,
        (meta, start[:, None], cosine, sine, *x_mine, *x_theirs, *w_pieces),
        [pltpu.VMEM((F, 16, d_local), F32), pltpu.VMEM((C, R, hw), BF)],
    )

    g_planes = [(g_mine, cx(g_mine))] + [zs(g_mine, k) for k in range(1, Z)]

    pieces = [att_pieces[0]] + [zs(att_pieces[k], k) for k in range(1, Z)]
    atts = pieces + [cx(t[1]) for t in pieces]
    outs = call(
        functools.partial(dispatch_kernel, (Z, F, S, R, D, G, hw, expert_of)),
        "dispatch",
        (shaped((T, D), F32), shaped((G * hw, D), BF))
        + (shaped((S * MOST, D + 128), BF),) * F,
        (meta, block_input, small, prev, route_rows, slot_rows, *atts, *o_pieces),
        [pltpu.VMEM((NF, S * MOST, D + 128), BF)],
    )
    hidden, out_w, toks = outs[0], outs[1], outs[2:]
    own = [toks[0]] + [fs(toks[k], k) for k in range(1, F)]
    own = jnp.concatenate(own, axis=0)
    n = own.shape[0]

    steps = 4 if CW % 512 == 0 else 2
    cut = CW // steps
    e_spec = pl.BlockSpec((3, d_local, cut), lambda i: (0, 0, i))
    act_spec = pl.BlockSpec((2 * n, cut), lambda i: (0, i))
    both_spec = pl.BlockSpec((D, 2 * n), lambda i: (0, 0))

    def ffn(at, rows, theirs, g_rows):
        own_plane = at == 0
        shapes = (shaped((2 * n, CW), BF),) * 3 + (shaped((D, 2 * n), BF),) * 2
        specs = (act_spec,) * 3 + (both_spec,) * 2
        scratch = [pltpu.VMEM((2 * n, D), BF), pltpu.VMEM((2 * n, D), BF)]
        scratch.append(pltpu.VMEM((3, D, cut), BF))
        if own_plane:
            shapes += (shaped((2, n, D), F32), shaped((2, n, D), BF))
            specs += (pl.BlockSpec((2, n, D), lambda i: (0, 0, 0)),) * 2
            scratch.append(pltpu.VMEM((2, 2 * n, D), F32))
        row_spec = pl.BlockSpec((n, D + 128), lambda i: (0, 0))
        g_spec = pl.BlockSpec((n, D), lambda i: (0, 0))
        return pl.pallas_call(
            functools.partial(ffn_kernel, (F, D), own_plane),
            out_shape=shapes,
            grid=(steps,),
            in_specs=[SMEM, row_spec, row_spec, g_spec, g_spec] + [e_spec] * F,
            out_specs=specs,
            scratch_shapes=scratch,
            compiler_params=params("experts" if at else "experts0", L > 2048),
        )(meta, rows, theirs, *g_rows, *e_pieces)

    *plane, back_mine, back_theirs = ffn(0, own, cx(own), g_planes[0])
    planes = [plane]
    back = (back_mine + cx(back_theirs).astype(F32)).astype(BF).reshape(2, F, S * MOST, D)
    rets = [back[:, 0]] + [fs(back[:, k], -k) for k in range(1, F)]
    ring = [own]
    for _ in range(1, Z):
        ring.append(zs(ring[-1], 1))

    def far(k, after):
        rows, g_rows, _ = lax.optimization_barrier((ring[k], g_planes[k], after))
        planes.append(ffn(k, rows, cx(rows), (g_rows, cx(g_rows))))

    far(1, back_mine)
    outs = call(
        functools.partial(combine_kernel, (Z, F, S, R, D, G, hw, per, expert_of)),
        "combine",
        (shaped((S, R, D), BF), shaped((T, D), F32), shaped((S, NE, R), F32))
        + (shaped((2, R, hw), BF),) * Z
        + (shaped((d_local + 16, D), BF),) * F,
        (meta, hidden, d_out, small, prev, route_rows, slot_rows, *rets, *atts, out_w),
        [
            pltpu.VMEM((F, 2, S * MOST, D), BF),
            pltpu.VMEM((G * hw, D), F32),
            pltpu.VMEM((T, D), BF),
            pltpu.VMEM((F, 16, d_local), BF),
        ],
    )
    out_block, hidden_grad, prev_grad = outs[:3]
    das, o_payloads = outs[3 : 3 + Z], outs[3 + Z :]
    grad_prev = prev_grad.transpose(0, 2, 1)

    do_pieces = [das[0]] + [zs(das[k], -k) for k in range(1, Z)]
    dos = do_pieces + [cx(t[1]) for t in do_pieces]

    for k in range(2, Z):
        far(k, hidden_grad)
    parts = 2
    width = CW // parts
    wide = min(256, width)
    flat = [t for plane in planes for t in plane]
    e_grads = []
    for part in range(parts):
        first_block_at = part * (width // wide)
        if Z > 4:
            lanes = slice(part * width, (part + 1) * width)
            trio = [
                sum(mm(plane[left], plane[right][:, lanes]) for plane in planes).astype(BF)
                for left, right in ((3, 1), (3, 2), (4, 0))
            ]
            trio = jnp.stack(trio).reshape(3, F, d_local, width)
            e_grads.append([pick(trio, (f + k) % F, 1) for k in range(F)])
            continue
        acts = pl.BlockSpec((2 * n, wide), lambda i, b=first_block_at: (0, b + i))
        e_grads.append(
            pl.pallas_call(
                functools.partial(weight_kernel, (F, D, Z)),
                out_shape=(shaped((3, d_local, width), BF),) * F,
                grid=(width // wide,),
                in_specs=[SMEM] + [acts, acts, acts, both_spec, both_spec] * Z,
                out_specs=(pl.BlockSpec((3, d_local, wide), lambda i: (0, 0, i)),) * F,
                scratch_shapes=[pltpu.VMEM((3, D, wide), BF)],
                compiler_params=params("expert_grads", L > 2048),
            )(meta, *flat)
        )
    dos[0], *_ = lax.optimization_barrier((dos[0], e_grads[-1][0]))
    outs = call(
        functools.partial(back_kernel, dims),
        "attend_back",
        (shaped((d_local + 16, 3 * hw), BF),) * F + (shaped((Z, R, D), BF),) * 2,
        (
            meta,
            start[:, None],
            cosine,
            sine,
            small,
            *x_mine,
            *x_theirs,
            *dos,
            normed,
            qkv_w,
            q,
            k_,
            v,
            o,
            lse,
        ),
        [
            pltpu.VMEM((hpd, L, HD), BF),
            pltpu.VMEM((hpd, L, HD), F32),
            pltpu.VMEM((hpd, L, HD), F32),
            pltpu.VMEM((hpd, L, HD), F32),
            pltpu.VMEM((L, 3 * hw), BF),
            pltpu.VMEM((D, 3 * hw), BF),
            pltpu.VMEM((F, 16, d_local), BF),
        ],
    )
    q_payloads, dn_mine, dn_theirs = outs[:F], outs[F], outs[F + 1]
    dns = call(
        functools.partial(pair_kernel, Z),
        "pair",
        (shaped((R, D), BF),) * Z,
        (meta, dn_mine, cx(dn_theirs)),
    )
    paired = dns[0]
    dns = [dns[0]] + [zs(dns[k], k) for k in range(1, Z)]
    (grad_x,) = call(
        functools.partial(last_kernel, (Z, S, R, D, G)),
        "input_grad",
        (shaped((S, R, D), F32),),
        (meta, block_input, hidden_grad, small, *dns),
        [pltpu.VMEM((S, R, D), F32)],
    )

    def moved_rows(parts):
        return [parts[0]] + [fs(parts[k], k) for k in range(1, F)]

    def summed_rows(parts):
        return sum(p.astype(F32) for p in parts).astype(BF)

    def over_ctx(t):
        step = 1
        while step < C:
            moved = lax.ppermute(t, "ctx", [(i, i ^ step) for i in range(C)])
            t = (t.astype(F32) + moved.astype(F32)).astype(BF)
            step *= 2
        return t

    payload = summed_rows(moved_rows(q_payloads))
    summed = payload.astype(F32)
    for j in range(1, S):
        moved = lax.ppermute(payload, "ctx", [(i, (i + j * G) % C) for i in range(C)])
        summed = summed + moved.astype(F32)
    payload = summed.astype(BF)[None]
    gathered = [payload]
    step = 1
    while step < G:
        gathered.append(lax.ppermute(payload, "ctx", [(i, i ^ step) for i in range(C)]))
        step *= 2
        if step < G:
            payload = jnp.concatenate([payload, gathered[-1]], axis=0)
    grad_qkv, grad_gain_one = call(
        functools.partial(qkv_grad_kernel, (G, D, d_local, hw)),
        "qkv_grad",
        (shaped((d_local, 3 * D), F32), shaped((1, d_local), F32)),
        (meta, *gathered),
        [pltpu.VMEM((G, d_local + 16, 3 * hw), BF)],
    )
    grad_gain_one = grad_gain_one[0]

    moved = moved_rows(o_payloads)
    moved, _ = lax.optimization_barrier((moved, paired))
    payload = over_ctx(summed_rows(moved)).astype(F32)
    grad_w_out = payload[:d_local]
    smalls = payload[d_local:, :d_local]

    ANY = pl.BlockSpec(memory_space=pl.ANY)
    placed = ()
    for part in range(parts):
        ours = [e_grads[part][0]] + [fs(e_grads[part][k], k) for k in range(1, F)]
        theirs = [cx(t) for t in ours]
        groups = [list(range(F))] if part < parts - 1 else [list(range(F - 1)), [F - 1]]
        for ks in groups:
            args = (meta, *[ours[k] for k in ks], *[theirs[k] for k in ks], *placed)
            at = 1 + 2 * len(ks)
            placed = pl.pallas_call(
                functools.partial(place_kernel, (F, per, CW, width), ks, part),
                out_shape=(shaped((d_local, NF, FF), F32),) * 3,
                in_specs=[SMEM] + [VMEM] * (2 * len(ks)) + [ANY] * len(placed),
                out_specs=(ANY,) * 3,
                input_output_aliases={at + i: i for i in range(len(placed))},
                scratch_shapes=[
                    pltpu.VMEM((6 * len(ks), d_local, width), F32),
                    pltpu.SemaphoreType.DMA((6 * len(ks),)),
                ],
                compiler_params=params("place", L > 2048),
            )(*args)
    grad_gate, grad_up, grad_down = placed
    return (
        out_block,
        grad_x,
        grad_prev,
        grad_gain_one,
        grad_qkv,
        grad_w_out,
        smalls[1],
        smalls[2:10].T,
        grad_gate,
        grad_up,
        grad_down,
        smalls[10:14].T,
        smalls[14:16].T,
    )


def solution(mesh):
    F, Z = mesh.shape["fsdp"], mesh.shape["ctx"] // 2

    def layer(*args):
        return body(*args, F=F, C=2 * Z)

    return jax.shard_map(
        layer,
        mesh=mesh,
        in_specs=(
            P("fsdp", "ctx", None),
            P("fsdp"),
            P("fsdp", None),
            P("fsdp", None),
            P("fsdp"),
            P("fsdp", None),
            P("fsdp", None, None),
            P("fsdp", None, None),
            P("fsdp", None, None),
            P("fsdp", None),
            P("fsdp", None),
            P("fsdp", "ctx", None),
            P("fsdp", "ctx", None),
            P("fsdp", None),
            P("fsdp", "ctx", None),
        ),
        out_specs=(
            P("fsdp", "ctx", None),
            P("fsdp", "ctx", None),
            P("fsdp", "ctx", None),
            P("fsdp"),
            P("fsdp", None),
            P("fsdp", None),
            P("fsdp"),
            P("fsdp", None),
            P("fsdp", None, None),
            P("fsdp", None, None),
            P("fsdp", None, None),
            P("fsdp", None),
            P("fsdp", None),
        ),
        check_vma=False,
    )
```

```python
import functools
import math

import jax
import jax.numpy as jnp
from jax import lax
from jax.experimental import pallas as pl
from jax.experimental.pallas import tpu as pltpu
from jax.sharding import PartitionSpec as P


H = 12
HD = 64
NF = 4
NC = 2
NE = 8
TOP = 2
MOST = 48
BF = jnp.bfloat16
F32 = jnp.float32


def dot(a, b, dims):
    return lax.dot_general(a, b, (dims, ((), ())), preferred_element_type=F32)


def mm(a, b):
    return dot(a, b, ((1,), (0,)))


def mm_nt(a, b):
    return dot(a, b, ((1,), (1,)))


def mm_tn(a, b):
    return dot(a, b, ((0,), (0,)))


def halves_swapped(t):
    half = t.shape[-1] // 2
    return jnp.concatenate([t[:, half:], t[:, :half]], axis=-1)


VMEM = pl.BlockSpec(memory_space=pltpu.VMEM)
SMEM = pl.BlockSpec(memory_space=pltpu.SMEM)


GRANTS = {
    "pack": 4,
    "stack": 2,
    "order": 4,
    "attend": 10,
    "dispatch": 4,
    "experts0": 20,
    "experts": 11,
    "combine": 12,
    "expert_grads": 14,
    "attend_back": 16,
    "normed_grad": 3,
    "pair": 2,
    "input_grad": 4,
    "place": 18,
    "qkv_grad": 4,
}


def params(name, long=False):
    return pltpu.CompilerParams(vmem_limit_bytes=(56 if long else GRANTS[name]) << 20)


def place_of():
    c = lax.axis_index("ctx")
    return lax.div(c, 2), lax.rem(c, 2), lax.axis_index("fsdp"), c


def norm_of(tile):
    return lax.rsqrt(jnp.mean(tile * tile, axis=-1, keepdims=True) + 1e-05)


def split(t):
    high = t.astype(BF)
    return high, (t - high.astype(F32)).astype(BF)


def pack_kernel(dims, grad, routes, w_qkv, gains, router, mix, vec, slots, *outs):
    F, S, R, D, G, hpd, expert_of = dims
    hw = hpd * HD
    _, _, f, c = place_of()
    d_local = D // F
    top = S * MOST
    outs, table = outs[:F], outs[F]
    group = lax.rem(c, G)
    own = outs[0]
    for g in range(G):
        width = max(0, min(hw, H * HD - g * hw))

        @pl.when(group == g)
        def _():
            for part in range(3):
                if width:
                    own[top : top + d_local, part * hw : part * hw + width] = w_qkv[
                        :, part * H * HD + g * hw : part * H * HD + g * hw + width
                    ]
                if width < hw:
                    own[top : top + d_local, part * hw + width : (part + 1) * hw] = jnp.zeros(
                        (d_local, hw - width), BF
                    )

    rows = [t[...].astype(F32) for t in (gains, router, mix, vec)]
    own[top + d_local :, :d_local] = jnp.concatenate(rows, axis=0).astype(BF)
    own[top + d_local :, d_local:] = jnp.zeros((16, D - d_local), BF)
    own[top : top + d_local, 3 * hw :] = jnp.zeros((d_local, D - 3 * hw), BF)
    for k in range(1, F):
        outs[k][top:, :] = own[top:, :]
    below = lax.broadcasted_iota(jnp.int32, (R, R), 0)
    earlier = (below < lax.broadcasted_iota(jnp.int32, (R, R), 1)).astype(F32).astype(BF)
    expert = lax.broadcasted_iota(jnp.int32, (8, R), 0)
    for s in range(S):
        named = [routes[2 * s + w : 2 * s + w + 1, :] for w in range(TOP)]
        hots = [(expert == t).astype(F32) for t in named]
        counts = mm((hots[0] + hots[1]).astype(BF), earlier)
        lines = []
        for w in range(TOP):
            rank = jnp.sum(hots[w] * counts, axis=0, keepdims=True).astype(jnp.int32)
            line = jnp.where(named[w] < NF, named[w] * MOST + rank, -1)
            slots[2 * s + w : 2 * s + w + 1, :] = line
            lines.append(line)
        slot = lax.broadcasted_iota(jnp.int32, (NF * MOST, R), 0)
        picks = (slot == lines[0]) | (slot == lines[1])
        moved = mm(picks.astype(F32).astype(BF), grad[s]).astype(BF)
        for e in range(NF):
            table[e, s * MOST : (s + 1) * MOST, :] = moved[e * MOST : (e + 1) * MOST, :]
    for k in range(F):
        outs[k][:top, :] = table[expert_of(lax.rem(f + k, F))]


def stack_kernel(n, *refs):
    out = refs[-1]
    for i, ref in enumerate(refs[:-1]):
        out[i * n : (i + 1) * n, :] = ref[:n, :]


def order_kernel(dims, *refs):
    meta = place_of()
    F = dims
    for k in range(F):
        e = lax.rem(meta[2] + k, F)
        for i in range(3):
            refs[3 + k][i] = refs[i][e]


def turn_tables(cos_low, sin_low, cos_high, sin_high, cosine, sine, L):
    low = cos_low.shape[0]
    for step in range(L // low):
        a, b = cos_high[step : step + 1, :], sin_high[step : step + 1, :]
        at = slice(step * low, (step + 1) * low)
        cosine[at, :] = a * cos_low[...] - b * sin_low[...]
        sine[at, :] = b * cos_low[...] + a * sin_low[...]


def signed(sine):
    lane = lax.broadcasted_iota(jnp.int32, sine.shape, 1)
    return jnp.where(lane < HD // 2, -sine, sine)


def attend_kernel(dims, blocks, start, cos_low, sin_low, cos_high, sin_high, *refs):
    Z, F, R, D, L, hpd, block = dims
    hw = hpd * HD
    xs, refs = refs[: 2 * Z], refs[2 * Z :]
    ws, refs = refs[:F], refs[F:]
    normed, weight, small_out, cos, sin, q_out, k_out, v_out, kt_out, ot_out, lse_out = refs[:11]
    refs = refs[11:]
    pieces, (small_s, vt_s, att_s) = refs[:Z], refs[Z:]
    z, core, f, _ = place_of()
    d_local = D // F
    top = ws[0].shape[0] - d_local - 16
    turn_tables(cos_low, sin_low, cos_high, sin_high, cos, sin, L)
    for k in range(F):
        row = pl.multiple_of(lax.rem(f - k + F, F) * d_local, d_local)
        weight[pl.ds(row, d_local), :] = ws[k][top : top + d_local, : 3 * hw]
        small_s[k] = ws[k][top + d_local :, :d_local].astype(F32)
    small = jnp.concatenate([small_s[lax.rem(f - i + F, F)] for i in range(F)], axis=1)
    small_out[...] = small
    gain_row = small[0:1, :]
    for k in range(Z):
        for side in range(2):
            at = lax.rem(z - k + Z, Z) * 2 + (core if side == 0 else 1 - core)
            tile = xs[side * Z + k][...].astype(F32)
            row = pl.multiple_of(at * R, R)
            normed[pl.ds(row, R), :] = (tile * norm_of(tile) * gain_row).astype(BF)

    def project(step, carry):
        rows = pl.ds(pl.multiple_of(step * block, block), block)
        mixed = mm(normed[rows, :], weight[...])
        cosine, sine = cos[rows, :], signed(sin[rows, :])
        for h in range(hpd):
            q = mixed[:, h * HD : (h + 1) * HD]
            k = mixed[:, hw + h * HD : hw + (h + 1) * HD]
            v = mixed[:, 2 * hw + h * HD : 2 * hw + (h + 1) * HD]
            q = (q * cosine + halves_swapped(q) * sine).astype(BF)
            q_out[h, rows, :] = (q.astype(F32) * HD ** (-0.5)).astype(BF)
            k = k * cosine + halves_swapped(k) * sine
            k_out[h, rows, :] = k.astype(BF)
            kt_out[h, :, rows] = k.T.astype(BF)
            v_out[h, rows, :] = v.astype(BF)
            vt_s[h, :, rows] = v.T.astype(BF)
        return carry

    lax.fori_loop(0, L // block, project, 0)

    def query_step(qb, carry):
        rows = pl.ds(pl.multiple_of(qb * block, block), block)
        first = start[:, rows]
        q_pos = qb * block + lax.broadcasted_iota(jnp.int32, (block, block), 1)
        down = lax.broadcasted_iota(jnp.int32, (block, block), 0)
        queries = [q_out[h, rows, :] for h in range(hpd)]

        def key_step(kb, state):
            keys = pl.ds(pl.multiple_of(kb * block, block), block)
            k_pos = kb * block + down
            allowed = (k_pos <= q_pos) & (k_pos >= first)
            new = []
            for h in range(hpd):
                high, total, acc = state[h]
                scores = mm_nt(k_out[h, keys, :], queries[h])
                scores = jnp.where(allowed, scores, -1e30)
                top = jnp.maximum(high, jnp.max(scores, axis=0, keepdims=True))
                scale = jnp.exp(high - top)
                weights = jnp.where(allowed, jnp.exp(scores - top), 0.0)
                total = total * scale + jnp.sum(weights, axis=0, keepdims=True)
                acc = acc * scale + mm(vt_s[h, :, keys], weights.astype(BF))
                new.append((top, total, acc))
            return tuple(new)

        begin = tuple(
            (
                jnp.full((1, block), -1e30, F32),
                jnp.zeros((1, block), F32),
                jnp.zeros((HD, block), F32),
            )
            for _ in range(hpd)
        )
        state = lax.fori_loop(blocks[qb], qb + 1, key_step, begin)
        outs = []
        for h in range(hpd):
            high, total, acc = state[h]
            out = acc / total
            ot_out[h, :, rows] = out
            lse_out[h, :, rows] = high + jnp.log(total)
            outs.append(out)
        whole = jnp.concatenate(outs, axis=0).T.astype(BF)
        for part in range(block // R):
            att_s[qb * (block // R) + part] = whole[part * R : (part + 1) * R, :]
        return carry

    lax.fori_loop(0, L // block, query_step, 0)
    for k in range(Z):
        chip = lax.rem(z + k, Z) * 2
        pieces[k][0] = att_s[chip + core]
        pieces[k][1] = att_s[chip + 1 - core]


def piece_at(dims, meta, k, side):
    Z, G = dims
    chip = lax.rem(meta[0] - k + Z, Z)
    group = lax.rem(2 * chip + (meta[1] if side == 0 else 1 - meta[1]), G)
    return lax.div(2 * chip, G), group


def columns_of(prev, routes, s):
    width = prev.shape[2]
    gap = jnp.zeros((2, width), F32)
    tall = jnp.concatenate([gap, prev[s], jnp.zeros((6, width), F32)], axis=0)
    named = routes[2 * s : 2 * s + 2, :].astype(F32)
    named = jnp.concatenate([named, jnp.zeros((6, width), F32)], axis=0)
    return tall.T, named.T.astype(jnp.int32)


def router_parts(logits, prev, routes):
    lane = lax.broadcasted_iota(jnp.int32, logits.shape, 1)
    inside = (lane >= 2) & (lane < 2 + NE)
    shown = jnp.where(inside, logits + prev, -1e30)
    weights = jnp.exp(shown - jnp.max(shown, axis=-1, keepdims=True))
    weights = jnp.where(inside, weights, 0.0)
    router = weights / jnp.sum(weights, axis=-1, keepdims=True)
    hots = [lane == routes[:, w : w + 1] + 2 for w in range(TOP)]
    gates = [jnp.sum(jnp.where(hot, router, 0.0), axis=-1, keepdims=True) for hot in hots]
    return lane, router, hots, gates


def dispatch_kernel(dims, x, small, prev, routes, slots, *refs):
    meta = place_of()
    Z, F, S, R, D, G, hw, expert_of = dims
    atts, refs = refs[: 2 * Z], refs[2 * Z :]
    ws, refs = refs[:F], refs[F:]
    hidden, w_full, toks, table = refs[0], refs[1], refs[2:-1], refs[-1]

    def att(k, side):
        return atts[k][0] if side == 0 else atts[Z + k][...]

    f = meta[2]
    d_local = D // F
    if G * hw > D:
        w_full[D:, :] = jnp.zeros((G * hw - D, D), BF)
    for k in range(F):
        row = pl.multiple_of(lax.rem(f - k + F, F) * d_local, d_local)
        w_full[pl.ds(row, d_local), :] = ws[k][...]
    for s in range(S):
        hidden[s * R : (s + 1) * R, :] = x[s].astype(F32)
    for k in range(Z):
        for side in range(2):
            seq, group = piece_at((Z, G), meta, k, side)
            rows = pl.ds(pl.multiple_of(seq * R, R), R)
            heads = pl.ds(pl.multiple_of(group * hw, hw), hw)
            hidden[rows, :] += mm(att(k, side), w_full[heads, :])
    gain = small[1:2, :]
    small_low = small[...].astype(BF)
    for s in range(S):
        at = slice(s * R, (s + 1) * R)
        tile = hidden[at, :]
        unit_low = (tile * norm_of(tile) * gain).astype(BF)
        logits = mm_nt(unit_low, small_low)
        _, _, _, gates = router_parts(logits, *columns_of(prev, routes, s))
        slot = lax.broadcasted_iota(jnp.int32, (NF * MOST, R), 0)
        picks = [
            (slot == slots[2 * s + w : 2 * s + w + 1, :]).astype(F32).astype(BF)
            for w in range(TOP)
        ]
        packed = mm(picks[0] + picks[1], unit_low).astype(BF)
        wide = lax.broadcasted_iota(jnp.int32, (R, 128), 1)
        columns = jnp.zeros((NF * MOST, 128), F32)
        for w in range(TOP):
            high, low = split(gates[w])
            both = jnp.where(
                wide == 0, high.astype(F32), jnp.where(wide == 1, low.astype(F32), 0.0)
            )
            columns = columns + mm(picks[w], both.astype(BF))
        for e in range(NF):
            to = slice(s * MOST, (s + 1) * MOST)
            table[e, to, :D] = packed[e * MOST : (e + 1) * MOST, :]
            table[e, to, D:] = columns[e * MOST : (e + 1) * MOST, :].astype(BF)
    for k in range(F):
        toks[k][...] = table[expert_of(lax.rem(f + k, F))]


def ffn_kernel(dims, own, rows_a, rows_b, g_a, g_b, *refs):
    meta = place_of()
    F, D = dims
    n = rows_a.shape[0]
    ws, refs = (refs[:F], refs[F:]) if own else ((), refs)
    if not own:
        w_s, refs = refs[0], refs[1:]
    (inner_out, gate_out, up_out, xt_out, drt_out), refs = refs[:5], refs[5:]
    if own:
        mine_out, theirs_out, w_s, x_s, dr_s, acc = refs
    else:
        x_s, dr_s = refs
    step = pl.program_id(0)
    d_local = D // F

    @pl.when(step == 0)
    def _():
        for i, (rows, g) in enumerate(((rows_a, g_a), (rows_b, g_b))):
            at = slice(i * n, (i + 1) * n)
            x_s[at, :] = rows[:, :D]
            xt_out[:, at] = rows[:, :D].T
            gate = rows[:, D : D + 1].astype(F32) + rows[:, D + 1 : D + 2].astype(F32)
            dr = (gate * g[...].astype(F32)).astype(BF)
            dr_s[at, :] = dr
            drt_out[:, at] = dr.T

    for k, piece in enumerate(ws):
        at = pl.ds(pl.multiple_of(lax.rem(meta[2] - k + F, F) * d_local, d_local), d_local)
        for i in range(3):
            w_s[i, at, :] = piece[i]
    piece = n // 2
    for r in range(4):
        rows = slice(r * piece, (r + 1) * piece)
        gate_act = mm(x_s[rows, :], w_s[0])
        up_act = mm(x_s[rows, :], w_s[1])
        inner_grad = mm(dr_s[rows, :], w_s[2])
        sig = 0.5 * jnp.tanh(0.5 * gate_act) + 0.5
        act = gate_act * sig
        inner_out[rows, :] = (act * up_act).astype(BF)
        gate_out[rows, :] = (inner_grad * up_act * (sig + act * (1.0 - sig))).astype(BF)
        up_out[rows, :] = (inner_grad * act).astype(BF)
    if own:
        result = mm_nt(inner_out[...], w_s[2])
        packed = mm_nt(gate_out[...], w_s[0]) + mm_nt(up_out[...], w_s[1])

        @pl.when(step == 0)
        def _():
            acc[0] = result
            acc[1] = packed

        @pl.when(step > 0)
        def _():
            acc[0] += result
            acc[1] += packed

        @pl.when(step == pl.num_programs(0) - 1)
        def _():
            mine_out[...] = acc[:, :n, :]
            theirs_out[...] = acc[:, n:, :].astype(BF)


def weight_kernel(dims, *refs):
    meta = place_of()
    F, D, Z = dims
    planes, refs = [refs[5 * p : 5 * p + 5] for p in range(Z)], refs[5 * Z :]
    outs, (acc,) = refs[:F], refs[F:]
    d_local = D // F
    for i, (left, right) in enumerate(((3, 1), (3, 2), (4, 0))):
        total = mm(planes[0][left][...], planes[0][right][...])
        for p in range(1, Z):
            total = total + mm(planes[p][left][...], planes[p][right][...])
        acc[i] = total.astype(BF)
    for k in range(F):
        at = pl.ds(pl.multiple_of(lax.rem(meta[2] + k, F) * d_local, d_local), d_local)
        for i in range(3):
            outs[k][i] = acc[i, at, :]


def combine_kernel(dims, hidden, grad, small, prev, routes, slots, *refs):
    meta = place_of()
    Z, F, S, R, D, G, hw, per, _ = dims
    rets, refs = refs[:F], refs[F:]
    atts, refs = refs[: 2 * Z], refs[2 * Z :]
    w_full, refs = refs[0], refs[1:]
    out_block, dh_out, prev_out, refs = refs[0], refs[1], refs[2], refs[3:]
    das, refs = refs[:Z], refs[Z:]
    payloads, refs = refs[:F], refs[F:]
    back_s, gw_s, dproj_s, rows_s = refs

    def att(k, side):
        return atts[k][0] if side == 0 else atts[Z + k][...]

    f = meta[2]
    d_local = D // F
    for k in range(F):
        back_s[lax.rem(f + k, F)] = rets[k][...]
    gain = small[1:2, :]
    small_all = small[...]
    small_low = small_all.astype(BF)
    small_grads = jnp.zeros((16, D), F32)
    gain_grad = jnp.zeros((1, D), F32)
    for s in range(S):
        at = slice(s * R, (s + 1) * R)
        tile = hidden[at, :]
        factor = norm_of(tile)
        normal = tile * factor
        unit = normal * gain
        unit_low = unit.astype(BF)
        logits = mm_nt(unit_low, small_low)
        before, route = columns_of(prev, routes, s)
        lane, router, hots, gates = router_parts(logits, before, route)
        g_low = grad[s]
        g = g_low.astype(F32)

        def column(t, index):
            return jnp.sum(jnp.where(lane == index, t, 0.0), axis=-1, keepdims=True)

        shares = []
        for i in range(NC):
            a, b = column(logits, 10 + 2 * i), column(logits, 11 + 2 * i)
            top = jnp.maximum(a, b)
            ea, eb = jnp.exp(a - top), jnp.exp(b - top)
            shares.append((ea / (ea + eb), eb / (ea + eb)))
        back = []
        for part in range(2):
            experts = []
            for e in range(NF):
                to = slice(s * MOST, (s + 1) * MOST)
                total = back_s[e * per, part, to, :]
                for j in range(1, per):
                    total = total.astype(F32) + back_s[e * per + j, part, to, :].astype(F32)
                experts.append(total.astype(BF))
            back.append(jnp.concatenate(experts, axis=0))
        slot = lax.broadcasted_iota(jnp.int32, (NF * MOST, R), 0)
        picks = [
            (slot == slots[2 * s + w : 2 * s + w + 1, :]).astype(F32).astype(BF)
            for w in range(TOP)
        ]
        values = [mm_tn(picks[w], back[0]) for w in range(TOP)]
        unit_grad = mm_tn(picks[0] + picks[1], back[1])
        ug = jnp.sum(unit * g, axis=-1, keepdims=True)
        vg_all = mm_nt(g_low, small_low)
        vg = [column(vg_all, 14 + i) for i in range(NC)]

        def named(w, e):
            return (route[:, w : w + 1] == e).astype(F32)

        gate_grads = []
        coef_unit = jnp.zeros((R, 1), F32)
        for w in range(TOP):
            total = jnp.sum(g * values[w], axis=-1, keepdims=True) + named(w, NF + 1) * ug
            coef_unit = coef_unit + gates[w] * named(w, NF + 1)
            for i in range(NC):
                here = named(w, NF + 2 + i)
                total = total + here * (shares[i][0] * ug + shares[i][1] * vg[i])
                coef_unit = coef_unit + gates[w] * here * shares[i][0]
            gate_grads.append(total)
        mixture = gates[0] * values[0] + gates[1] * values[1] + coef_unit * unit
        prob_grad = sum(jnp.where(hots[w], gate_grads[w], 0.0) for w in range(TOP))
        prev_grad = router * (prob_grad - jnp.sum(router * prob_grad, axis=-1, keepdims=True))
        prev_out[s] = prev_grad.T[2 : 2 + NE, :]
        left = prev_grad
        right = jnp.zeros_like(prev_grad)
        for i in range(NC):
            amount = sum(gates[w] * named(w, NF + 2 + i) for w in range(TOP))
            s0, s1 = shares[i]
            mixture = mixture + amount * s1 * small_all[14 + i : 15 + i, :]
            d0, d1 = amount * ug, amount * vg[i]
            inner = s0 * d0 + s1 * d1
            left = left + jnp.where(lane == 10 + 2 * i, s0 * (d0 - inner), 0.0)
            left = left + jnp.where(lane == 11 + 2 * i, s1 * (d1 - inner), 0.0)
            right = right + jnp.where(lane == 14 + i, amount * s1, 0.0)
        out_block[s] = (tile + mixture).astype(BF)
        left_high, left_low = split(left)
        right_high, right_low = split(right)
        unit_grad = unit_grad + mm(left_high, small_low) + mm(left_low, small_low)
        unit_grad = unit_grad + coef_unit * g
        small_grads = small_grads + mm_tn(left_high, unit_low) + mm_tn(left_low, unit_low)
        small_grads = small_grads + mm_tn(right_high, g_low) + mm_tn(right_low, g_low)
        gain_grad = gain_grad + jnp.sum(unit_grad * normal, axis=0, keepdims=True)
        scaled = unit_grad * gain
        dh = g + factor * (scaled - normal * jnp.mean(scaled * normal, axis=-1, keepdims=True))
        dh_out[at, :] = dh
        dproj_s[at, :] = dh.astype(BF)
    row = lax.broadcasted_iota(jnp.int32, (16, D), 0)
    small_grads = jnp.where(row == 1, gain_grad, small_grads).astype(BF)
    for i in range(F):
        rows_s[i] = small_grads[:, i * d_local : (i + 1) * d_local]
    gw_s[...] = jnp.zeros_like(gw_s)
    for k in range(Z):
        for side in range(2):
            seq, group = piece_at((Z, G), meta, k, side)
            dproj = dproj_s[pl.ds(pl.multiple_of(seq * R, R), R), :]
            heads = pl.ds(pl.multiple_of(group * hw, hw), hw)
            das[k][side] = mm_nt(dproj, w_full[heads, :]).astype(BF)
            gw_s[heads, :] += mm_tn(att(k, side), dproj)
    for k in range(F):
        ff = lax.rem(f + k, F)
        at = pl.ds(pl.multiple_of(ff * d_local, d_local), d_local)
        payloads[k][:d_local, :] = gw_s[at, :].astype(BF)
        payloads[k][d_local:, :d_local] = rows_s[ff]
        payloads[k][d_local:, d_local:] = jnp.zeros((16, D - d_local), BF)


def back_kernel(dims, blocks, start, cos, sin, small, *refs):
    Z, F, R, D, L, hpd, block = dims
    hw = hpd * HD
    dos, refs = refs[: 2 * Z], refs[2 * Z :]
    (normed, weight, q_in, k_in, v_in, kt_in, ot_in, lse_in), refs = refs[:8], refs[8:]
    payloads, refs = refs[:F], refs[F:]
    mixed_s, do_s, delta_s, dq_s, dk_s, dv_s, gw_s, rows_s = refs
    z, core, f, _ = place_of()
    d_local = D // F
    for k in range(Z):
        for side in range(2):
            at = lax.rem(z + k, Z) * 2 + (core if side == 0 else 1 - core)
            rows = pl.ds(pl.multiple_of(at * R, R), R)
            tile = dos[k][0] if side == 0 else dos[Z + k][...]
            turned = tile.astype(F32).T
            for h in range(hpd):
                heads = slice(h * HD, (h + 1) * HD)
                do_s[h, rows, :] = tile[:, heads]
                delta_s[h, :, rows] = jnp.sum(
                    turned[heads, :] * ot_in[h, :, rows], axis=0, keepdims=True
                )
    dk_s[...] = jnp.zeros_like(dk_s)
    dv_s[...] = jnp.zeros_like(dv_s)

    def query_step(qb, carry):
        rows = pl.ds(pl.multiple_of(qb * block, block), block)
        first = start[:, rows]
        q_pos = qb * block + lax.broadcasted_iota(jnp.int32, (block, block), 1)
        down = lax.broadcasted_iota(jnp.int32, (block, block), 0)
        queries = [q_in[h, rows, :] for h in range(hpd)]
        upstream = [do_s[h, rows, :] for h in range(hpd)]
        lses = [lse_in[h, :, rows] for h in range(hpd)]
        deltas = [delta_s[h, :, rows] for h in range(hpd)]

        def key_step(kb, state):
            keys = pl.ds(pl.multiple_of(kb * block, block), block)
            k_pos = kb * block + down
            allowed = (k_pos <= q_pos) & (k_pos >= first)
            new = []
            for h in range(hpd):
                scores = mm_nt(k_in[h, keys, :], queries[h])
                weights = jnp.where(allowed, jnp.exp(scores - lses[h]), 0.0)
                dp = mm_nt(v_in[h, keys, :], upstream[h])
                ds = (weights * (dp - deltas[h])).astype(BF)
                dv_s[h, keys, :] += mm(weights.astype(BF), upstream[h])
                dk_s[h, keys, :] += mm(ds, queries[h])
                new.append(state[h] + mm(kt_in[h, :, keys], ds))
            return tuple(new)

        begin = tuple(jnp.zeros((HD, block), F32) for _ in range(hpd))
        state = lax.fori_loop(blocks[qb], qb + 1, key_step, begin)
        for h in range(hpd):
            dq_s[h, rows, :] = state[h].T * HD ** (-0.5)
        return carry

    lax.fori_loop(0, L // block, query_step, 0)

    def unrotate(step, carry):
        rows = pl.ds(pl.multiple_of(step * block, block), block)
        cosine, sine = cos[rows, :], signed(sin[rows, :])
        parts = [[], [], []]
        for h in range(hpd):
            dq = dq_s[h, rows, :]
            dk = dk_s[h, rows, :]
            parts[0].append((dq * cosine - halves_swapped(dq) * sine).astype(BF))
            parts[1].append((dk * cosine - halves_swapped(dk) * sine).astype(BF))
            parts[2].append(dv_s[h, rows, :].astype(BF))
        mixed_s[rows, :] = jnp.concatenate(parts[0] + parts[1] + parts[2], axis=-1)
        return carry

    lax.fori_loop(0, L // block, unrotate, 0)
    gw = mm_tn(normed[...], mixed_s[...])
    gw_s[...] = gw.astype(BF)
    high, low = split(gw * weight[...].astype(F32))
    ones = jnp.ones((16, 3 * hw), BF)
    total = ((mm_nt(ones, high) + mm_nt(ones, low)) / small[0:1, :]).astype(BF)
    for i in range(F):
        rows_s[i] = total[:, i * d_local : (i + 1) * d_local]
    for k in range(F):
        ff = lax.rem(f + k, F)
        at = pl.ds(pl.multiple_of(ff * d_local, d_local), d_local)
        payloads[k][:d_local, :] = gw_s[at, :]
        payloads[k][d_local:, :d_local] = rows_s[ff]
        if d_local < 3 * hw:
            payloads[k][d_local:, d_local:] = jnp.zeros((16, 3 * hw - d_local), BF)


def normed_grad_kernel(dims, mixed, weight, mine, theirs):
    Z, R = dims
    core = place_of()[1]
    for chip in range(Z):
        for parity in range(2):
            row = (2 * chip + parity) * R
            part = mm_nt(mixed[row : row + R, :], weight[...]).astype(BF)

            @pl.when(core == parity)
            def _():
                mine[chip] = part

            @pl.when(core != parity)
            def _():
                theirs[chip] = part


def pair_kernel(Z, mine, theirs, *outs):
    meta = place_of()
    for k in range(Z):
        chip = lax.rem(meta[0] + k, Z)
        outs[k][...] = (mine[chip].astype(F32) + theirs[chip].astype(F32)).astype(BF)


def last_kernel(dims, x, dh, small, *refs):
    meta = place_of()
    Z, S, R, _, G = dims
    dns, out, acc = refs[:Z], refs[Z], refs[Z + 1]
    acc[...] = jnp.zeros_like(acc)
    for k in range(Z):
        seq, _ = piece_at((Z, G), meta, k, 0)
        acc[seq] += dns[k][...].astype(F32)
    gain = small[0:1, :]
    for s in range(S):
        tile = x[s].astype(F32)
        factor = norm_of(tile)
        normal = tile * factor
        scaled = acc[s] * gain
        out[s] = dh[s * R : (s + 1) * R, :] + factor * (
            scaled - normal * jnp.mean(scaled * normal, axis=-1, keepdims=True)
        )


def place_kernel(dims, ks, left, *refs):
    meta = place_of()
    F, per, CW, width = dims
    n = len(ks)
    ours, theirs, refs = refs[:n], refs[n : 2 * n], refs[2 * n :]
    outs, (buf, sems) = refs[-5:-2], refs[-2:]
    copies = []
    for side in range(2):
        for j, k in enumerate(ks):
            dev = lax.rem(meta[2] - k + F, F)
            core = meta[1] if side == 0 else 1 - meta[1]
            e = lax.div(dev, per)
            lane = (lax.rem(dev, per) * 2 + core) * CW + left
            lanes = pl.ds(pl.multiple_of(lane, 128), width)
            for i in range(3):
                at = (side * n + j) * 3 + i
                buf[at] = (ours if side == 0 else theirs)[j][i].astype(F32)
                copy = pltpu.make_async_copy(buf.at[at], outs[i].at[:, e, lanes], sems.at[at])
                copy.start()
                copies.append(copy)
    for copy in copies:
        copy.wait()


def qkv_grad_kernel(dims, *refs):
    meta = place_of()
    G, D, d_local, hw = dims
    pieces, (out, gain_out, table) = refs[:-3], refs[-3:]
    group = lax.rem(meta[3], G)
    at = 0
    for piece in pieces:
        for j in range(piece.shape[0]):
            table[at] = piece[j]
            at += 1
    gain = jnp.zeros((1, d_local), F32)
    for i in range(G):
        tile = table[jnp.bitwise_xor(group, i)].astype(F32)
        gain = gain + tile[d_local : d_local + 1, :d_local]
        width = max(0, min(hw, D - i * hw))
        if width:
            for part in range(3):
                out[:, part * D + i * hw : part * D + i * hw + width] = tile[
                    :d_local, part * hw : part * hw + width
                ]
    gain_out[...] = gain


def body(
    block_input,
    attn_gain,
    w_qkv,
    w_out,
    ffn_gain,
    w_router,
    w_gate,
    w_up,
    w_down,
    const_mix,
    const_vec,
    prev_logits,
    routes,
    doc_ids,
    d_out,
    *,
    F,
    C,
):
    S, R, D = block_input.shape
    L = doc_ids.shape[1]
    Z = C // 2
    G = C // S
    hpd = -(-H // G)
    hw = hpd * HD
    FF = w_gate.shape[2]
    per = F // NF
    CW = FF // (2 * per)
    d_local = D // F
    T = S * R
    block = min(512, L)
    shaped = jax.ShapeDtypeStruct
    f = lax.axis_index("fsdp")
    c = lax.axis_index("ctx")
    core = c % 2
    z = c // 2

    def fs(t, k):
        return lax.ppermute(t, "fsdp", [(i, (i + k) % F) for i in range(F)])

    def zs(t, k):
        return lax.ppermute(
            t, "ctx", [(2 * i + j, 2 * ((i + k) % Z) + j) for i in range(Z) for j in range(2)]
        )

    def cx(t):
        return lax.ppermute(t, "ctx", [(i, i ^ 1) for i in range(C)])

    def pick(t, index, axis=0):
        return lax.dynamic_index_in_dim(t, index, axis, keepdims=False)

    def seq_of(chip):
        return chip // (Z // S)

    def expert_of(dev):
        return lax.div(dev, per)

    def chunk_of(dev):
        return (dev % per) * 2 + core

    def call(kernel, name, out_shape, args, scratch=(), smem=0, **kw):
        return pl.pallas_call(
            kernel,
            out_shape=out_shape,
            in_specs=[SMEM] * smem + [VMEM] * (len(args) - smem),
            out_specs=tuple([VMEM] * len(out_shape)),
            scratch_shapes=list(scratch),
            compiler_params=params(name, L > 2048),
            **kw,
        )(*args)

    x_mine = [pick(block_input, seq_of(z))] + [
        zs(pick(block_input, seq_of((z + k) % Z)), k) for k in range(1, Z)
    ]
    x_theirs = [cx(t) for t in x_mine]

    my_docs = pick(doc_ids, c // G)
    start = jnp.sum((my_docs[None, :] < my_docs[:, None]).astype(jnp.int32), axis=1)
    first_block = start.reshape(L // block, block)[:, 0] // block
    route_rows = routes.transpose(0, 2, 1).reshape(S * TOP, R)
    prev = prev_logits.transpose(0, 2, 1)

    slot_rows, *packs = call(
        functools.partial(pack_kernel, (F, S, R, D, G, hpd, expert_of)),
        "pack",
        (shaped((S * TOP, R), jnp.int32),) + (shaped((S * MOST + d_local + 16, D), BF),) * F,
        (
            d_out,
            route_rows,
            w_qkv,
            jnp.stack([attn_gain, ffn_gain]),
            w_router.T,
            const_mix.T,
            const_vec.T,
        ),
        [pltpu.VMEM((NF, S * MOST, D), BF)],
    )
    w_pieces = [packs[0]] + [fs(packs[k], k) for k in range(1, F)]
    (g_mine,) = call(
        functools.partial(stack_kernel, S * MOST),
        "stack",
        (shaped((F * S * MOST, D), BF),),
        tuple(w_pieces),
    )
    o_pieces = [w_out] + [fs(w_out, k) for k in range(1, F)]

    def expert_slices():
        if per == 1:
            cut = [
                lax.dynamic_slice_in_dim(w, core * CW, CW, 2).transpose(1, 0, 2)
                for w in (w_gate, w_up, w_down)
            ]
            cut = lax.optimization_barrier(cut)
            return call(
                functools.partial(order_kernel, F),
                "order",
                (shaped((3, d_local, CW), BF),) * F,
                tuple(cut),
            )
        out = []
        for k in range(F):
            dev = (f + k) % F
            out.append(
                jnp.stack(
                    [
                        pick(
                            lax.dynamic_slice_in_dim(w, chunk_of(dev) * CW, CW, 2),
                            expert_of(dev),
                            1,
                        )
                        for w in (w_gate, w_up, w_down)
                    ]
                )
            )
        return out

    slices = expert_slices()
    e_pieces = [slices[0]] + [fs(slices[k], k) for k in range(1, F)]

    frequency = jnp.exp(jnp.arange(HD // 2, dtype=F32) * (-2.0 * math.log(10000.0) / HD))
    frequency = jnp.concatenate([frequency, frequency])
    low = jnp.arange(32).astype(F32)[:, None] * frequency[None, :]
    high = (32 * jnp.arange(L // 32)).astype(F32)[:, None] * frequency[None, :]
    tables = (jnp.cos(low), jnp.sin(low), jnp.cos(high), jnp.sin(high))
    dims = (Z, F, R, D, L, hpd, block)
    normed, qkv_w, small, cosine, sine, q, k_, v, kt, ot, lse, *att_pieces = call(
        functools.partial(attend_kernel, dims),
        "attend",
        (
            shaped((L, D), BF),
            shaped((D, 3 * hw), BF),
            shaped((16, D), F32),
            shaped((L, HD), F32),
            shaped((L, HD), F32),
            shaped((hpd, L, HD), BF),
            shaped((hpd, L, HD), BF),
            shaped((hpd, L, HD), BF),
            shaped((hpd, HD, L), BF),
            shaped((hpd, HD, L), F32),
            shaped((hpd, 1, L), F32),
        )
        + (shaped((2, R, hw), BF),) * Z,
        (first_block, start[None], *tables, *x_mine, *x_theirs, *w_pieces),
        [
            pltpu.VMEM((F, 16, d_local), F32),
            pltpu.VMEM((hpd, HD, L), BF),
            pltpu.VMEM((C, R, hw), BF),
        ],
        smem=1,
    )

    g_planes = [(g_mine, cx(g_mine))] + [zs(g_mine, k) for k in range(1, Z)]

    pieces = [att_pieces[0]] + [zs(att_pieces[k], k) for k in range(1, Z)]
    atts = pieces + [cx(t[1]) for t in pieces]
    outs = call(
        functools.partial(dispatch_kernel, (Z, F, S, R, D, G, hw, expert_of)),
        "dispatch",
        (shaped((T, D), F32), shaped((G * hw, D), BF))
        + (shaped((S * MOST, D + 128), BF),) * F,
        (block_input, small, prev, route_rows, slot_rows, *atts, *o_pieces),
        [pltpu.VMEM((NF, S * MOST, D + 128), BF)],
    )
    hidden, out_w, toks = outs[0], outs[1], outs[2:]
    own = [toks[0]] + [fs(toks[k], k) for k in range(1, F)]
    (own,) = call(
        functools.partial(stack_kernel, S * MOST),
        "stack",
        (shaped((F * S * MOST, D + 128), BF),),
        tuple(own),
    )
    n = own.shape[0]

    steps = 4 if CW % 512 == 0 else 2
    cut = CW // steps
    e_spec = pl.BlockSpec((3, d_local, cut), lambda i: (0, 0, i))
    act_spec = pl.BlockSpec((2 * n, cut), lambda i: (0, i))
    both_spec = pl.BlockSpec((D, 2 * n), lambda i: (0, 0))

    def ffn(at, rows, theirs, g_rows):
        own_plane = at == 0
        shapes = (shaped((2 * n, CW), BF),) * 3 + (shaped((D, 2 * n), BF),) * 2
        specs = (act_spec,) * 3 + (both_spec,) * 2
        scratch = [pltpu.VMEM((2 * n, D), BF), pltpu.VMEM((2 * n, D), BF)]
        w_spec = pl.BlockSpec((3, D, cut), lambda i: (0, 0, i))
        if own_plane:
            shapes += (shaped((2, n, D), F32), shaped((2, n, D), BF), shaped((3, D, CW), BF))
            specs += (pl.BlockSpec((2, n, D), lambda i: (0, 0, 0)),) * 2 + (w_spec,)
            scratch.append(pltpu.VMEM((2, 2 * n, D), F32))
        row_spec = pl.BlockSpec((n, D + 128), lambda i: (0, 0))
        g_spec = pl.BlockSpec((n, D), lambda i: (0, 0))
        return pl.pallas_call(
            functools.partial(ffn_kernel, (F, D), own_plane),
            out_shape=shapes,
            grid=(steps,),
            in_specs=[row_spec, row_spec, g_spec, g_spec]
            + ([e_spec] * F if own_plane else [w_spec]),
            out_specs=specs,
            scratch_shapes=scratch,
            compiler_params=params("experts" if at else "experts0", L > 2048),
        )(rows, theirs, *g_rows, *(e_pieces if own_plane else [weights]))

    *plane, back_mine, back_theirs, weights = ffn(0, own, cx(own), g_planes[0])
    planes = [plane]
    back = (back_mine + cx(back_theirs).astype(F32)).astype(BF).reshape(2, F, S * MOST, D)
    rets = [back[:, 0]] + [fs(back[:, k], -k) for k in range(1, F)]
    ring = [own]
    for _ in range(1, Z):
        ring.append(zs(ring[-1], 1))

    def far(k, after):
        rows, g_rows, _ = lax.optimization_barrier((ring[k], g_planes[k], after))
        planes.append(ffn(k, rows, cx(rows), (g_rows, cx(g_rows))))

    far(1, back_mine)
    outs = call(
        functools.partial(combine_kernel, (Z, F, S, R, D, G, hw, per, expert_of)),
        "combine",
        (shaped((S, R, D), BF), shaped((T, D), F32), shaped((S, NE, R), F32))
        + (shaped((2, R, hw), BF),) * Z
        + (shaped((d_local + 16, D), BF),) * F,
        (hidden, d_out, small, prev, route_rows, slot_rows, *rets, *atts, out_w),
        [
            pltpu.VMEM((F, 2, S * MOST, D), BF),
            pltpu.VMEM((G * hw, D), F32),
            pltpu.VMEM((T, D), BF),
            pltpu.VMEM((F, 16, d_local), BF),
        ],
    )
    out_block, hidden_grad, prev_grad = outs[:3]
    das, o_payloads = outs[3 : 3 + Z], outs[3 + Z :]
    grad_prev = prev_grad.transpose(0, 2, 1)

    do_pieces = [das[0]] + [zs(das[k], -k) for k in range(1, Z)]
    dos = do_pieces + [cx(t[1]) for t in do_pieces]

    for k in range(2, Z):
        far(k, hidden_grad)
    flat = [t for plane in planes for t in plane]
    wide = 256
    widths = [CW - wide, wide]
    e_grads = []
    for part, width in enumerate(widths):
        left = sum(widths[:part])
        if Z > 4:
            lanes = slice(left, left + width)
            trio = [
                sum(mm(plane[a], plane[b][:, lanes]) for plane in planes).astype(BF)
                for a, b in ((3, 1), (3, 2), (4, 0))
            ]
            trio = jnp.stack(trio).reshape(3, F, d_local, width)
            e_grads.append([pick(trio, (f + k) % F, 1) for k in range(F)])
            continue
        acts = pl.BlockSpec((2 * n, wide), lambda i, b=left // wide: (0, b + i))
        e_grads.append(
            pl.pallas_call(
                functools.partial(weight_kernel, (F, D, Z)),
                out_shape=(shaped((3, d_local, width), BF),) * F,
                grid=(width // wide,),
                in_specs=[acts, acts, acts, both_spec, both_spec] * Z,
                out_specs=(pl.BlockSpec((3, d_local, wide), lambda i: (0, 0, i)),) * F,
                scratch_shapes=[pltpu.VMEM((3, D, wide), BF)],
                compiler_params=params("expert_grads", L > 2048),
            )(*flat)
        )
    dos[0], *_ = lax.optimization_barrier((dos[0], e_grads[-1][0]))
    outs = call(
        functools.partial(back_kernel, dims),
        "attend_back",
        (shaped((d_local + 16, 3 * hw), BF),) * F + (shaped((L, 3 * hw), BF),),
        (
            first_block,
            start[None],
            cosine,
            sine,
            small,
            *dos,
            normed,
            qkv_w,
            q,
            k_,
            v,
            kt,
            ot,
            lse,
        ),
        [
            pltpu.VMEM((hpd, L, HD), BF),
            pltpu.VMEM((hpd, 1, L), F32),
            pltpu.VMEM((hpd, L, HD), F32),
            pltpu.VMEM((hpd, L, HD), F32),
            pltpu.VMEM((hpd, L, HD), F32),
            pltpu.VMEM((D, 3 * hw), BF),
            pltpu.VMEM((F, 16, d_local), BF),
        ],
        smem=1,
    )
    q_payloads, mixed_grad = outs[:F], outs[F]
    dn_mine, dn_theirs = call(
        functools.partial(normed_grad_kernel, (Z, R)),
        "normed_grad",
        (shaped((Z, R, D), BF),) * 2,
        (mixed_grad, qkv_w),
    )
    dns = call(
        functools.partial(pair_kernel, Z),
        "pair",
        (shaped((R, D), BF),) * Z,
        (dn_mine, cx(dn_theirs)),
    )
    dns = [dns[0]] + [zs(dns[k], k) for k in range(1, Z)]
    (grad_x,) = call(
        functools.partial(last_kernel, (Z, S, R, D, G)),
        "input_grad",
        (shaped((S, R, D), F32),),
        (block_input, hidden_grad, small, *dns),
        [pltpu.VMEM((S, R, D), F32)],
    )

    def moved_rows(parts):
        return [parts[0]] + [fs(parts[k], k) for k in range(1, F)]

    def summed_rows(parts):
        return sum(p.astype(F32) for p in parts).astype(BF)

    def over_ctx(t):
        step = 1
        while step < C:
            moved = lax.ppermute(t, "ctx", [(i, i ^ step) for i in range(C)])
            t = (t.astype(F32) + moved.astype(F32)).astype(BF)
            step *= 2
        return t

    payload = summed_rows(moved_rows(q_payloads))
    summed = payload.astype(F32)
    for j in range(1, S):
        moved = lax.ppermute(payload, "ctx", [(i, (i + j * G) % C) for i in range(C)])
        summed = summed + moved.astype(F32)
    payload = summed.astype(BF)[None]
    gathered = [payload]
    step = 1
    while step < G:
        gathered.append(lax.ppermute(payload, "ctx", [(i, i ^ step) for i in range(C)]))
        step *= 2
        if step < G:
            payload = jnp.concatenate([payload, gathered[-1]], axis=0)
    grad_qkv, grad_gain_one = call(
        functools.partial(qkv_grad_kernel, (G, D, d_local, hw)),
        "qkv_grad",
        (shaped((d_local, 3 * D), F32), shaped((1, d_local), F32)),
        tuple(gathered),
        [pltpu.VMEM((G, d_local + 16, 3 * hw), BF)],
    )
    grad_gain_one = grad_gain_one[0]

    moved = moved_rows(o_payloads)
    payload = over_ctx(summed_rows(moved)).astype(F32)
    grad_w_out = payload[:d_local]
    smalls = payload[d_local:, :d_local]

    ANY = pl.BlockSpec(memory_space=pl.ANY)
    placed = ()
    for part, width in enumerate(widths):
        ours = [e_grads[part][0]] + [fs(e_grads[part][k], k) for k in range(1, F)]
        theirs = [cx(t) for t in ours]
        groups = [list(range(F))]
        for ks in groups:
            args = (*[ours[k] for k in ks], *[theirs[k] for k in ks], *placed)
            at = 2 * len(ks)
            placed = pl.pallas_call(
                functools.partial(
                    place_kernel, (F, per, CW, width), ks, sum(widths[:part])
                ),
                out_shape=(shaped((d_local, NF, FF), F32),) * 3,
                in_specs=[VMEM] * (2 * len(ks)) + [ANY] * len(placed),
                out_specs=(ANY,) * 3,
                input_output_aliases={at + i: i for i in range(len(placed))},
                scratch_shapes=[
                    pltpu.VMEM((6 * len(ks), d_local, width), F32),
                    pltpu.SemaphoreType.DMA((6 * len(ks),)),
                ],
                compiler_params=params("place", L > 2048),
            )(*args)
    grad_gate, grad_up, grad_down = placed
    return (
        out_block,
        grad_x,
        grad_prev,
        grad_gain_one,
        grad_qkv,
        grad_w_out,
        smalls[1],
        smalls[2:10].T,
        grad_gate,
        grad_up,
        grad_down,
        smalls[10:14].T,
        smalls[14:16].T,
    )


def solution(mesh):
    F, Z = mesh.shape["fsdp"], mesh.shape["ctx"] // 2

    def layer(*args):
        return body(*args, F=F, C=2 * Z)

    return jax.shard_map(
        layer,
        mesh=mesh,
        in_specs=(
            P("fsdp", "ctx", None),
            P("fsdp"),
            P("fsdp", None),
            P("fsdp", None),
            P("fsdp"),
            P("fsdp", None),
            P("fsdp", None, None),
            P("fsdp", None, None),
            P("fsdp", None, None),
            P("fsdp", None),
            P("fsdp", None),
            P("fsdp", "ctx", None),
            P("fsdp", "ctx", None),
            P("fsdp", None),
            P("fsdp", "ctx", None),
        ),
        out_specs=(
            P("fsdp", "ctx", None),
            P("fsdp", "ctx", None),
            P("fsdp", "ctx", None),
            P("fsdp"),
            P("fsdp", None),
            P("fsdp", None),
            P("fsdp"),
            P("fsdp", None),
            P("fsdp", None, None),
            P("fsdp", None, None),
            P("fsdp", None, None),
            P("fsdp", None),
            P("fsdp", None),
        ),
        check_vma=False,
    )
```

```python
import functools
import math

import jax
import jax.numpy as jnp
from jax import lax
from jax.experimental import pallas as pl
from jax.experimental.pallas import tpu as pltpu
from jax.sharding import PartitionSpec as P


H = 12
HD = 64
NF = 4
NC = 2
NE = 8
TOP = 2
MOST = 48
FS, CT = "fsdp", "ctx"
BF = jnp.bfloat16
F32 = jnp.float32


def dot(a, b, dims):
    return lax.dot_general(a, b, (dims, ((), ())), preferred_element_type=F32)


def mm(a, b):
    return dot(a, b, ((1,), (0,)))


def mm_nt(a, b):
    return dot(a, b, ((1,), (1,)))


def mm_tn(a, b):
    return dot(a, b, ((0,), (0,)))


def halves_swapped(t):
    half = t.shape[-1] // 2
    return jnp.concatenate([t[:, half:], t[:, :half]], axis=-1)


VMEM = pl.BlockSpec(memory_space=pltpu.VMEM)
SMEM = pl.BlockSpec(memory_space=pltpu.SMEM)


GRANTS = {
    "pack": 3,
    "rows": 3,
    "stack": 2,
    "order": 4,
    "attend": 10,
    "disp": 4,
    "ex0": 20,
    "ex": 11,
    "combine": 12,
    "wg": 14,
    "back": 16,
    "ng": 3,
    "pair": 2,
    "ig": 4,
    "place": 18,
    "qg": 4,
}


def params(name, long=False):
    return pltpu.CompilerParams(vmem_limit_bytes=(56 if long else GRANTS[name]) << 20)


def place_of():
    c = lax.axis_index(CT)
    return lax.div(c, 2), lax.rem(c, 2), lax.axis_index(FS), c


def norm_of(tile):
    return lax.rsqrt(jnp.mean(tile * tile, axis=-1, keepdims=True) + 1e-05)


def split(t):
    high = t.astype(BF)
    return high, (t - high.astype(F32)).astype(BF)


def pack_kernel(dims, w_qkv, gains, router, mix, vec, first):
    meta = place_of()
    F, D, G, hpd = dims
    hw = hpd * HD
    d_local = D // F
    group = lax.rem(meta[3], G)
    for g in range(G):
        width = max(0, min(hw, H * HD - g * hw))

        @pl.when(group == g)
        def _():
            for part in range(3):
                if width:
                    first[:d_local, part * hw : part * hw + width] = w_qkv[
                        :, part * H * HD + g * hw : part * H * HD + g * hw + width
                    ]
                if width < hw:
                    first[:d_local, part * hw + width : (part + 1) * hw] = jnp.zeros(
                        (d_local, hw - width), BF
                    )

    rows = [t[...].astype(F32) for t in (gains, router, mix, vec)]
    first[d_local:, :d_local] = jnp.concatenate(rows, axis=0).astype(BF)
    if d_local < 3 * hw:
        first[d_local:, d_local:] = jnp.zeros((16, 3 * hw - d_local), BF)


def grad_rows_kernel(dims, grad, routes, slots, *outs):
    meta = place_of()
    F, S, R, _, expert_of = dims
    table = outs[-1]
    below = lax.broadcasted_iota(jnp.int32, (R, R), 0)
    earlier = (below < lax.broadcasted_iota(jnp.int32, (R, R), 1)).astype(F32).astype(BF)
    expert = lax.broadcasted_iota(jnp.int32, (8, R), 0)
    for s in range(S):
        named = [routes[2 * s + w : 2 * s + w + 1, :] for w in range(TOP)]
        hots = [(expert == t).astype(F32) for t in named]
        counts = mm((hots[0] + hots[1]).astype(BF), earlier)
        lines = []
        for w in range(TOP):
            rank = jnp.sum(hots[w] * counts, axis=0, keepdims=True).astype(jnp.int32)
            line = jnp.where(named[w] < NF, named[w] * MOST + rank, -1)
            slots[2 * s + w : 2 * s + w + 1, :] = line
            lines.append(line)
        slot = lax.broadcasted_iota(jnp.int32, (NF * MOST, R), 0)
        picks = (slot == lines[0]) | (slot == lines[1])
        moved = mm(picks.astype(F32).astype(BF), grad[s]).astype(BF)
        for e in range(NF):
            table[e, s * MOST : (s + 1) * MOST, :] = moved[e * MOST : (e + 1) * MOST, :]
    for k in range(F):
        outs[k][...] = table[expert_of(lax.rem(meta[2] + k, F))]


def stack_kernel(n, *refs):
    out = refs[-1]
    for i, ref in enumerate(refs[:-1]):
        out[i * n : (i + 1) * n, :] = ref[:n, :]


def order_kernel(dims, *refs):
    F, half = dims
    z, _, f, _ = place_of()
    lanes = pl.ds(pl.multiple_of(lax.rem(z, 2) * half, 128), half)
    for k in range(F):
        e = jnp.bitwise_xor(f, k)
        for i in range(3):
            refs[3 + k][i] = refs[i][e] if k < F - 1 else refs[i][e, :, lanes]


def turn_tables(cos_low, sin_low, cos_high, sin_high, cosine, sine, L):
    low = cos_low.shape[0]
    for step in range(L // low):
        a, b = cos_high[step : step + 1, :], sin_high[step : step + 1, :]
        at = slice(step * low, (step + 1) * low)
        cosine[at, :] = a * cos_low[...] - b * sin_low[...]
        sine[at, :] = b * cos_low[...] + a * sin_low[...]


def signed(sine):
    lane = lax.broadcasted_iota(jnp.int32, sine.shape, 1)
    return jnp.where(lane < HD // 2, -sine, sine)


def attend_kernel(dims, blocks, start, cos_low, sin_low, cos_high, sin_high, *refs):
    Z, F, R, D, L, hpd, block = dims
    hw = hpd * HD
    xs, refs = refs[: 2 * Z], refs[2 * Z :]
    ws, refs = refs[:F], refs[F:]
    normed, weight, small_out, cos, sin, q_out, k_out, v_out, kt_out, ot_out, lse_out = refs[:11]
    refs = refs[11:]
    pieces, (small_s, vt_s, att_s) = refs[:Z], refs[Z:]
    z, core, f, _ = place_of()
    d_local = D // F
    top = ws[0].shape[0] - d_local - 16
    turn_tables(cos_low, sin_low, cos_high, sin_high, cos, sin, L)
    for k in range(F):
        row = pl.multiple_of(lax.rem(f - k + F, F) * d_local, d_local)
        weight[pl.ds(row, d_local), :] = ws[k][top : top + d_local, : 3 * hw]
        small_s[k] = ws[k][top + d_local :, :d_local].astype(F32)
    small = jnp.concatenate([small_s[lax.rem(f - i + F, F)] for i in range(F)], axis=1)
    small_out[...] = small
    gain_row = small[0:1, :]
    for k in range(Z):
        for side in range(2):
            at = lax.rem(z - k + Z, Z) * 2 + (core if side == 0 else 1 - core)
            tile = xs[side * Z + k][...].astype(F32)
            row = pl.multiple_of(at * R, R)
            normed[pl.ds(row, R), :] = (tile * norm_of(tile) * gain_row).astype(BF)

    def project(step, carry):
        rows = pl.ds(pl.multiple_of(step * block, block), block)
        mixed = mm(normed[rows, :], weight[...])
        cosine, sine = cos[rows, :], signed(sin[rows, :])
        for h in range(hpd):
            q = mixed[:, h * HD : (h + 1) * HD]
            k = mixed[:, hw + h * HD : hw + (h + 1) * HD]
            v = mixed[:, 2 * hw + h * HD : 2 * hw + (h + 1) * HD]
            q = (q * cosine + halves_swapped(q) * sine).astype(BF)
            q_out[h, rows, :] = (q.astype(F32) * HD ** (-0.5)).astype(BF)
            k = k * cosine + halves_swapped(k) * sine
            k_out[h, rows, :] = k.astype(BF)
            kt_out[h, :, rows] = k.T.astype(BF)
            v_out[h, rows, :] = v.astype(BF)
            vt_s[h, :, rows] = v.T.astype(BF)
        return carry

    lax.fori_loop(0, L // block, project, 0)

    def query_step(qb, carry):
        rows = pl.ds(pl.multiple_of(qb * block, block), block)
        first = start[:, rows]
        q_pos = qb * block + lax.broadcasted_iota(jnp.int32, (block, block), 1)
        down = lax.broadcasted_iota(jnp.int32, (block, block), 0)
        queries = [q_out[h, rows, :] for h in range(hpd)]

        def key_step(kb, state):
            keys = pl.ds(pl.multiple_of(kb * block, block), block)
            k_pos = kb * block + down
            allowed = (k_pos <= q_pos) & (k_pos >= first)
            new = []
            for h in range(hpd):
                high, total, acc = state[h]
                scores = mm_nt(k_out[h, keys, :], queries[h])
                scores = jnp.where(allowed, scores, -1e30)
                top = jnp.maximum(high, jnp.max(scores, axis=0, keepdims=True))
                scale = jnp.exp(high - top)
                weights = jnp.where(allowed, jnp.exp(scores - top), 0.0)
                total = total * scale + jnp.sum(weights, axis=0, keepdims=True)
                acc = acc * scale + mm(vt_s[h, :, keys], weights.astype(BF))
                new.append((top, total, acc))
            return tuple(new)

        begin = tuple(
            (
                jnp.full((1, block), -1e30, F32),
                jnp.zeros((1, block), F32),
                jnp.zeros((HD, block), F32),
            )
            for _ in range(hpd)
        )
        state = lax.fori_loop(blocks[qb], qb + 1, key_step, begin)
        outs = []
        for h in range(hpd):
            high, total, acc = state[h]
            out = acc / total
            ot_out[h, :, rows] = out
            lse_out[h, :, rows] = high + jnp.log(total)
            outs.append(out)
        whole = jnp.concatenate(outs, axis=0).T.astype(BF)
        for part in range(block // R):
            att_s[qb * (block // R) + part] = whole[part * R : (part + 1) * R, :]
        return carry

    lax.fori_loop(0, L // block, query_step, 0)
    for k in range(Z):
        chip = lax.rem(z + k, Z) * 2
        pieces[k][0] = att_s[chip + core]
        pieces[k][1] = att_s[chip + 1 - core]


def piece_at(dims, meta, k, side):
    Z, G = dims
    chip = lax.rem(meta[0] - k + Z, Z)
    group = lax.rem(2 * chip + (meta[1] if side == 0 else 1 - meta[1]), G)
    return lax.div(2 * chip, G), group


def columns_of(prev, routes, s):
    width = prev.shape[2]
    gap = jnp.zeros((2, width), F32)
    tall = jnp.concatenate([gap, prev[s], jnp.zeros((6, width), F32)], axis=0)
    named = routes[2 * s : 2 * s + 2, :].astype(F32)
    named = jnp.concatenate([named, jnp.zeros((6, width), F32)], axis=0)
    return tall.T, named.T.astype(jnp.int32)


def router_parts(logits, prev, routes):
    lane = lax.broadcasted_iota(jnp.int32, logits.shape, 1)
    inside = (lane >= 2) & (lane < 2 + NE)
    shown = jnp.where(inside, logits + prev, -1e30)
    weights = jnp.exp(shown - jnp.max(shown, axis=-1, keepdims=True))
    weights = jnp.where(inside, weights, 0.0)
    router = weights / jnp.sum(weights, axis=-1, keepdims=True)
    hots = [lane == routes[:, w : w + 1] + 2 for w in range(TOP)]
    gates = [jnp.sum(jnp.where(hot, router, 0.0), axis=-1, keepdims=True) for hot in hots]
    return lane, router, hots, gates


def dispatch_kernel(dims, x, small, prev, routes, slots, *refs):
    meta = place_of()
    Z, F, S, R, D, G, hw, expert_of = dims
    atts, refs = refs[: 2 * Z], refs[2 * Z :]
    ws, refs = refs[: 2 * F], refs[2 * F :]
    hidden, w_full, toks, table = refs[0], refs[1], refs[2:-1], refs[-1]

    def att(k, side):
        return atts[k][0] if side == 0 else atts[Z + k][...]

    f = meta[2]
    d_local = D // F
    if G * hw > D:
        w_full[D:, :] = jnp.zeros((G * hw - D, D), BF)
    for k in range(F):
        row = pl.multiple_of(lax.rem(f - k + F, F) * d_local, d_local)
        for side in range(2):
            half = meta[1] if side == 0 else 1 - meta[1]
            lanes = pl.ds(pl.multiple_of(half * (D // 2), 128), D // 2)
            w_full[pl.ds(row, d_local), lanes] = ws[side * F + k][...]
    for s in range(S):
        hidden[s * R : (s + 1) * R, :] = x[s].astype(F32)
    for k in range(Z):
        for side in range(2):
            seq, group = piece_at((Z, G), meta, k, side)
            rows = pl.ds(pl.multiple_of(seq * R, R), R)
            heads = pl.ds(pl.multiple_of(group * hw, hw), hw)
            hidden[rows, :] += mm(att(k, side), w_full[heads, :])
    gain = small[1:2, :]
    small_low = small[...].astype(BF)
    for s in range(S):
        at = slice(s * R, (s + 1) * R)
        tile = hidden[at, :]
        unit_low = (tile * norm_of(tile) * gain).astype(BF)
        logits = mm_nt(unit_low, small_low)
        _, _, _, gates = router_parts(logits, *columns_of(prev, routes, s))
        slot = lax.broadcasted_iota(jnp.int32, (NF * MOST, R), 0)
        picks = [
            (slot == slots[2 * s + w : 2 * s + w + 1, :]).astype(F32).astype(BF)
            for w in range(TOP)
        ]
        packed = mm(picks[0] + picks[1], unit_low).astype(BF)
        wide = lax.broadcasted_iota(jnp.int32, (R, 128), 1)
        columns = jnp.zeros((NF * MOST, 128), F32)
        for w in range(TOP):
            high, low = split(gates[w])
            both = jnp.where(
                wide == 0, high.astype(F32), jnp.where(wide == 1, low.astype(F32), 0.0)
            )
            columns = columns + mm(picks[w], both.astype(BF))
        for e in range(NF):
            to = slice(s * MOST, (s + 1) * MOST)
            table[e, to, :D] = packed[e * MOST : (e + 1) * MOST, :]
            table[e, to, D:] = columns[e * MOST : (e + 1) * MOST, :].astype(BF)
    for k in range(F):
        toks[k][...] = table[expert_of(lax.rem(f + k, F))]


def ffn_kernel(dims, own, rows_a, rows_b, g_a, g_b, *refs):
    meta = place_of()
    F, D, n_weights = dims
    n = rows_a.shape[0]
    ws, refs = (refs[:n_weights], refs[n_weights:]) if own else ((), refs)
    if not own:
        w_s, refs = refs[0], refs[1:]
    (inner_out, gate_out, up_out, xt_out, drt_out), refs = refs[:5], refs[5:]
    if own:
        mine_out, theirs_out, w_s, x_s, dr_s, acc = refs
    else:
        x_s, dr_s = refs
    step = pl.program_id(0)
    d_local = D // F

    @pl.when(step == 0)
    def _():
        for i, (rows, g) in enumerate(((rows_a, g_a), (rows_b, g_b))):
            at = slice(i * n, (i + 1) * n)
            x_s[at, :] = rows[:, :D]
            xt_out[:, at] = rows[:, :D].T
            gate = rows[:, D : D + 1].astype(F32) + rows[:, D + 1 : D + 2].astype(F32)
            dr = (gate * g[...].astype(F32)).astype(BF)
            dr_s[at, :] = dr
            drt_out[:, at] = dr.T

    def weight_rows(dev):
        return pl.ds(pl.multiple_of(dev * d_local, d_local), d_local)

    for k, piece in enumerate(ws[:F] if len(ws) == F else ws[: F - 1]):
        dev = lax.rem(meta[2] - k + F, F) if len(ws) == F else jnp.bitwise_xor(meta[2], k)
        for i in range(3):
            w_s[i, weight_rows(dev), :] = piece[i]
    if len(ws) > F:
        at = weight_rows(jnp.bitwise_xor(meta[2], F - 1))
        cut = w_s.shape[2]
        each = ws[F].shape[2] // cut
        lanes = pl.ds(pl.multiple_of(lax.rem(step, each) * cut, 128), cut)
        for side in range(2):

            @pl.when(lax.div(step, each) == lax.rem(meta[0] + side, 2))
            def _():
                for i in range(3):
                    w_s[i, at, :] = ws[F - 1 + side][i, :, lanes]

    piece = n // 2
    for r in range(4):
        rows = slice(r * piece, (r + 1) * piece)
        gate_act = mm(x_s[rows, :], w_s[0])
        up_act = mm(x_s[rows, :], w_s[1])
        inner_grad = mm(dr_s[rows, :], w_s[2])
        sig = 0.5 * jnp.tanh(0.5 * gate_act) + 0.5
        act = gate_act * sig
        inner_out[rows, :] = (act * up_act).astype(BF)
        gate_out[rows, :] = (inner_grad * up_act * (sig + act * (1.0 - sig))).astype(BF)
        up_out[rows, :] = (inner_grad * act).astype(BF)
    if own:
        result = mm_nt(inner_out[...], w_s[2])
        packed = mm_nt(gate_out[...], w_s[0]) + mm_nt(up_out[...], w_s[1])

        @pl.when(step == 0)
        def _():
            acc[0] = result
            acc[1] = packed

        @pl.when(step > 0)
        def _():
            acc[0] += result
            acc[1] += packed

        @pl.when(step == pl.num_programs(0) - 1)
        def _():
            mine_out[...] = acc[:, :n, :]
            theirs_out[...] = acc[:, n:, :].astype(BF)


def weight_kernel(dims, *refs):
    meta = place_of()
    F, D, Z = dims
    planes, refs = [refs[5 * p : 5 * p + 5] for p in range(Z)], refs[5 * Z :]
    outs, (acc,) = refs[:F], refs[F:]
    d_local = D // F
    for i, (left, right) in enumerate(((3, 1), (3, 2), (4, 0))):
        total = mm(planes[0][left][...], planes[0][right][...])
        for p in range(1, Z):
            total = total + mm(planes[p][left][...], planes[p][right][...])
        acc[i] = total.astype(BF)
    for k in range(F):
        at = pl.ds(pl.multiple_of(lax.rem(meta[2] + k, F) * d_local, d_local), d_local)
        for i in range(3):
            outs[k][i] = acc[i, at, :]


def combine_kernel(dims, hidden, grad, small, prev, routes, slots, *refs):
    meta = place_of()
    Z, F, S, R, D, G, hw, per, _ = dims
    rets, refs = refs[:F], refs[F:]
    atts, refs = refs[: 2 * Z], refs[2 * Z :]
    w_full, refs = refs[0], refs[1:]
    out_block, dh_out, prev_out, refs = refs[0], refs[1], refs[2], refs[3:]
    das, refs = refs[:Z], refs[Z:]
    payloads, refs = refs[:F], refs[F:]
    back_s, gw_s, dproj_s, rows_s = refs

    def att(k, side):
        return atts[k][0] if side == 0 else atts[Z + k][...]

    f = meta[2]
    d_local = D // F
    for k in range(F):
        back_s[lax.rem(f + k, F)] = rets[k][...]
    gain = small[1:2, :]
    small_all = small[...]
    small_low = small_all.astype(BF)
    small_grads = jnp.zeros((16, D), F32)
    gain_grad = jnp.zeros((1, D), F32)
    for s in range(S):
        at = slice(s * R, (s + 1) * R)
        tile = hidden[at, :]
        factor = norm_of(tile)
        normal = tile * factor
        unit = normal * gain
        unit_low = unit.astype(BF)
        logits = mm_nt(unit_low, small_low)
        before, route = columns_of(prev, routes, s)
        lane, router, hots, gates = router_parts(logits, before, route)
        g_low = grad[s]
        g = g_low.astype(F32)

        def column(t, index):
            return jnp.sum(jnp.where(lane == index, t, 0.0), axis=-1, keepdims=True)

        shares = []
        for i in range(NC):
            a, b = column(logits, 10 + 2 * i), column(logits, 11 + 2 * i)
            top = jnp.maximum(a, b)
            ea, eb = jnp.exp(a - top), jnp.exp(b - top)
            shares.append((ea / (ea + eb), eb / (ea + eb)))
        back = []
        for part in range(2):
            experts = []
            for e in range(NF):
                to = slice(s * MOST, (s + 1) * MOST)
                total = back_s[e * per, part, to, :]
                for j in range(1, per):
                    total = total.astype(F32) + back_s[e * per + j, part, to, :].astype(F32)
                experts.append(total.astype(BF))
            back.append(jnp.concatenate(experts, axis=0))
        slot = lax.broadcasted_iota(jnp.int32, (NF * MOST, R), 0)
        picks = [
            (slot == slots[2 * s + w : 2 * s + w + 1, :]).astype(F32).astype(BF)
            for w in range(TOP)
        ]
        values = [mm_tn(picks[w], back[0]) for w in range(TOP)]
        unit_grad = mm_tn(picks[0] + picks[1], back[1])
        ug = jnp.sum(unit * g, axis=-1, keepdims=True)
        vg_all = mm_nt(g_low, small_low)
        vg = [column(vg_all, 14 + i) for i in range(NC)]

        def named(w, e):
            return (route[:, w : w + 1] == e).astype(F32)

        gate_grads = []
        coef_unit = jnp.zeros((R, 1), F32)
        for w in range(TOP):
            total = jnp.sum(g * values[w], axis=-1, keepdims=True) + named(w, NF + 1) * ug
            coef_unit = coef_unit + gates[w] * named(w, NF + 1)
            for i in range(NC):
                here = named(w, NF + 2 + i)
                total = total + here * (shares[i][0] * ug + shares[i][1] * vg[i])
                coef_unit = coef_unit + gates[w] * here * shares[i][0]
            gate_grads.append(total)
        mixture = gates[0] * values[0] + gates[1] * values[1] + coef_unit * unit
        prob_grad = sum(jnp.where(hots[w], gate_grads[w], 0.0) for w in range(TOP))
        prev_grad = router * (prob_grad - jnp.sum(router * prob_grad, axis=-1, keepdims=True))
        prev_out[s] = prev_grad.T[2 : 2 + NE, :]
        left = prev_grad
        right = jnp.zeros_like(prev_grad)
        for i in range(NC):
            amount = sum(gates[w] * named(w, NF + 2 + i) for w in range(TOP))
            s0, s1 = shares[i]
            mixture = mixture + amount * s1 * small_all[14 + i : 15 + i, :]
            d0, d1 = amount * ug, amount * vg[i]
            inner = s0 * d0 + s1 * d1
            left = left + jnp.where(lane == 10 + 2 * i, s0 * (d0 - inner), 0.0)
            left = left + jnp.where(lane == 11 + 2 * i, s1 * (d1 - inner), 0.0)
            right = right + jnp.where(lane == 14 + i, amount * s1, 0.0)
        out_block[s] = (tile + mixture).astype(BF)
        left_high, left_low = split(left)
        right_high, right_low = split(right)
        unit_grad = unit_grad + mm(left_high, small_low) + mm(left_low, small_low)
        unit_grad = unit_grad + coef_unit * g
        small_grads = small_grads + mm_tn(left_high, unit_low) + mm_tn(left_low, unit_low)
        small_grads = small_grads + mm_tn(right_high, g_low) + mm_tn(right_low, g_low)
        gain_grad = gain_grad + jnp.sum(unit_grad * normal, axis=0, keepdims=True)
        scaled = unit_grad * gain
        dh = g + factor * (scaled - normal * jnp.mean(scaled * normal, axis=-1, keepdims=True))
        dh_out[at, :] = dh
        dproj_s[at, :] = dh.astype(BF)
    row = lax.broadcasted_iota(jnp.int32, (16, D), 0)
    small_grads = jnp.where(row == 1, gain_grad, small_grads).astype(BF)
    for i in range(F):
        rows_s[i] = small_grads[:, i * d_local : (i + 1) * d_local]
    gw_s[...] = jnp.zeros_like(gw_s)
    for k in range(Z):
        for side in range(2):
            seq, group = piece_at((Z, G), meta, k, side)
            dproj = dproj_s[pl.ds(pl.multiple_of(seq * R, R), R), :]
            heads = pl.ds(pl.multiple_of(group * hw, hw), hw)
            das[k][side] = mm_nt(dproj, w_full[heads, :]).astype(BF)
            gw_s[heads, :] += mm_tn(att(k, side), dproj)
    for k in range(F):
        ff = lax.rem(f + k, F)
        at = pl.ds(pl.multiple_of(ff * d_local, d_local), d_local)
        payloads[k][:d_local, :] = gw_s[at, :].astype(BF)
        payloads[k][d_local:, :d_local] = rows_s[ff]
        payloads[k][d_local:, d_local:] = jnp.zeros((16, D - d_local), BF)


def back_kernel(dims, blocks, start, cos, sin, small, *refs):
    Z, F, R, D, L, hpd, block = dims
    hw = hpd * HD
    dos, refs = refs[: 2 * Z], refs[2 * Z :]
    (normed, weight, q_in, k_in, v_in, kt_in, ot_in, lse_in), refs = refs[:8], refs[8:]
    payloads, refs = refs[:F], refs[F:]
    mixed_s, do_s, delta_s, dq_s, dk_s, dv_s, gw_s, rows_s = refs
    z, core, f, _ = place_of()
    d_local = D // F
    for k in range(Z):
        for side in range(2):
            at = lax.rem(z + k, Z) * 2 + (core if side == 0 else 1 - core)
            rows = pl.ds(pl.multiple_of(at * R, R), R)
            tile = dos[k][0] if side == 0 else dos[Z + k][...]
            turned = tile.astype(F32).T
            for h in range(hpd):
                heads = slice(h * HD, (h + 1) * HD)
                do_s[h, rows, :] = tile[:, heads]
                delta_s[h, :, rows] = jnp.sum(
                    turned[heads, :] * ot_in[h, :, rows], axis=0, keepdims=True
                )
    dk_s[...] = jnp.zeros_like(dk_s)
    dv_s[...] = jnp.zeros_like(dv_s)

    def query_step(qb, carry):
        rows = pl.ds(pl.multiple_of(qb * block, block), block)
        first = start[:, rows]
        q_pos = qb * block + lax.broadcasted_iota(jnp.int32, (block, block), 1)
        down = lax.broadcasted_iota(jnp.int32, (block, block), 0)
        queries = [q_in[h, rows, :] for h in range(hpd)]
        upstream = [do_s[h, rows, :] for h in range(hpd)]
        lses = [lse_in[h, :, rows] for h in range(hpd)]
        deltas = [delta_s[h, :, rows] for h in range(hpd)]

        def key_step(kb, state):
            keys = pl.ds(pl.multiple_of(kb * block, block), block)
            k_pos = kb * block + down
            allowed = (k_pos <= q_pos) & (k_pos >= first)
            new = []
            for h in range(hpd):
                scores = mm_nt(k_in[h, keys, :], queries[h])
                weights = jnp.where(allowed, jnp.exp(scores - lses[h]), 0.0)
                dp = mm_nt(v_in[h, keys, :], upstream[h])
                ds = (weights * (dp - deltas[h])).astype(BF)
                dv_s[h, keys, :] += mm(weights.astype(BF), upstream[h])
                dk_s[h, keys, :] += mm(ds, queries[h])
                new.append(state[h] + mm(kt_in[h, :, keys], ds))
            return tuple(new)

        begin = tuple(jnp.zeros((HD, block), F32) for _ in range(hpd))
        state = lax.fori_loop(blocks[qb], qb + 1, key_step, begin)
        for h in range(hpd):
            dq_s[h, rows, :] = state[h].T * HD ** (-0.5)
        return carry

    lax.fori_loop(0, L // block, query_step, 0)

    def unrotate(step, carry):
        rows = pl.ds(pl.multiple_of(step * block, block), block)
        cosine, sine = cos[rows, :], signed(sin[rows, :])
        parts = [[], [], []]
        for h in range(hpd):
            dq = dq_s[h, rows, :]
            dk = dk_s[h, rows, :]
            parts[0].append((dq * cosine - halves_swapped(dq) * sine).astype(BF))
            parts[1].append((dk * cosine - halves_swapped(dk) * sine).astype(BF))
            parts[2].append(dv_s[h, rows, :].astype(BF))
        mixed_s[rows, :] = jnp.concatenate(parts[0] + parts[1] + parts[2], axis=-1)
        return carry

    lax.fori_loop(0, L // block, unrotate, 0)
    gw = mm_tn(normed[...], mixed_s[...])
    gw_s[...] = gw.astype(BF)
    high, low = split(gw * weight[...].astype(F32))
    ones = jnp.ones((16, 3 * hw), BF)
    total = ((mm_nt(ones, high) + mm_nt(ones, low)) / small[0:1, :]).astype(BF)
    for i in range(F):
        rows_s[i] = total[:, i * d_local : (i + 1) * d_local]
    for k in range(F):
        ff = lax.rem(f + k, F)
        at = pl.ds(pl.multiple_of(ff * d_local, d_local), d_local)
        payloads[k][:d_local, :] = gw_s[at, :]
        payloads[k][d_local:, :d_local] = rows_s[ff]
        if d_local < 3 * hw:
            payloads[k][d_local:, d_local:] = jnp.zeros((16, 3 * hw - d_local), BF)


def normed_grad_kernel(dims, mixed, weight, mine, theirs, turned):
    Z, R = dims
    core = place_of()[1]
    turned[...] = weight[...].T

    def chip_step(chip, carry):
        for side in range(2):
            at = 2 * chip + (core if side == 0 else 1 - core)
            rows = pl.ds(pl.multiple_of(at * R, R), R)
            (mine if side == 0 else theirs)[chip] = mm(mixed[rows, :], turned[...]).astype(BF)
        return carry

    lax.fori_loop(0, Z, chip_step, 0)


def pair_kernel(Z, mine, theirs, *outs):
    meta = place_of()
    for k in range(Z):
        chip = lax.rem(meta[0] + k, Z)
        outs[k][...] = (mine[chip].astype(F32) + theirs[chip].astype(F32)).astype(BF)


def last_kernel(dims, x, dh, small, *refs):
    meta = place_of()
    Z, S, R, _, G = dims
    dns, out, acc = refs[:Z], refs[Z], refs[Z + 1]
    acc[...] = jnp.zeros_like(acc)
    for k in range(Z):
        seq, _ = piece_at((Z, G), meta, k, 0)
        acc[seq] += dns[k][...].astype(F32)
    gain = small[0:1, :]
    for s in range(S):
        tile = x[s].astype(F32)
        factor = norm_of(tile)
        normal = tile * factor
        scaled = acc[s] * gain
        out[s] = dh[s * R : (s + 1) * R, :] + factor * (
            scaled - normal * jnp.mean(scaled * normal, axis=-1, keepdims=True)
        )


def place_kernel(dims, ks, left, *refs):
    meta = place_of()
    F, per, CW, width = dims
    n = len(ks)
    ours, theirs, refs = refs[:n], refs[n : 2 * n], refs[2 * n :]
    outs, (buf, sems) = refs[-5:-2], refs[-2:]
    copies = []
    for side in range(2):
        for j, k in enumerate(ks):
            dev = lax.rem(meta[2] - k + F, F)
            core = meta[1] if side == 0 else 1 - meta[1]
            e = lax.div(dev, per)
            lane = (lax.rem(dev, per) * 2 + core) * CW + left
            lanes = pl.ds(pl.multiple_of(lane, 128), width)
            for i in range(3):
                at = (side * n + j) * 3 + i
                buf[at] = (ours if side == 0 else theirs)[j][i].astype(F32)
                copy = pltpu.make_async_copy(buf.at[at], outs[i].at[:, e, lanes], sems.at[at])
                copy.start()
                copies.append(copy)
    for copy in copies:
        copy.wait()


def qkv_grad_kernel(dims, *refs):
    meta = place_of()
    G, D, d_local, hw, offsets = dims
    pieces, (out, gain_out, table) = refs[:-3], refs[-3:]
    group = lax.rem(meta[3], G)
    at = 0
    for piece in pieces:
        for j in range(piece.shape[0]):
            table[offsets[at]] = piece[j]
            at += 1
    gain = jnp.zeros((1, d_local), F32)
    for i in range(G):
        tile = table[jnp.bitwise_xor(group, i)].astype(F32)
        gain = gain + tile[d_local : d_local + 1, :d_local]
        width = max(0, min(hw, D - i * hw))
        if width:
            for part in range(3):
                out[:, part * D + i * hw : part * D + i * hw + width] = tile[
                    :d_local, part * hw : part * hw + width
                ]
    gain_out[...] = gain


def body(
    block_input,
    attn_gain,
    w_qkv,
    w_out,
    ffn_gain,
    w_router,
    w_gate,
    w_up,
    w_down,
    const_mix,
    const_vec,
    prev_logits,
    routes,
    doc_ids,
    d_out,
    *,
    F,
    C,
):
    S, R, D = block_input.shape
    L = doc_ids.shape[1]
    Z = C // 2
    G = C // S
    hpd = -(-H // G)
    hw = hpd * HD
    FF = w_gate.shape[2]
    per = F // NF
    CW = FF // (2 * per)
    d_local = D // F
    T = S * R
    block = min(512, L)
    shaped = jax.ShapeDtypeStruct
    f = lax.axis_index(FS)
    c = lax.axis_index(CT)
    core = c % 2
    z = c // 2

    def fs(t, k):
        return lax.ppermute(t, FS, [(i, (i + k) % F) for i in range(F)])

    def zs(t, k):
        return lax.ppermute(
            t, CT, [(2 * i + j, 2 * ((i + k) % Z) + j) for i in range(Z) for j in range(2)]
        )

    def cx(t):
        return lax.ppermute(t, CT, [(i, i ^ 1) for i in range(C)])

    def pick(t, index, axis=0):
        return lax.dynamic_index_in_dim(t, index, axis, keepdims=False)

    def seq_of(chip):
        return chip // (Z // S)

    def expert_of(dev):
        return lax.div(dev, per)

    def chunk_of(dev):
        return (dev % per) * 2 + core

    def call(kernel, name, out_shape, args, scratch=(), smem=0, **kw):
        return pl.pallas_call(
            kernel,
            out_shape=out_shape,
            in_specs=[SMEM] * smem + [VMEM] * (len(args) - smem),
            out_specs=tuple([VMEM] * len(out_shape)),
            scratch_shapes=list(scratch),
            compiler_params=params(name, L > 2048),
            **kw,
        )(*args)

    x_mine = [pick(block_input, seq_of(z))] + [
        zs(pick(block_input, seq_of((z + k) % Z)), k) for k in range(1, Z)
    ]
    x_theirs = [cx(t) for t in x_mine]

    my_docs = pick(doc_ids, c // G)
    start = jnp.sum((my_docs[None, :] < my_docs[:, None]).astype(jnp.int32), axis=1)
    first_block = start.reshape(L // block, block)[:, 0] // block
    route_rows = routes.transpose(0, 2, 1).reshape(S * TOP, R)
    prev = prev_logits.transpose(0, 2, 1)

    (first,) = call(
        functools.partial(pack_kernel, (F, D, G, hpd)),
        "pack",
        (shaped((d_local + 16, 3 * hw), BF),),
        (
            w_qkv,
            jnp.stack([attn_gain, ffn_gain]),
            w_router.T,
            const_mix.T,
            const_vec.T,
        ),
    )
    w_pieces = [first] + [fs(first, k) for k in range(1, F)]
    slot_rows, *g_outs = call(
        functools.partial(grad_rows_kernel, (F, S, R, D, expert_of)),
        "rows",
        (shaped((S * TOP, R), jnp.int32),) + (shaped((S * MOST, D), BF),) * F,
        (d_out, route_rows),
        [pltpu.VMEM((NF, S * MOST, D), BF)],
    )
    g_rows = [g_outs[0]] + [fs(g_outs[k], k) for k in range(1, F)]
    (g_mine,) = call(
        functools.partial(stack_kernel, S * MOST),
        "stack",
        (shaped((F * S * MOST, D), BF),),
        tuple(g_rows),
    )
    half = lax.dynamic_slice_in_dim(w_out, core * (D // 2), D // 2, 1)
    o_pieces = [half] + [fs(half, k) for k in range(1, F)]
    o_pieces = o_pieces + [cx(t) for t in o_pieces]

    def expert_slices():
        if per == 1:
            cut = [
                lax.dynamic_slice_in_dim(w, core * CW, CW, 2).transpose(1, 0, 2)
                for w in (w_gate, w_up, w_down)
            ]
            cut = lax.optimization_barrier(cut)
            return call(
                functools.partial(order_kernel, (F, CW // 2)),
                "order",
                (shaped((3, d_local, CW), BF),) * (F - 1) + (shaped((3, d_local, CW // 2), BF),),
                tuple(cut),
            )
        out = []
        for k in range(F):
            dev = (f + k) % F
            out.append(
                jnp.stack(
                    [
                        pick(
                            lax.dynamic_slice_in_dim(w, chunk_of(dev) * CW, CW, 2),
                            expert_of(dev),
                            1,
                        )
                        for w in (w_gate, w_up, w_down)
                    ]
                )
            )
        return out

    slices = expert_slices()
    if per == 1:
        e_pieces = [slices[0]]
        for k in range(1, F):
            e_pieces.append(lax.ppermute(slices[k], FS, [(i, i ^ k) for i in range(F)]))
        e_pieces.append(lax.ppermute(e_pieces[-1], CT, [(i, i ^ 2) for i in range(C)]))
    else:
        e_pieces = [slices[0]] + [fs(slices[k], k) for k in range(1, F)]

    frequency = jnp.exp(jnp.arange(HD // 2, dtype=F32) * (-2.0 * math.log(10000.0) / HD))
    frequency = jnp.concatenate([frequency, frequency])
    low = jnp.arange(32).astype(F32)[:, None] * frequency[None, :]
    high = (32 * jnp.arange(L // 32)).astype(F32)[:, None] * frequency[None, :]
    tables = (jnp.cos(low), jnp.sin(low), jnp.cos(high), jnp.sin(high))
    dims = (Z, F, R, D, L, hpd, block)
    normed, qkv_w, small, cosine, sine, q, k_, v, kt, ot, lse, *att_pieces = call(
        functools.partial(attend_kernel, dims),
        "attend",
        (
            shaped((L, D), BF),
            shaped((D, 3 * hw), BF),
            shaped((16, D), F32),
            shaped((L, HD), F32),
            shaped((L, HD), F32),
            shaped((hpd, L, HD), BF),
            shaped((hpd, L, HD), BF),
            shaped((hpd, L, HD), BF),
            shaped((hpd, HD, L), BF),
            shaped((hpd, HD, L), F32),
            shaped((hpd, 1, L), F32),
        )
        + (shaped((2, R, hw), BF),) * Z,
        (first_block, start[None], *tables, *x_mine, *x_theirs, *w_pieces),
        [
            pltpu.VMEM((F, 16, d_local), F32),
            pltpu.VMEM((hpd, HD, L), BF),
            pltpu.VMEM((C, R, hw), BF),
        ],
        smem=1,
    )

    g_planes = [g_mine] + [zs(g_mine, k) for k in range(1, Z) if k < 2 or k == Z - 1]
    for k in range(2, Z - 1):
        g_planes.insert(k, zs(g_planes[k - 1], 1))
    g_planes = [(t, cx(t)) for t in g_planes]

    pieces = [att_pieces[0]] + [zs(att_pieces[k], k) for k in range(1, Z)]
    atts = pieces + [cx(t[1]) for t in pieces]
    outs = call(
        functools.partial(dispatch_kernel, (Z, F, S, R, D, G, hw, expert_of)),
        "disp",
        (shaped((T, D), F32), shaped((G * hw, D), BF))
        + (shaped((S * MOST, D + 128), BF),) * F,
        (block_input, small, prev, route_rows, slot_rows, *atts, *o_pieces),
        [pltpu.VMEM((NF, S * MOST, D + 128), BF)],
    )
    hidden, out_w, toks = outs[0], outs[1], outs[2:]
    own = [toks[0]] + [fs(toks[k], k) for k in range(1, F)]
    (own,) = call(
        functools.partial(stack_kernel, S * MOST),
        "stack",
        (shaped((F * S * MOST, D + 128), BF),),
        tuple(own),
    )
    n = own.shape[0]

    steps = 4 if CW % 512 == 0 else 2
    cut = CW // steps
    e_spec = pl.BlockSpec((3, d_local, cut), lambda i: (0, 0, i))
    e_specs = [e_spec] * F
    if len(e_pieces) > F:
        e_specs = [e_spec] * (F - 1) + [pl.BlockSpec((3, d_local, CW // 2), lambda i: (0, 0, 0))] * 2
    act_spec = pl.BlockSpec((2 * n, cut), lambda i: (0, i))
    both_spec = pl.BlockSpec((D, 2 * n), lambda i: (0, 0))

    def ffn(at, rows, theirs, g_rows):
        own_plane = at == 0
        shapes = (shaped((2 * n, CW), BF),) * 3 + (shaped((D, 2 * n), BF),) * 2
        specs = (act_spec,) * 3 + (both_spec,) * 2
        scratch = [pltpu.VMEM((2 * n, D), BF), pltpu.VMEM((2 * n, D), BF)]
        w_spec = pl.BlockSpec((3, D, cut), lambda i: (0, 0, i))
        if own_plane:
            shapes += (shaped((2, n, D), F32), shaped((2, n, D), BF), shaped((3, D, CW), BF))
            specs += (pl.BlockSpec((2, n, D), lambda i: (0, 0, 0)),) * 2 + (w_spec,)
            scratch.append(pltpu.VMEM((2, 2 * n, D), F32))
        row_spec = pl.BlockSpec((n, D + 128), lambda i: (0, 0))
        g_spec = pl.BlockSpec((n, D), lambda i: (0, 0))
        return pl.pallas_call(
            functools.partial(ffn_kernel, (F, D, len(e_pieces)), own_plane),
            out_shape=shapes,
            grid=(steps,),
            in_specs=[row_spec, row_spec, g_spec, g_spec]
            + (e_specs if own_plane else [w_spec]),
            out_specs=specs,
            scratch_shapes=scratch,
            compiler_params=params("ex" if at else "ex0", L > 2048),
        )(rows, theirs, *g_rows, *(e_pieces if own_plane else [weights]))

    *plane, back_mine, back_theirs, weights = ffn(0, own, cx(own), g_planes[0])
    planes = [plane]
    back = (back_mine + cx(back_theirs).astype(F32)).astype(BF).reshape(2, F, S * MOST, D)
    rets = [back[:, 0]] + [fs(back[:, k], -k) for k in range(1, F)]
    ring = [own]
    for _ in range(1, Z):
        ring.append(zs(ring[-1], 1))

    def far(k, after):
        rows, g_rows, _ = lax.optimization_barrier((ring[k], g_planes[k], after))
        planes.append(ffn(k, rows, cx(rows), g_rows))

    far(1, back_mine)
    outs = call(
        functools.partial(combine_kernel, (Z, F, S, R, D, G, hw, per, expert_of)),
        "combine",
        (shaped((S, R, D), BF), shaped((T, D), F32), shaped((S, NE, R), F32))
        + (shaped((2, R, hw), BF),) * Z
        + (shaped((d_local + 16, D), BF),) * F,
        (hidden, d_out, small, prev, route_rows, slot_rows, *rets, *atts, out_w),
        [
            pltpu.VMEM((F, 2, S * MOST, D), BF),
            pltpu.VMEM((G * hw, D), F32),
            pltpu.VMEM((T, D), BF),
            pltpu.VMEM((F, 16, d_local), BF),
        ],
    )
    out_block, hidden_grad, prev_grad = outs[:3]
    das, o_payloads = outs[3 : 3 + Z], outs[3 + Z :]
    grad_prev = prev_grad.transpose(0, 2, 1)

    do_pieces = [das[0]] + [zs(das[k], -k) for k in range(1, Z)]
    dos = do_pieces + [cx(t[1]) for t in do_pieces]

    if Z > 2:
        far(2, hidden_grad)
    dos[0], *_ = lax.optimization_barrier((dos[0], planes[-1][0]))
    outs = call(
        functools.partial(back_kernel, dims),
        "back",
        (shaped((d_local + 16, 3 * hw), BF),) * F + (shaped((L, 3 * hw), BF),),
        (
            first_block,
            start[None],
            cosine,
            sine,
            small,
            *dos,
            normed,
            qkv_w,
            q,
            k_,
            v,
            kt,
            ot,
            lse,
        ),
        [
            pltpu.VMEM((hpd, L, HD), BF),
            pltpu.VMEM((hpd, 1, L), F32),
            pltpu.VMEM((hpd, L, HD), F32),
            pltpu.VMEM((hpd, L, HD), F32),
            pltpu.VMEM((hpd, L, HD), F32),
            pltpu.VMEM((D, 3 * hw), BF),
            pltpu.VMEM((F, 16, d_local), BF),
        ],
        smem=1,
    )
    q_payloads, mixed_grad = outs[:F], outs[F]
    for k in range(3, Z):
        far(k, mixed_grad)
    flat = [t for plane in planes for t in plane]
    flat[0], _ = lax.optimization_barrier((flat[0], mixed_grad))
    wide = 256
    widths = [wide, CW - 2 * wide, wide] if CW > 2 * wide else [wide, wide]
    e_grads = []
    for part, width in enumerate(widths):
        left = sum(widths[:part])
        if Z > 4:
            lanes = slice(left, left + width)
            trio = [
                sum(mm(plane[a], plane[b][:, lanes]) for plane in planes).astype(BF)
                for a, b in ((3, 1), (3, 2), (4, 0))
            ]
            trio = jnp.stack(trio).reshape(3, F, d_local, width)
            e_grads.append([pick(trio, (f + k) % F, 1) for k in range(F)])
            continue
        acts = pl.BlockSpec((2 * n, wide), lambda i, b=left // wide: (0, b + i))
        e_grads.append(
            pl.pallas_call(
                functools.partial(weight_kernel, (F, D, Z)),
                out_shape=(shaped((3, d_local, width), BF),) * F,
                grid=(width // wide,),
                in_specs=[acts, acts, acts, both_spec, both_spec] * Z,
                out_specs=(pl.BlockSpec((3, d_local, wide), lambda i: (0, 0, i)),) * F,
                scratch_shapes=[pltpu.VMEM((3, D, wide), BF)],
                compiler_params=params("wg", L > 2048),
            )(*flat)
        )
    dn_mine, dn_theirs = call(
        functools.partial(normed_grad_kernel, (Z, R)),
        "ng",
        (shaped((Z, R, D), BF),) * 2,
        (mixed_grad, qkv_w),
        [pltpu.VMEM((3 * hw, D), BF)],
    )
    dns = call(
        functools.partial(pair_kernel, Z),
        "pair",
        (shaped((R, D), BF),) * Z,
        (dn_mine, cx(dn_theirs)),
    )
    dns = [dns[0]] + [zs(dns[k], k) for k in range(1, Z)]
    (grad_x,) = call(
        functools.partial(last_kernel, (Z, S, R, D, G)),
        "ig",
        (shaped((S, R, D), F32),),
        (block_input, hidden_grad, small, *dns),
        [pltpu.VMEM((S, R, D), F32)],
    )

    def moved_rows(parts):
        return [parts[0]] + [fs(parts[k], k) for k in range(1, F)]

    def summed_rows(parts):
        return sum(p.astype(F32) for p in parts).astype(BF)

    def over_ctx(t):
        step = 1
        while step < C:
            moved = lax.ppermute(t, CT, [(i, i ^ step) for i in range(C)])
            t = (t.astype(F32) + moved.astype(F32)).astype(BF)
            step *= 2
        return t

    payload = summed_rows(moved_rows(q_payloads))
    summed = payload.astype(F32)
    for j in range(1, S):
        moved = lax.ppermute(payload, CT, [(i, (i + j * G) % C) for i in range(C)])
        summed = summed + moved.astype(F32)
    payload = summed.astype(BF)[None]
    gathered, offsets = [payload], (0,)
    step = G // 2
    while step:
        gathered.append(lax.ppermute(payload, CT, [(i, i ^ step) for i in range(C)]))
        offsets += tuple(i ^ step for i in offsets)
        step //= 2
        if step:
            payload = jnp.concatenate([payload, gathered[-1]], axis=0)
    grad_qkv, grad_gain_one = call(
        functools.partial(qkv_grad_kernel, (G, D, d_local, hw, offsets)),
        "qg",
        (shaped((d_local, 3 * D), F32), shaped((1, d_local), F32)),
        tuple(gathered),
        [pltpu.VMEM((G, d_local + 16, 3 * hw), BF)],
    )
    grad_gain_one = grad_gain_one[0]

    moved = moved_rows(o_payloads)
    payload = over_ctx(summed_rows(moved)).astype(F32)
    grad_w_out = payload[:d_local]
    smalls = payload[d_local:, :d_local]

    ANY = pl.BlockSpec(memory_space=pl.ANY)
    placed = ()
    for part, width in enumerate(widths):
        ours = [e_grads[part][0]] + [fs(e_grads[part][k], k) for k in range(1, F)]
        theirs = [cx(t) for t in ours]
        groups = [list(range(F))]
        for ks in groups:
            args = (*[ours[k] for k in ks], *[theirs[k] for k in ks], *placed)
            at = 2 * len(ks)
            placed = pl.pallas_call(
                functools.partial(
                    place_kernel, (F, per, CW, width), ks, sum(widths[:part])
                ),
                out_shape=(shaped((d_local, NF, FF), F32),) * 3,
                in_specs=[VMEM] * (2 * len(ks)) + [ANY] * len(placed),
                out_specs=(ANY,) * 3,
                input_output_aliases={at + i: i for i in range(len(placed))},
                scratch_shapes=[
                    pltpu.VMEM((6 * len(ks), d_local, width), F32),
                    pltpu.SemaphoreType.DMA((6 * len(ks),)),
                ],
                compiler_params=params("place", L > 2048),
            )(*args)
    grad_gate, grad_up, grad_down = placed
    return (
        out_block,
        grad_x,
        grad_prev,
        grad_gain_one,
        grad_qkv,
        grad_w_out,
        smalls[1],
        smalls[2:10].T,
        grad_gate,
        grad_up,
        grad_down,
        smalls[10:14].T,
        smalls[14:16].T,
    )


def solution(mesh):
    F, Z = mesh.shape[FS], mesh.shape[CT] // 2

    def layer(*args):
        return body(*args, F=F, C=2 * Z)

    return jax.shard_map(
        layer,
        mesh=mesh,
        in_specs=(
            P(FS, CT, None),
            P(FS),
            P(FS, None),
            P(FS, None),
            P(FS),
            P(FS, None),
            P(FS, None, None),
            P(FS, None, None),
            P(FS, None, None),
            P(FS, None),
            P(FS, None),
            P(FS, CT, None),
            P(FS, CT, None),
            P(FS, None),
            P(FS, CT, None),
        ),
        out_specs=(
            P(FS, CT, None),
            P(FS, CT, None),
            P(FS, CT, None),
            P(FS),
            P(FS, None),
            P(FS, None),
            P(FS),
            P(FS, None),
            P(FS, None, None),
            P(FS, None, None),
            P(FS, None, None),
            P(FS, None),
            P(FS, None),
        ),
        check_vma=False,
    )
```

```python
import functools
import math

import jax
import jax.numpy as jnp
from jax import lax
from jax.experimental import pallas as pl
from jax.experimental.pallas import tpu as pltpu
from jax.sharding import PartitionSpec as P


H = 12
HD = 64
NF = 4
NC = 2
NE = 8
TOP = 2
MOST = 48
FS, CT = "fsdp", "ctx"
BF = jnp.bfloat16
F32 = jnp.float32


def dot(a, b, dims):
    return lax.dot_general(a, b, (dims, ((), ())), preferred_element_type=F32)


def mm(a, b):
    return dot(a, b, ((1,), (0,)))


def mm_nt(a, b):
    return dot(a, b, ((1,), (1,)))


def mm_tn(a, b):
    return dot(a, b, ((0,), (0,)))


def halves_swapped(t):
    half = t.shape[-1] // 2
    return jnp.concatenate([t[:, half:], t[:, :half]], axis=-1)


VMEM = pl.BlockSpec(memory_space=pltpu.VMEM)
SMEM = pl.BlockSpec(memory_space=pltpu.SMEM)


GRANTS = {
    "pack": 3,
    "rows": 3,
    "stack": 2,
    "order": 4,
    "attend": 10,
    "disp": 4,
    "ex0": 20,
    "ex": 11,
    "combine": 12,
    "wg": 14,
    "back": 16,
    "ng": 3,
    "pair": 2,
    "ig": 4,
    "place": 18,
    "qg": 4,
}


def params(name, long=False):
    return pltpu.CompilerParams(vmem_limit_bytes=(56 if long else GRANTS[name]) << 20)


def place_of():
    c = lax.axis_index(CT)
    return lax.div(c, 2), lax.rem(c, 2), lax.axis_index(FS), c


def norm_of(tile):
    return lax.rsqrt(jnp.mean(tile * tile, axis=-1, keepdims=True) + 1e-05)


def split(t):
    high = t.astype(BF)
    return high, (t - high.astype(F32)).astype(BF)


def pack_kernel(dims, w_qkv, gains, router, mix, vec, first):
    meta = place_of()
    F, D, G, hpd = dims
    hw = hpd * HD
    d_local = D // F
    group = lax.rem(meta[3], G)
    for g in range(G):
        width = max(0, min(hw, H * HD - g * hw))

        @pl.when(group == g)
        def _():
            for part in range(3):
                if width:
                    first[:d_local, part * hw : part * hw + width] = w_qkv[
                        :, part * H * HD + g * hw : part * H * HD + g * hw + width
                    ]
                if width < hw:
                    first[:d_local, part * hw + width : (part + 1) * hw] = jnp.zeros(
                        (d_local, hw - width), BF
                    )

    rows = [t[...].astype(F32) for t in (gains, router, mix, vec)]
    first[d_local:, :d_local] = jnp.concatenate(rows, axis=0).astype(BF)
    if d_local < 3 * hw:
        first[d_local:, d_local:] = jnp.zeros((16, 3 * hw - d_local), BF)


def grad_rows_kernel(dims, grad, routes, slots, *outs):
    meta = place_of()
    F, S, R, _, expert_of = dims
    table = outs[-1]
    below = lax.broadcasted_iota(jnp.int32, (R, R), 0)
    earlier = (below < lax.broadcasted_iota(jnp.int32, (R, R), 1)).astype(F32).astype(BF)
    expert = lax.broadcasted_iota(jnp.int32, (8, R), 0)
    for s in range(S):
        named = [routes[2 * s + w : 2 * s + w + 1, :] for w in range(TOP)]
        hots = [(expert == t).astype(F32) for t in named]
        counts = mm((hots[0] + hots[1]).astype(BF), earlier)
        lines = []
        for w in range(TOP):
            rank = jnp.sum(hots[w] * counts, axis=0, keepdims=True).astype(jnp.int32)
            line = jnp.where(named[w] < NF, named[w] * MOST + rank, -1)
            slots[2 * s + w : 2 * s + w + 1, :] = line
            lines.append(line)
        slot = lax.broadcasted_iota(jnp.int32, (NF * MOST, R), 0)
        picks = (slot == lines[0]) | (slot == lines[1])
        moved = mm(picks.astype(F32).astype(BF), grad[s]).astype(BF)
        for e in range(NF):
            table[e, s * MOST : (s + 1) * MOST, :] = moved[e * MOST : (e + 1) * MOST, :]
    for k in range(F):
        outs[k][...] = table[expert_of(lax.rem(meta[2] + k, F))]


def stack_kernel(n, *refs):
    out = refs[-1]
    for i, ref in enumerate(refs[:-1]):
        out[i * n : (i + 1) * n, :] = ref[:n, :]


def order_kernel(dims, *refs):
    F, half = dims
    z, _, f, _ = place_of()
    lanes = pl.ds(pl.multiple_of(lax.rem(z, 2) * half, 128), half)
    for k in range(F):
        e = jnp.bitwise_xor(f, k)
        for i in range(3):
            refs[3 + k][i] = refs[i][e] if k < F - 1 else refs[i][e, :, lanes]


def turn_tables(cos_low, sin_low, cos_high, sin_high, cosine, sine, L):
    low = cos_low.shape[0]
    for step in range(L // low):
        a, b = cos_high[step : step + 1, :], sin_high[step : step + 1, :]
        at = slice(step * low, (step + 1) * low)
        cosine[at, :] = a * cos_low[...] - b * sin_low[...]
        sine[at, :] = b * cos_low[...] + a * sin_low[...]


def signed(sine):
    lane = lax.broadcasted_iota(jnp.int32, sine.shape, 1)
    return jnp.where(lane < HD // 2, -sine, sine)


def attend_kernel(dims, blocks, start, cos_low, sin_low, cos_high, sin_high, *refs):
    Z, F, R, D, L, hpd, block = dims
    hw = hpd * HD
    xs, refs = refs[: 2 * Z], refs[2 * Z :]
    ws, refs = refs[:F], refs[F:]
    normed, weight, small_out, cos, sin, q_out, k_out, v_out, kt_out, ot_out, lse_out = refs[:11]
    refs = refs[11:]
    pieces, (small_s, vt_s, att_s) = refs[:Z], refs[Z:]
    z, core, f, _ = place_of()
    d_local = D // F
    top = ws[0].shape[0] - d_local - 16
    turn_tables(cos_low, sin_low, cos_high, sin_high, cos, sin, L)
    for k in range(F):
        row = pl.multiple_of(lax.rem(f - k + F, F) * d_local, d_local)
        weight[pl.ds(row, d_local), :] = ws[k][top : top + d_local, : 3 * hw]
        small_s[k] = ws[k][top + d_local :, :d_local].astype(F32)
    small = jnp.concatenate([small_s[lax.rem(f - i + F, F)] for i in range(F)], axis=1)
    small_out[...] = small
    gain_row = small[0:1, :]
    for k in range(Z):
        for side in range(2):
            at = lax.rem(z - k + Z, Z) * 2 + (core if side == 0 else 1 - core)
            tile = xs[side * Z + k][...].astype(F32)
            row = pl.multiple_of(at * R, R)
            normed[pl.ds(row, R), :] = (tile * norm_of(tile) * gain_row).astype(BF)

    def project(step, carry):
        rows = pl.ds(pl.multiple_of(step * block, block), block)
        mixed = mm(normed[rows, :], weight[...])
        cosine, sine = cos[rows, :], signed(sin[rows, :])
        for h in range(hpd):
            q = mixed[:, h * HD : (h + 1) * HD]
            k = mixed[:, hw + h * HD : hw + (h + 1) * HD]
            v = mixed[:, 2 * hw + h * HD : 2 * hw + (h + 1) * HD]
            q = (q * cosine + halves_swapped(q) * sine).astype(BF)
            q_out[h, rows, :] = (q.astype(F32) * HD ** (-0.5)).astype(BF)
            k = k * cosine + halves_swapped(k) * sine
            k_out[h, rows, :] = k.astype(BF)
            kt_out[h, :, rows] = k.T.astype(BF)
            v_out[h, rows, :] = v.astype(BF)
            vt_s[h, :, rows] = v.T.astype(BF)
        return carry

    lax.fori_loop(0, L // block, project, 0)

    def query_step(qb, carry):
        rows = pl.ds(pl.multiple_of(qb * block, block), block)
        first = start[:, rows]
        q_pos = qb * block + lax.broadcasted_iota(jnp.int32, (block, block), 1)
        down = lax.broadcasted_iota(jnp.int32, (block, block), 0)
        queries = [q_out[h, rows, :] for h in range(hpd)]

        def key_step(kb, state):
            keys = pl.ds(pl.multiple_of(kb * block, block), block)
            k_pos = kb * block + down
            allowed = (k_pos <= q_pos) & (k_pos >= first)
            new = []
            for h in range(hpd):
                high, total, acc = state[h]
                scores = mm_nt(k_out[h, keys, :], queries[h])
                scores = jnp.where(allowed, scores, -1e30)
                top = jnp.maximum(high, jnp.max(scores, axis=0, keepdims=True))
                scale = jnp.exp(high - top)
                weights = jnp.where(allowed, jnp.exp(scores - top), 0.0)
                total = total * scale + jnp.sum(weights, axis=0, keepdims=True)
                acc = acc * scale + mm(vt_s[h, :, keys], weights.astype(BF))
                new.append((top, total, acc))
            return tuple(new)

        begin = tuple(
            (
                jnp.full((1, block), -1e30, F32),
                jnp.zeros((1, block), F32),
                jnp.zeros((HD, block), F32),
            )
            for _ in range(hpd)
        )
        state = lax.fori_loop(blocks[qb], qb + 1, key_step, begin)
        outs = []
        for h in range(hpd):
            high, total, acc = state[h]
            out = acc / total
            ot_out[h, :, rows] = out
            lse_out[h, :, rows] = high + jnp.log(total)
            outs.append(out)
        whole = jnp.concatenate(outs, axis=0).T.astype(BF)
        for part in range(block // R):
            att_s[qb * (block // R) + part] = whole[part * R : (part + 1) * R, :]
        return carry

    lax.fori_loop(0, L // block, query_step, 0)
    for k in range(Z):
        chip = lax.rem(z + k, Z) * 2
        pieces[k][0] = att_s[chip + core]
        pieces[k][1] = att_s[chip + 1 - core]


def piece_at(dims, meta, k, side):
    Z, G = dims
    chip = lax.rem(meta[0] - k + Z, Z)
    group = lax.rem(2 * chip + (meta[1] if side == 0 else 1 - meta[1]), G)
    return lax.div(2 * chip, G), group


def columns_of(prev, routes, s):
    width = prev.shape[2]
    gap = jnp.zeros((2, width), F32)
    tall = jnp.concatenate([gap, prev[s], jnp.zeros((6, width), F32)], axis=0)
    named = routes[2 * s : 2 * s + 2, :].astype(F32)
    named = jnp.concatenate([named, jnp.zeros((6, width), F32)], axis=0)
    return tall.T, named.T.astype(jnp.int32)


def router_parts(logits, prev, routes):
    lane = lax.broadcasted_iota(jnp.int32, logits.shape, 1)
    inside = (lane >= 2) & (lane < 2 + NE)
    shown = jnp.where(inside, logits + prev, -1e30)
    weights = jnp.exp(shown - jnp.max(shown, axis=-1, keepdims=True))
    weights = jnp.where(inside, weights, 0.0)
    router = weights / jnp.sum(weights, axis=-1, keepdims=True)
    hots = [lane == routes[:, w : w + 1] + 2 for w in range(TOP)]
    gates = [jnp.sum(jnp.where(hot, router, 0.0), axis=-1, keepdims=True) for hot in hots]
    return lane, router, hots, gates


def dispatch_kernel(dims, x, small, prev, routes, slots, *refs):
    meta = place_of()
    Z, F, S, R, D, G, hw, expert_of = dims
    atts, refs = refs[: 2 * Z], refs[2 * Z :]
    ws, refs = refs[: 2 * F], refs[2 * F :]
    hidden, w_full, toks, table = refs[0], refs[1], refs[2:-1], refs[-1]

    def att(k, side):
        return atts[k][0] if side == 0 else atts[Z + k][...]

    f = meta[2]
    d_local = D // F
    if G * hw > D:
        w_full[D:, :] = jnp.zeros((G * hw - D, D), BF)
    for k in range(F):
        row = pl.multiple_of(lax.rem(f - k + F, F) * d_local, d_local)
        for side in range(2):
            half = meta[1] if side == 0 else 1 - meta[1]
            lanes = pl.ds(pl.multiple_of(half * (D // 2), 128), D // 2)
            w_full[pl.ds(row, d_local), lanes] = ws[side * F + k][...]
    for s in range(S):
        hidden[s * R : (s + 1) * R, :] = x[s].astype(F32)
    for k in range(Z):
        for side in range(2):
            seq, group = piece_at((Z, G), meta, k, side)
            rows = pl.ds(pl.multiple_of(seq * R, R), R)
            heads = pl.ds(pl.multiple_of(group * hw, hw), hw)
            hidden[rows, :] += mm(att(k, side), w_full[heads, :])
    gain = small[1:2, :]
    small_low = small[...].astype(BF)
    for s in range(S):
        at = slice(s * R, (s + 1) * R)
        tile = hidden[at, :]
        unit_low = (tile * norm_of(tile) * gain).astype(BF)
        logits = mm_nt(unit_low, small_low)
        _, _, _, gates = router_parts(logits, *columns_of(prev, routes, s))
        slot = lax.broadcasted_iota(jnp.int32, (NF * MOST, R), 0)
        picks = [
            (slot == slots[2 * s + w : 2 * s + w + 1, :]).astype(F32).astype(BF)
            for w in range(TOP)
        ]
        packed = mm(picks[0] + picks[1], unit_low).astype(BF)
        wide = lax.broadcasted_iota(jnp.int32, (R, 128), 1)
        columns = jnp.zeros((NF * MOST, 128), F32)
        for w in range(TOP):
            high, low = split(gates[w])
            both = jnp.where(
                wide == 0, high.astype(F32), jnp.where(wide == 1, low.astype(F32), 0.0)
            )
            columns = columns + mm(picks[w], both.astype(BF))
        for e in range(NF):
            to = slice(s * MOST, (s + 1) * MOST)
            table[e, to, :D] = packed[e * MOST : (e + 1) * MOST, :]
            table[e, to, D:] = columns[e * MOST : (e + 1) * MOST, :].astype(BF)
    for k in range(F):
        toks[k][...] = table[expert_of(lax.rem(f + k, F))]


def ffn_kernel(dims, own, rows_a, rows_b, g_a, g_b, *refs):
    meta = place_of()
    F, D, n_weights = dims
    n = rows_a.shape[0]
    ws, refs = (refs[:n_weights], refs[n_weights:]) if own else ((), refs)
    if not own:
        w_s, refs = refs[0], refs[1:]
    (inner_out, gate_out, up_out, xt_out, drt_out), refs = refs[:5], refs[5:]
    if own:
        mine_out, theirs_out, w_s, x_s, dr_s, acc = refs
    else:
        x_s, dr_s = refs
    step = pl.program_id(0)
    d_local = D // F

    @pl.when(step == 0)
    def _():
        for i, (rows, g) in enumerate(((rows_a, g_a), (rows_b, g_b))):
            at = slice(i * n, (i + 1) * n)
            x_s[at, :] = rows[:, :D]
            xt_out[:, at] = rows[:, :D].T
            gate = rows[:, D : D + 1].astype(F32) + rows[:, D + 1 : D + 2].astype(F32)
            dr = (gate * g[...].astype(F32)).astype(BF)
            dr_s[at, :] = dr
            drt_out[:, at] = dr.T

    def weight_rows(dev):
        return pl.ds(pl.multiple_of(dev * d_local, d_local), d_local)

    for k, piece in enumerate(ws[:F] if len(ws) == F else ws[: F - 1]):
        dev = lax.rem(meta[2] - k + F, F) if len(ws) == F else jnp.bitwise_xor(meta[2], k)
        for i in range(3):
            w_s[i, weight_rows(dev), :] = piece[i]
    if len(ws) > F:
        at = weight_rows(jnp.bitwise_xor(meta[2], F - 1))
        cut = w_s.shape[2]
        each = ws[F].shape[2] // cut
        lanes = pl.ds(pl.multiple_of(lax.rem(step, each) * cut, 128), cut)
        for side in range(2):

            @pl.when(lax.div(step, each) == lax.rem(meta[0] + side, 2))
            def _():
                for i in range(3):
                    w_s[i, at, :] = ws[F - 1 + side][i, :, lanes]

    piece = n // 2
    for r in range(4):
        rows = slice(r * piece, (r + 1) * piece)
        gate_act = mm(x_s[rows, :], w_s[0])
        up_act = mm(x_s[rows, :], w_s[1])
        inner_grad = mm(dr_s[rows, :], w_s[2])
        sig = 0.5 * jnp.tanh(0.5 * gate_act) + 0.5
        act = gate_act * sig
        inner_out[rows, :] = (act * up_act).astype(BF)
        gate_out[rows, :] = (inner_grad * up_act * (sig + act * (1.0 - sig))).astype(BF)
        up_out[rows, :] = (inner_grad * act).astype(BF)
    if own:
        result = mm_nt(inner_out[...], w_s[2])
        packed = mm_nt(gate_out[...], w_s[0]) + mm_nt(up_out[...], w_s[1])

        @pl.when(step == 0)
        def _():
            acc[0] = result
            acc[1] = packed

        @pl.when(step > 0)
        def _():
            acc[0] += result
            acc[1] += packed

        @pl.when(step == pl.num_programs(0) - 1)
        def _():
            mine_out[...] = acc[:, :n, :]
            theirs_out[...] = acc[:, n:, :].astype(BF)


def weight_kernel(dims, *refs):
    meta = place_of()
    F, D, Z = dims
    planes, refs = [refs[5 * p : 5 * p + 5] for p in range(Z)], refs[5 * Z :]
    outs, (acc,) = refs[:F], refs[F:]
    d_local = D // F
    for i, (left, right) in enumerate(((3, 1), (3, 2), (4, 0))):
        total = mm(planes[0][left][...], planes[0][right][...])
        for p in range(1, Z):
            total = total + mm(planes[p][left][...], planes[p][right][...])
        acc[i] = total.astype(BF)
    for k in range(F):
        at = pl.ds(pl.multiple_of(lax.rem(meta[2] + k, F) * d_local, d_local), d_local)
        for i in range(3):
            outs[k][i] = acc[i, at, :]


def combine_kernel(dims, hidden, grad, small, prev, routes, slots, *refs):
    meta = place_of()
    Z, F, S, R, D, G, hw, per, _ = dims
    rets, refs = refs[:F], refs[F:]
    atts, refs = refs[: 2 * Z], refs[2 * Z :]
    w_full, refs = refs[0], refs[1:]
    out_block, dh_out, prev_out, refs = refs[0], refs[1], refs[2], refs[3:]
    das, refs = refs[:Z], refs[Z:]
    payloads, refs = refs[:F], refs[F:]
    back_s, gw_s, dproj_s, rows_s = refs

    def att(k, side):
        return atts[k][0] if side == 0 else atts[Z + k][...]

    f = meta[2]
    d_local = D // F
    for k in range(F):
        back_s[lax.rem(f + k, F)] = rets[k][...]
    gain = small[1:2, :]
    small_all = small[...]
    small_low = small_all.astype(BF)
    small_grads = jnp.zeros((16, D), F32)
    gain_grad = jnp.zeros((1, D), F32)
    for s in range(S):
        at = slice(s * R, (s + 1) * R)
        tile = hidden[at, :]
        factor = norm_of(tile)
        normal = tile * factor
        unit = normal * gain
        unit_low = unit.astype(BF)
        logits = mm_nt(unit_low, small_low)
        before, route = columns_of(prev, routes, s)
        lane, router, hots, gates = router_parts(logits, before, route)
        g_low = grad[s]
        g = g_low.astype(F32)

        def column(t, index):
            return jnp.sum(jnp.where(lane == index, t, 0.0), axis=-1, keepdims=True)

        shares = []
        for i in range(NC):
            a, b = column(logits, 10 + 2 * i), column(logits, 11 + 2 * i)
            top = jnp.maximum(a, b)
            ea, eb = jnp.exp(a - top), jnp.exp(b - top)
            shares.append((ea / (ea + eb), eb / (ea + eb)))
        back = []
        for part in range(2):
            experts = []
            for e in range(NF):
                to = slice(s * MOST, (s + 1) * MOST)
                total = back_s[e * per, part, to, :]
                for j in range(1, per):
                    total = total.astype(F32) + back_s[e * per + j, part, to, :].astype(F32)
                experts.append(total.astype(BF))
            back.append(jnp.concatenate(experts, axis=0))
        slot = lax.broadcasted_iota(jnp.int32, (NF * MOST, R), 0)
        picks = [
            (slot == slots[2 * s + w : 2 * s + w + 1, :]).astype(F32).astype(BF)
            for w in range(TOP)
        ]
        values = [mm_tn(picks[w], back[0]) for w in range(TOP)]
        unit_grad = mm_tn(picks[0] + picks[1], back[1])
        ug = jnp.sum(unit * g, axis=-1, keepdims=True)
        vg_all = mm_nt(g_low, small_low)
        vg = [column(vg_all, 14 + i) for i in range(NC)]

        def named(w, e):
            return (route[:, w : w + 1] == e).astype(F32)

        gate_grads = []
        coef_unit = jnp.zeros((R, 1), F32)
        for w in range(TOP):
            total = jnp.sum(g * values[w], axis=-1, keepdims=True) + named(w, NF + 1) * ug
            coef_unit = coef_unit + gates[w] * named(w, NF + 1)
            for i in range(NC):
                here = named(w, NF + 2 + i)
                total = total + here * (shares[i][0] * ug + shares[i][1] * vg[i])
                coef_unit = coef_unit + gates[w] * here * shares[i][0]
            gate_grads.append(total)
        mixture = gates[0] * values[0] + gates[1] * values[1] + coef_unit * unit
        prob_grad = sum(jnp.where(hots[w], gate_grads[w], 0.0) for w in range(TOP))
        prev_grad = router * (prob_grad - jnp.sum(router * prob_grad, axis=-1, keepdims=True))
        prev_out[s] = prev_grad.T[2 : 2 + NE, :]
        left = prev_grad
        right = jnp.zeros_like(prev_grad)
        for i in range(NC):
            amount = sum(gates[w] * named(w, NF + 2 + i) for w in range(TOP))
            s0, s1 = shares[i]
            mixture = mixture + amount * s1 * small_all[14 + i : 15 + i, :]
            d0, d1 = amount * ug, amount * vg[i]
            inner = s0 * d0 + s1 * d1
            left = left + jnp.where(lane == 10 + 2 * i, s0 * (d0 - inner), 0.0)
            left = left + jnp.where(lane == 11 + 2 * i, s1 * (d1 - inner), 0.0)
            right = right + jnp.where(lane == 14 + i, amount * s1, 0.0)
        out_block[s] = (tile + mixture).astype(BF)
        left_high, left_low = split(left)
        right_high, right_low = split(right)
        unit_grad = unit_grad + mm(left_high, small_low) + mm(left_low, small_low)
        unit_grad = unit_grad + coef_unit * g
        small_grads = small_grads + mm_tn(left_high, unit_low) + mm_tn(left_low, unit_low)
        small_grads = small_grads + mm_tn(right_high, g_low) + mm_tn(right_low, g_low)
        gain_grad = gain_grad + jnp.sum(unit_grad * normal, axis=0, keepdims=True)
        scaled = unit_grad * gain
        dh = g + factor * (scaled - normal * jnp.mean(scaled * normal, axis=-1, keepdims=True))
        dh_out[at, :] = dh
        dproj_s[at, :] = dh.astype(BF)
    row = lax.broadcasted_iota(jnp.int32, (16, D), 0)
    small_grads = jnp.where(row == 1, gain_grad, small_grads).astype(BF)
    for i in range(F):
        rows_s[i] = small_grads[:, i * d_local : (i + 1) * d_local]
    gw_s[...] = jnp.zeros_like(gw_s)
    for k in range(Z):
        for side in range(2):
            seq, group = piece_at((Z, G), meta, k, side)
            dproj = dproj_s[pl.ds(pl.multiple_of(seq * R, R), R), :]
            heads = pl.ds(pl.multiple_of(group * hw, hw), hw)
            das[k][side] = mm_nt(dproj, w_full[heads, :]).astype(BF)
            gw_s[heads, :] += mm_tn(att(k, side), dproj)
    for k in range(F):
        ff = lax.rem(f + k, F)
        at = pl.ds(pl.multiple_of(ff * d_local, d_local), d_local)
        payloads[k][:d_local, :] = gw_s[at, :].astype(BF)
        payloads[k][d_local:, :d_local] = rows_s[ff]
        payloads[k][d_local:, d_local:] = jnp.zeros((16, D - d_local), BF)


def back_kernel(dims, blocks, start, cos, sin, small, *refs):
    Z, F, R, D, L, hpd, block = dims
    hw = hpd * HD
    dos, refs = refs[: 2 * Z], refs[2 * Z :]
    (normed, weight, q_in, k_in, v_in, kt_in, ot_in, lse_in), refs = refs[:8], refs[8:]
    payloads, refs = refs[:F], refs[F:]
    mixed_s, do_s, delta_s, dq_s, dk_s, dv_s, gw_s, rows_s = refs
    z, core, f, _ = place_of()
    d_local = D // F
    for k in range(Z):
        for side in range(2):
            at = lax.rem(z + k, Z) * 2 + (core if side == 0 else 1 - core)
            rows = pl.ds(pl.multiple_of(at * R, R), R)
            tile = dos[k][0] if side == 0 else dos[Z + k][...]
            turned = tile.astype(F32).T
            for h in range(hpd):
                heads = slice(h * HD, (h + 1) * HD)
                do_s[h, rows, :] = tile[:, heads]
                delta_s[h, :, rows] = jnp.sum(
                    turned[heads, :] * ot_in[h, :, rows], axis=0, keepdims=True
                )
    dk_s[...] = jnp.zeros_like(dk_s)
    dv_s[...] = jnp.zeros_like(dv_s)

    def query_step(qb, carry):
        rows = pl.ds(pl.multiple_of(qb * block, block), block)
        first = start[:, rows]
        q_pos = qb * block + lax.broadcasted_iota(jnp.int32, (block, block), 1)
        down = lax.broadcasted_iota(jnp.int32, (block, block), 0)
        queries = [q_in[h, rows, :] for h in range(hpd)]
        upstream = [do_s[h, rows, :] for h in range(hpd)]
        lses = [lse_in[h, :, rows] for h in range(hpd)]
        deltas = [delta_s[h, :, rows] for h in range(hpd)]

        def key_step(kb, state):
            keys = pl.ds(pl.multiple_of(kb * block, block), block)
            k_pos = kb * block + down
            allowed = (k_pos <= q_pos) & (k_pos >= first)
            new = []
            for h in range(hpd):
                scores = mm_nt(k_in[h, keys, :], queries[h])
                weights = jnp.where(allowed, jnp.exp(scores - lses[h]), 0.0)
                dp = mm_nt(v_in[h, keys, :], upstream[h])
                ds = (weights * (dp - deltas[h])).astype(BF)
                dv_s[h, keys, :] += mm(weights.astype(BF), upstream[h])
                dk_s[h, keys, :] += mm(ds, queries[h])
                new.append(state[h] + mm(kt_in[h, :, keys], ds))
            return tuple(new)

        begin = tuple(jnp.zeros((HD, block), F32) for _ in range(hpd))
        state = lax.fori_loop(blocks[qb], qb + 1, key_step, begin)
        for h in range(hpd):
            dq_s[h, rows, :] = state[h].T * HD ** (-0.5)
        return carry

    lax.fori_loop(0, L // block, query_step, 0)

    def unrotate(step, carry):
        rows = pl.ds(pl.multiple_of(step * block, block), block)
        cosine, sine = cos[rows, :], signed(sin[rows, :])
        parts = [[], [], []]
        for h in range(hpd):
            dq = dq_s[h, rows, :]
            dk = dk_s[h, rows, :]
            parts[0].append((dq * cosine - halves_swapped(dq) * sine).astype(BF))
            parts[1].append((dk * cosine - halves_swapped(dk) * sine).astype(BF))
            parts[2].append(dv_s[h, rows, :].astype(BF))
        mixed_s[rows, :] = jnp.concatenate(parts[0] + parts[1] + parts[2], axis=-1)
        return carry

    lax.fori_loop(0, L // block, unrotate, 0)
    gw = mm_tn(normed[...], mixed_s[...])
    gw_s[...] = gw.astype(BF)
    high, low = split(gw * weight[...].astype(F32))
    ones = jnp.ones((16, 3 * hw), BF)
    total = ((mm_nt(ones, high) + mm_nt(ones, low)) / small[0:1, :]).astype(BF)
    for i in range(F):
        rows_s[i] = total[:, i * d_local : (i + 1) * d_local]
    for k in range(F):
        ff = lax.rem(f + k, F)
        at = pl.ds(pl.multiple_of(ff * d_local, d_local), d_local)
        payloads[k][:d_local, :] = gw_s[at, :]
        payloads[k][d_local:, :d_local] = rows_s[ff]
        if d_local < 3 * hw:
            payloads[k][d_local:, d_local:] = jnp.zeros((16, 3 * hw - d_local), BF)


def normed_grad_kernel(dims, mixed, weight, mine, theirs, turned):
    Z, R = dims
    core = place_of()[1]
    turned[...] = weight[...].T

    def chip_step(chip, carry):
        for side in range(2):
            at = 2 * chip + (core if side == 0 else 1 - core)
            rows = pl.ds(pl.multiple_of(at * R, R), R)
            (mine if side == 0 else theirs)[chip] = mm(mixed[rows, :], turned[...]).astype(BF)
        return carry

    lax.fori_loop(0, Z, chip_step, 0)


def pair_kernel(Z, mine, theirs, *outs):
    meta = place_of()
    for k in range(Z):
        chip = lax.rem(meta[0] + k, Z)
        outs[k][...] = (mine[chip].astype(F32) + theirs[chip].astype(F32)).astype(BF)


def last_kernel(dims, x, dh, small, *refs):
    meta = place_of()
    Z, S, R, _, G = dims
    dns, out, acc = refs[:Z], refs[Z], refs[Z + 1]
    acc[...] = jnp.zeros_like(acc)
    for k in range(Z):
        seq, _ = piece_at((Z, G), meta, k, 0)
        acc[seq] += dns[k][...].astype(F32)
    gain = small[0:1, :]
    for s in range(S):
        tile = x[s].astype(F32)
        factor = norm_of(tile)
        normal = tile * factor
        scaled = acc[s] * gain
        out[s] = dh[s * R : (s + 1) * R, :] + factor * (
            scaled - normal * jnp.mean(scaled * normal, axis=-1, keepdims=True)
        )


def place_kernel(dims, ks, left, *refs):
    meta = place_of()
    F, per, CW, width = dims
    n = len(ks)
    ours, theirs, refs = refs[:n], refs[n : 2 * n], refs[2 * n :]
    outs, (buf, sems) = refs[-5:-2], refs[-2:]
    copies = []
    for side in range(2):
        for j, k in enumerate(ks):
            dev = lax.rem(meta[2] - k + F, F)
            core = meta[1] if side == 0 else 1 - meta[1]
            e = lax.div(dev, per)
            lane = (lax.rem(dev, per) * 2 + core) * CW + left
            lanes = pl.ds(pl.multiple_of(lane, 128), width)
            for i in range(3):
                at = (side * n + j) * 3 + i
                buf[at] = (ours if side == 0 else theirs)[j][i].astype(F32)
                copy = pltpu.make_async_copy(buf.at[at], outs[i].at[:, e, lanes], sems.at[at])
                copy.start()
                copies.append(copy)
    for copy in copies:
        copy.wait()


def qkv_grad_kernel(dims, *refs):
    meta = place_of()
    G, D, d_local, hw, offsets = dims
    pieces, (out, gain_out, table) = refs[:-3], refs[-3:]
    group = lax.rem(meta[3], G)
    at = 0
    for piece in pieces:
        for j in range(piece.shape[0]):
            table[offsets[at]] = piece[j]
            at += 1
    gain = jnp.zeros((1, d_local), F32)
    for i in range(G):
        tile = table[jnp.bitwise_xor(group, i)].astype(F32)
        gain = gain + tile[d_local : d_local + 1, :d_local]
        width = max(0, min(hw, D - i * hw))
        if width:
            for part in range(3):
                out[:, part * D + i * hw : part * D + i * hw + width] = tile[
                    :d_local, part * hw : part * hw + width
                ]
    gain_out[...] = gain


def body(
    block_input,
    attn_gain,
    w_qkv,
    w_out,
    ffn_gain,
    w_router,
    w_gate,
    w_up,
    w_down,
    const_mix,
    const_vec,
    prev_logits,
    routes,
    doc_ids,
    d_out,
    *,
    F,
    C,
):
    S, R, D = block_input.shape
    L = doc_ids.shape[1]
    Z = C // 2
    G = C // S
    hpd = -(-H // G)
    hw = hpd * HD
    FF = w_gate.shape[2]
    per = F // NF
    CW = FF // (2 * per)
    d_local = D // F
    T = S * R
    block = min(512, L)
    shaped = jax.ShapeDtypeStruct
    f = lax.axis_index(FS)
    c = lax.axis_index(CT)
    core = c % 2
    z = c // 2

    def fs(t, k):
        return lax.ppermute(t, FS, [(i, (i + k) % F) for i in range(F)])

    def zs(t, k):
        return lax.ppermute(
            t, CT, [(2 * i + j, 2 * ((i + k) % Z) + j) for i in range(Z) for j in range(2)]
        )

    def cx(t):
        return lax.ppermute(t, CT, [(i, i ^ 1) for i in range(C)])

    def pick(t, index, axis=0):
        return lax.dynamic_index_in_dim(t, index, axis, keepdims=False)

    def seq_of(chip):
        return chip // (Z // S)

    def expert_of(dev):
        return lax.div(dev, per)

    def chunk_of(dev):
        return (dev % per) * 2 + core

    def call(kernel, name, out_shape, args, scratch=(), smem=0, **kw):
        return pl.pallas_call(
            kernel,
            out_shape=out_shape,
            in_specs=[SMEM] * smem + [VMEM] * (len(args) - smem),
            out_specs=tuple([VMEM] * len(out_shape)),
            scratch_shapes=list(scratch),
            compiler_params=params(name, L > 2048),
            **kw,
        )(*args)

    x_mine = [pick(block_input, seq_of(z))] + [
        zs(pick(block_input, seq_of((z + k) % Z)), k) for k in range(1, Z)
    ]
    x_theirs = [cx(t) for t in x_mine]

    my_docs = pick(doc_ids, c // G)
    start = jnp.sum((my_docs[None, :] < my_docs[:, None]).astype(jnp.int32), axis=1)
    first_block = start.reshape(L // block, block)[:, 0] // block
    route_rows = routes.transpose(0, 2, 1).reshape(S * TOP, R)
    prev = prev_logits.transpose(0, 2, 1)

    (first,) = call(
        functools.partial(pack_kernel, (F, D, G, hpd)),
        "pack",
        (shaped((d_local + 16, 3 * hw), BF),),
        (
            w_qkv,
            jnp.stack([attn_gain, ffn_gain]),
            w_router.T,
            const_mix.T,
            const_vec.T,
        ),
    )
    w_pieces = [first] + [fs(first, k) for k in range(1, F)]
    slot_rows, *g_outs = call(
        functools.partial(grad_rows_kernel, (F, S, R, D, expert_of)),
        "rows",
        (shaped((S * TOP, R), jnp.int32),) + (shaped((S * MOST, D), BF),) * F,
        (d_out, route_rows),
        [pltpu.VMEM((NF, S * MOST, D), BF)],
    )
    g_rows = [g_outs[0]] + [fs(g_outs[k], k) for k in range(1, F)]
    (g_mine,) = call(
        functools.partial(stack_kernel, S * MOST),
        "stack",
        (shaped((F * S * MOST, D), BF),),
        tuple(g_rows),
    )
    half = lax.dynamic_slice_in_dim(w_out, core * (D // 2), D // 2, 1)
    o_pieces = [half] + [fs(half, k) for k in range(1, F)]
    o_pieces = o_pieces + [cx(t) for t in o_pieces]

    def expert_slices():
        if per == 1:
            cut = [
                lax.dynamic_slice_in_dim(w, core * CW, CW, 2).transpose(1, 0, 2)
                for w in (w_gate, w_up, w_down)
            ]
            cut = lax.optimization_barrier(cut)
            return call(
                functools.partial(order_kernel, (F, CW // 2)),
                "order",
                (shaped((3, d_local, CW), BF),) * (F - 1) + (shaped((3, d_local, CW // 2), BF),),
                tuple(cut),
            )
        out = []
        for k in range(F):
            dev = (f + k) % F
            out.append(
                jnp.stack(
                    [
                        pick(
                            lax.dynamic_slice_in_dim(w, chunk_of(dev) * CW, CW, 2),
                            expert_of(dev),
                            1,
                        )
                        for w in (w_gate, w_up, w_down)
                    ]
                )
            )
        return out

    slices = expert_slices()
    if per == 1:
        e_pieces = [slices[0]]
        for k in range(1, F):
            e_pieces.append(lax.ppermute(slices[k], FS, [(i, i ^ k) for i in range(F)]))
        e_pieces.append(lax.ppermute(e_pieces[-1], CT, [(i, i ^ 2) for i in range(C)]))
    else:
        e_pieces = [slices[0]] + [fs(slices[k], k) for k in range(1, F)]

    frequency = jnp.exp(jnp.arange(HD // 2, dtype=F32) * (-2.0 * math.log(10000.0) / HD))
    frequency = jnp.concatenate([frequency, frequency])
    low = jnp.arange(32).astype(F32)[:, None] * frequency[None, :]
    high = (32 * jnp.arange(L // 32)).astype(F32)[:, None] * frequency[None, :]
    tables = (jnp.cos(low), jnp.sin(low), jnp.cos(high), jnp.sin(high))
    dims = (Z, F, R, D, L, hpd, block)
    normed, qkv_w, small, cosine, sine, q, k_, v, kt, ot, lse, *att_pieces = call(
        functools.partial(attend_kernel, dims),
        "attend",
        (
            shaped((L, D), BF),
            shaped((D, 3 * hw), BF),
            shaped((16, D), F32),
            shaped((L, HD), F32),
            shaped((L, HD), F32),
            shaped((hpd, L, HD), BF),
            shaped((hpd, L, HD), BF),
            shaped((hpd, L, HD), BF),
            shaped((hpd, HD, L), BF),
            shaped((hpd, HD, L), F32),
            shaped((hpd, 1, L), F32),
        )
        + (shaped((2, R, hw), BF),) * Z,
        (first_block, start[None], *tables, *x_mine, *x_theirs, *w_pieces),
        [
            pltpu.VMEM((F, 16, d_local), F32),
            pltpu.VMEM((hpd, HD, L), BF),
            pltpu.VMEM((C, R, hw), BF),
        ],
        smem=1,
    )

    g_planes = [g_mine] + [zs(g_mine, k) for k in range(1, Z) if k < 2 or k == Z - 1]
    for k in range(2, Z - 1):
        g_planes.insert(k, zs(g_planes[k - 1], 1))
    g_planes = [(t, cx(t)) for t in g_planes]

    pieces = [att_pieces[0]] + [zs(att_pieces[k], k) for k in range(1, Z)]
    atts = pieces + [cx(t[1]) for t in pieces]
    outs = call(
        functools.partial(dispatch_kernel, (Z, F, S, R, D, G, hw, expert_of)),
        "disp",
        (shaped((T, D), F32), shaped((G * hw, D), BF))
        + (shaped((S * MOST, D + 128), BF),) * F,
        (block_input, small, prev, route_rows, slot_rows, *atts, *o_pieces),
        [pltpu.VMEM((NF, S * MOST, D + 128), BF)],
    )
    hidden, out_w, toks = outs[0], outs[1], outs[2:]
    own = [toks[0]] + [fs(toks[k], k) for k in range(1, F)]
    (own,) = call(
        functools.partial(stack_kernel, S * MOST),
        "stack",
        (shaped((F * S * MOST, D + 128), BF),),
        tuple(own),
    )
    n = own.shape[0]

    steps = 4 if CW % 512 == 0 else 2
    cut = CW // steps
    e_spec = pl.BlockSpec((3, d_local, cut), lambda i: (0, 0, i))
    e_specs = [e_spec] * F
    if len(e_pieces) > F:
        e_specs = [e_spec] * (F - 1) + [pl.BlockSpec((3, d_local, CW // 2), lambda i: (0, 0, 0))] * 2
    act_spec = pl.BlockSpec((2 * n, cut), lambda i: (0, i))
    both_spec = pl.BlockSpec((D, 2 * n), lambda i: (0, 0))

    def ffn(at, rows, theirs, g_rows):
        own_plane = at == 0
        shapes = (shaped((2 * n, CW), BF),) * 3 + (shaped((D, 2 * n), BF),) * 2
        specs = (act_spec,) * 3 + (both_spec,) * 2
        scratch = [pltpu.VMEM((2 * n, D), BF), pltpu.VMEM((2 * n, D), BF)]
        w_spec = pl.BlockSpec((3, D, cut), lambda i: (0, 0, i))
        if own_plane:
            shapes += (shaped((2, n, D), F32), shaped((2, n, D), BF), shaped((3, D, CW), BF))
            specs += (pl.BlockSpec((2, n, D), lambda i: (0, 0, 0)),) * 2 + (w_spec,)
            scratch.append(pltpu.VMEM((2, 2 * n, D), F32))
        row_spec = pl.BlockSpec((n, D + 128), lambda i: (0, 0))
        g_spec = pl.BlockSpec((n, D), lambda i: (0, 0))
        return pl.pallas_call(
            functools.partial(ffn_kernel, (F, D, len(e_pieces)), own_plane),
            out_shape=shapes,
            grid=(steps,),
            in_specs=[row_spec, row_spec, g_spec, g_spec]
            + (e_specs if own_plane else [w_spec]),
            out_specs=specs,
            scratch_shapes=scratch,
            compiler_params=params("ex" if at else "ex0", L > 2048),
        )(rows, theirs, *g_rows, *(e_pieces if own_plane else [weights]))

    *plane, back_mine, back_theirs, weights = ffn(0, own, cx(own), g_planes[0])
    planes = [plane]
    back_theirs = cx(back_theirs)
    back = (back_mine + back_theirs.astype(F32)).astype(BF).reshape(2, F, S * MOST, D)
    rets = [back[:, k] for k in range(F)]
    rets = [rets[0]] + [fs(rets[k], -k) for k in range(1, F)]
    ring = [own]
    for _ in range(1, Z):
        ring.append(zs(ring[-1], 1))

    def far(k, after):
        rows, g_rows, _ = lax.optimization_barrier((ring[k], g_planes[k], after))
        planes.append(ffn(k, rows, cx(rows), g_rows))

    far(1, back_mine)
    outs = call(
        functools.partial(combine_kernel, (Z, F, S, R, D, G, hw, per, expert_of)),
        "combine",
        (shaped((S, R, D), BF), shaped((T, D), F32), shaped((S, NE, R), F32))
        + (shaped((2, R, hw), BF),) * Z
        + (shaped((d_local + 16, D), BF),) * F,
        (hidden, d_out, small, prev, route_rows, slot_rows, *rets, *atts, out_w),
        [
            pltpu.VMEM((F, 2, S * MOST, D), BF),
            pltpu.VMEM((G * hw, D), F32),
            pltpu.VMEM((T, D), BF),
            pltpu.VMEM((F, 16, d_local), BF),
        ],
    )
    out_block, hidden_grad, prev_grad = outs[:3]
    das, o_payloads = outs[3 : 3 + Z], outs[3 + Z :]
    grad_prev = prev_grad.transpose(0, 2, 1)

    do_pieces = [das[0]] + [zs(das[k], -k) for k in range(1, Z)]
    dos = do_pieces + [cx(t[1]) for t in do_pieces]

    if Z > 2:
        far(2, hidden_grad)
    dos[0], *_ = lax.optimization_barrier((dos[0], planes[-1][0]))
    outs = call(
        functools.partial(back_kernel, dims),
        "back",
        (shaped((d_local + 16, 3 * hw), BF),) * F + (shaped((L, 3 * hw), BF),),
        (
            first_block,
            start[None],
            cosine,
            sine,
            small,
            *dos,
            normed,
            qkv_w,
            q,
            k_,
            v,
            kt,
            ot,
            lse,
        ),
        [
            pltpu.VMEM((hpd, L, HD), BF),
            pltpu.VMEM((hpd, 1, L), F32),
            pltpu.VMEM((hpd, L, HD), F32),
            pltpu.VMEM((hpd, L, HD), F32),
            pltpu.VMEM((hpd, L, HD), F32),
            pltpu.VMEM((D, 3 * hw), BF),
            pltpu.VMEM((F, 16, d_local), BF),
        ],
        smem=1,
    )
    q_payloads, mixed_grad = outs[:F], outs[F]
    for k in range(3, Z):
        far(k, mixed_grad)
    flat = [t for plane in planes for t in plane]
    flat[0], _ = lax.optimization_barrier((flat[0], mixed_grad))
    wide = 256
    widths = [CW // 2, CW // 2]
    e_grads = []
    for part, width in enumerate(widths):
        left = sum(widths[:part])
        if Z > 4:
            lanes = slice(left, left + width)
            trio = [
                sum(mm(plane[a], plane[b][:, lanes]) for plane in planes).astype(BF)
                for a, b in ((3, 1), (3, 2), (4, 0))
            ]
            trio = jnp.stack(trio).reshape(3, F, d_local, width)
            e_grads.append([pick(trio, (f + k) % F, 1) for k in range(F)])
            continue
        acts = pl.BlockSpec((2 * n, wide), lambda i, b=left // wide: (0, b + i))
        e_grads.append(
            pl.pallas_call(
                functools.partial(weight_kernel, (F, D, Z)),
                out_shape=(shaped((3, d_local, width), BF),) * F,
                grid=(width // wide,),
                in_specs=[acts, acts, acts, both_spec, both_spec] * Z,
                out_specs=(pl.BlockSpec((3, d_local, wide), lambda i: (0, 0, i)),) * F,
                scratch_shapes=[pltpu.VMEM((3, D, wide), BF)],
                compiler_params=params("wg", L > 2048),
            )(*flat)
        )
    dn_mine, dn_theirs = call(
        functools.partial(normed_grad_kernel, (Z, R)),
        "ng",
        (shaped((Z, R, D), BF),) * 2,
        (mixed_grad, qkv_w),
        [pltpu.VMEM((3 * hw, D), BF)],
    )
    dns = call(
        functools.partial(pair_kernel, Z),
        "pair",
        (shaped((R, D), BF),) * Z,
        (dn_mine, cx(dn_theirs)),
    )
    dns = [dns[0]] + [zs(dns[k], k) for k in range(1, Z)]
    (grad_x,) = call(
        functools.partial(last_kernel, (Z, S, R, D, G)),
        "ig",
        (shaped((S, R, D), F32),),
        (block_input, hidden_grad, small, *dns),
        [pltpu.VMEM((S, R, D), F32)],
    )

    def moved_rows(parts):
        return [parts[0]] + [fs(parts[k], k) for k in range(1, F)]

    def summed_rows(parts):
        return sum(p.astype(F32) for p in parts).astype(BF)

    def over_ctx(t):
        step = 1
        while step < C:
            moved = lax.ppermute(t, CT, [(i, i ^ step) for i in range(C)])
            t = (t.astype(F32) + moved.astype(F32)).astype(BF)
            step *= 2
        return t

    payload = summed_rows(moved_rows(q_payloads))
    summed = payload.astype(F32)
    for j in range(1, S):
        moved = lax.ppermute(payload, CT, [(i, (i + j * G) % C) for i in range(C)])
        summed = summed + moved.astype(F32)
    payload = summed.astype(BF)[None]
    gathered, offsets = [payload], (0,)
    step = G // 2
    while step:
        gathered.append(lax.ppermute(payload, CT, [(i, i ^ step) for i in range(C)]))
        offsets += tuple(i ^ step for i in offsets)
        step //= 2
        if step:
            payload = jnp.concatenate([payload, gathered[-1]], axis=0)
    grad_qkv, grad_gain_one = call(
        functools.partial(qkv_grad_kernel, (G, D, d_local, hw, offsets)),
        "qg",
        (shaped((d_local, 3 * D), F32), shaped((1, d_local), F32)),
        tuple(gathered),
        [pltpu.VMEM((G, d_local + 16, 3 * hw), BF)],
    )
    grad_gain_one = grad_gain_one[0]

    moved = moved_rows(o_payloads)
    payload = over_ctx(summed_rows(moved)).astype(F32)
    payload = lax.optimization_barrier(payload)
    grad_w_out = payload[:d_local]
    smalls = payload[d_local:, :d_local]

    ANY = pl.BlockSpec(memory_space=pl.ANY)
    placed = ()
    for part, width in enumerate(widths):
        ours = [e_grads[part][0]] + [fs(e_grads[part][k], k) for k in range(1, F)]
        theirs = [cx(t) for t in ours]
        groups = [list(range(F))]
        for ks in groups:
            args = (*[ours[k] for k in ks], *[theirs[k] for k in ks], *placed)
            at = 2 * len(ks)
            placed = pl.pallas_call(
                functools.partial(
                    place_kernel, (F, per, CW, width), ks, sum(widths[:part])
                ),
                out_shape=(shaped((d_local, NF, FF), F32),) * 3,
                in_specs=[VMEM] * (2 * len(ks)) + [ANY] * len(placed),
                out_specs=(ANY,) * 3,
                input_output_aliases={at + i: i for i in range(len(placed))},
                scratch_shapes=[
                    pltpu.VMEM((6 * len(ks), d_local, width), F32),
                    pltpu.SemaphoreType.DMA((6 * len(ks),)),
                ],
                compiler_params=params("place", L > 2048),
            )(*args)
    grad_gate, grad_up, grad_down = placed
    return (
        out_block,
        grad_x,
        grad_prev,
        grad_gain_one,
        grad_qkv,
        grad_w_out,
        smalls[1],
        smalls[2:10].T,
        grad_gate,
        grad_up,
        grad_down,
        smalls[10:14].T,
        smalls[14:16].T,
    )


def solution(mesh):
    F, Z = mesh.shape[FS], mesh.shape[CT] // 2

    def layer(*args):
        return body(*args, F=F, C=2 * Z)

    return jax.shard_map(
        layer,
        mesh=mesh,
        in_specs=(
            P(FS, CT, None),
            P(FS),
            P(FS, None),
            P(FS, None),
            P(FS),
            P(FS, None),
            P(FS, None, None),
            P(FS, None, None),
            P(FS, None, None),
            P(FS, None),
            P(FS, None),
            P(FS, CT, None),
            P(FS, CT, None),
            P(FS, None),
            P(FS, CT, None),
        ),
        out_specs=(
            P(FS, CT, None),
            P(FS, CT, None),
            P(FS, CT, None),
            P(FS),
            P(FS, None),
            P(FS, None),
            P(FS),
            P(FS, None),
            P(FS, None, None),
            P(FS, None, None),
            P(FS, None, None),
            P(FS, None),
            P(FS, None),
        ),
        check_vma=False,
    )
```
